256 devices in a mesh: gx: 16 (over x, z_hi), gy: 16 (over z_lo, y, core).
Axes of the slice: x: 4, y: 4, z: 8 (z_hi: 4, z_lo: 2; z = z_hi * 2 + z_lo), core: 2. Of those that a mesh axis runs over, the one named last changes fastest.
Arguments:
- field: bfloat16 [20, 32, 64, 512], P(None, 'gx', 'gy'), may hold values from -6 to 6
- cotangent: bfloat16 [20, 32, 64, 512], P(None, 'gx', 'gy'), may hold values from -6 to 6
- spectral_weight: float32 [64, 2, 20, 20, 16, 16], P('gx', None, None, None, 'gy'), may hold values from -3 to 3
- pointwise_weight: bfloat16 [20, 20], replicated, may hold values from -1.25 to 1.25
- channel_bias: float32 [20], replicated, may hold values from -3 to 3
Outputs:
- layer_out: bfloat16 [20, 32, 64, 512], P(None, 'gx', 'gy')
- grad_field: bfloat16 [20, 32, 64, 512], P(None, 'gx', 'gy')
- grad_spectral: float32 [64, 2, 20, 20, 16, 16], P('gx', None, None, None, 'gy')
The draws below stay inside these ranges and needn't reach their ends.
All inputs are finite; a program needn't handle non-finite values.
Results may differ from the reference program's by a relative error of at most 0.0061.
Values sent between devices are 32-bit elements; how exact they have to be, the bound alone decides.
A program may use at most 64 MiB of HBM per device.

```python
import math
import jax
import jax.numpy as jnp
from jax import lax

W = 20
KX = 16
KY = 16
KZ = 16
KT = 4
NZ = 32
NT = 16
MZT = 64
NX = 32
NY = 64


def steps_of(key, shape, pieces, low, largest):
    def one(axis_at, blocks):
        heights = jax.random.uniform(jax.random.fold_in(jax.random.fold_in(key, 6), axis_at), (blocks,), jnp.float32, low / len(pieces), largest / len(pieces))
        return jnp.repeat(jnp.exp(heights), shape[axis_at] // blocks).reshape((-1,) + (1,) * (len(shape) - axis_at - 1))

    loudness = one(*pieces[0])
    for cut in pieces[1:]:
        loudness = loudness * one(*cut)
    return loudness


def noise(rng, dims, width, bound, shards=(), kind=jnp.bfloat16):
    drawn = width * jax.random.normal(rng, dims, jnp.float32)
    if shards:
        drawn = drawn * steps_of(rng, dims, shards, -0.22, 0.18)
    return jnp.clip(drawn, -bound, bound).astype(kind)


def setup_inputs(seed: int = 0) -> dict:
    key_of = jax.random.split(jax.random.key(seed), 6)
    field = noise(key_of[0], (W, NX, NY, NZ * NT), 1.0, 6.0, ((1, 16), (2, 16)))
    cotangent = noise(key_of[1], (W, NX, NY, NZ * NT), 1.0, 6.0, ((1, 16), (2, 16)))
    spectral_weight = noise(key_of[2], (MZT, 2, W, W, KX, KY), 0.5, 3.0, ((0, 16), (4, 16)), jnp.float32)
    pointwise_weight = noise(key_of[3], (W, W), W ** -0.5, 1.25)
    channel_bias = noise(key_of[4], (W,), 0.5, 3.0, (), jnp.float32)
    return {"field": field, "cotangent": cotangent, "spectral_weight": spectral_weight, "pointwise_weight": pointwise_weight, "channel_bias": channel_bias}


HIGHEST_PRECISION = lax.Precision.HIGHEST

def rotation(length, kept_modes, phase_sign, cell_count, offset):
    position = offset + jnp.arange(cell_count, dtype=jnp.int32)
    mode_index = jnp.arange(kept_modes, dtype=jnp.int32)
    frequency = jnp.where(mode_index < kept_modes // 2, mode_index, mode_index - kept_modes)
    phase_int = jnp.mod(position[:, None] * frequency[None, :], length)
    angles = phase_int.astype(jnp.float32) * (phase_sign * 2.0 * math.pi / length)
    factor = 1.0 / math.sqrt(length)
    cosine = jnp.cos(angles) * factor
    sine_part = jnp.sin(angles) * factor
    return jnp.stack([jnp.stack([cosine, sine_part]), jnp.stack([-sine_part, cosine])])

def depth_time_table(depth_cells, time_cells, modes_depth, modes_time):
    depth_pos = jnp.arange(depth_cells, dtype=jnp.int32)
    time_pos = jnp.arange(time_cells, dtype=jnp.int32)
    depth_index = jnp.arange(modes_depth, dtype=jnp.int32)
    depth_freq = jnp.where(depth_index < modes_depth // 2, depth_index, depth_index - modes_depth)
    time_freq = jnp.arange(modes_time, dtype=jnp.int32)
    total_cells = depth_cells * time_cells
    phase_int = depth_pos[:, None, None, None] * depth_freq[None, None, :, None] * time_cells + time_pos[None, :, None, None] * time_freq[None, None, None, :] * depth_cells
    phase_int = jnp.mod(phase_int, total_cells).reshape(total_cells, modes_depth * modes_time)
    angles = phase_int.astype(jnp.float32) * (2.0 * math.pi / total_cells)
    factor = 1.0 / math.sqrt(total_cells)
    return jnp.stack([jnp.cos(angles) * factor, -jnp.sin(angles) * factor], axis=1)

def mode_weight(first_mode, mode_count, modes_time):
    mode_ids = first_mode + jnp.arange(mode_count, dtype=jnp.int32)
    weights = jnp.where(jnp.mod(mode_ids, modes_time) == 0, 1.0, 2.0).astype(jnp.float32)
    return weights.reshape(mode_count, 1, 1, 1, 1)

def mix_pair(left_part, right_part):
    return jnp.einsum('mwkj,mwokj->mokj', left_part, right_part, precision=HIGHEST_PRECISION)

def adjoint_pair(left_part, right_part):
    return jnp.einsum('mwokj,mokj->mwkj', left_part, right_part, precision=HIGHEST_PRECISION)

def complex_mix(spectra, weights):
    real_in, imag_in = (spectra[:, 0], spectra[:, 1])
    real_w, imag_w = (weights[:, 0], weights[:, 1])
    real_out = mix_pair(real_in, real_w) - mix_pair(imag_in, imag_w)
    imag_out = mix_pair(real_in, imag_w) + mix_pair(imag_in, real_w)
    return jnp.stack([real_out, imag_out], axis=1)

def adjoint_mix(weights, spectra):
    real_w, imag_w = (weights[:, 0], weights[:, 1])
    real_in, imag_in = (spectra[:, 0], spectra[:, 1])
    real_out = adjoint_pair(real_w, real_in) + adjoint_pair(imag_w, imag_in)
    imag_out = adjoint_pair(real_w, imag_in) - adjoint_pair(imag_w, real_in)
    return jnp.stack([real_out, imag_out], axis=1)

def weight_grad(inputs, outputs):
    real_in = inputs[:, 0][:, :, None]
    imag_in = inputs[:, 1][:, :, None]
    real_out = outputs[:, 0][:, None]
    imag_out = outputs[:, 1][:, None]
    real_part = real_in * real_out + imag_in * imag_out
    imag_part = real_in * imag_out - imag_in * real_out
    return jnp.stack([real_part, imag_part], axis=1)

def forward_spectrum(values, table_half):
    first_section = jnp.einsum('wxyq,qsm->mswyx', values, table_half, preferred_element_type=jnp.float32)
    table_first = rotation(NX, KX, -1.0, NX, 0)
    second_section = jnp.einsum('mswyx,srxk->mrwky', first_section, table_first, precision=HIGHEST_PRECISION)
    table_second = rotation(NY, KY, -1.0, NY, 0)
    return jnp.einsum('mswky,sryj->mrwkj', second_section, table_second, precision=HIGHEST_PRECISION)

def inverse_modes(spectra):
    table_second = rotation(NY, KY, 1.0, NY, 0)
    first_section = jnp.einsum('msokj,sryj->mroky', spectra, table_second, precision=HIGHEST_PRECISION)
    table_first = rotation(NX, KX, 1.0, NX, 0)
    return jnp.einsum('msoky,srxk->mroyx', first_section, table_first, precision=HIGHEST_PRECISION)

def reference(field, cotangent, spectral_weight, pointwise_weight, channel_bias):
    table_float = depth_time_table(NZ, NT, KZ, KT)
    table_half = table_float.astype(jnp.bfloat16)
    weights_modes = mode_weight(0, KZ * KT, KT)
    spectra = forward_spectrum(field, table_half)
    mixed_modes = complex_mix(spectra, spectral_weight) * weights_modes
    inverse = inverse_modes(mixed_modes)

    def channel_out(inputs):
        channel_modes, column, offset_value, channel_cot = inputs
        spatial = jnp.einsum('msyx,qsm->xyq', channel_modes, table_float, precision=HIGHEST_PRECISION)
        local_term = jnp.einsum('w,wxyq->xyq', column, field, preferred_element_type=jnp.float32)
        pre_act = spatial + local_term + offset_value
        activated, pullback = jax.vjp(jax.nn.gelu, pre_act)
        scaled = pullback(channel_cot.astype(jnp.float32))[0]
        return (activated.astype(jnp.bfloat16), scaled.astype(jnp.bfloat16))
    layer_out, signal = lax.map(channel_out, (jnp.moveaxis(inverse, 2, 0), pointwise_weight.T, channel_bias, cotangent))
    back_spectra = forward_spectrum(signal, table_half) * weights_modes
    grad_spectral = weight_grad(spectra, back_spectra)
    back_inverse = inverse_modes(adjoint_mix(spectral_weight, back_spectra))

    def channel_in(inputs):
        channel_modes, row_weights = inputs
        spatial = jnp.einsum('msyx,qsm->xyq', channel_modes, table_float, precision=HIGHEST_PRECISION)
        local_term = jnp.einsum('o,oxyq->xyq', row_weights, signal, preferred_element_type=jnp.float32)
        return (spatial + local_term).astype(jnp.bfloat16)
    grad_field = lax.map(channel_in, (jnp.moveaxis(back_inverse, 2, 0), pointwise_weight))
    return (layer_out, grad_field, grad_spectral)
```

```python
import math

import jax
import jax.numpy as jnp
from jax import lax
from jax.sharding import PartitionSpec as P

KX = 16
KY = 16
KZ = 16
KT = 4
NZ = 32
NT = 16


HIGHEST_PRECISION = lax.Precision.HIGHEST


def rotation(length, kept_modes, phase_sign, cell_count, offset):
    position = offset + jnp.arange(cell_count, dtype=jnp.int32)
    mode_index = jnp.arange(kept_modes, dtype=jnp.int32)
    frequency = jnp.where(mode_index < kept_modes // 2, mode_index, mode_index - kept_modes)
    phase_int = jnp.mod(position[:, None] * frequency[None, :], length)
    angles = phase_int.astype(jnp.float32) * (phase_sign * 2.0 * math.pi / length)
    factor = 1.0 / math.sqrt(length)
    cosine = jnp.cos(angles) * factor
    sine_part = jnp.sin(angles) * factor
    return jnp.stack([jnp.stack([cosine, sine_part]), jnp.stack([-sine_part, cosine])])


def depth_time_table(depth_cells, time_cells, modes_depth, modes_time):
    depth_pos = jnp.arange(depth_cells, dtype=jnp.int32)
    time_pos = jnp.arange(time_cells, dtype=jnp.int32)
    depth_index = jnp.arange(modes_depth, dtype=jnp.int32)
    depth_freq = jnp.where(depth_index < modes_depth // 2, depth_index, depth_index - modes_depth)
    time_freq = jnp.arange(modes_time, dtype=jnp.int32)
    total_cells = depth_cells * time_cells
    phase_int = (
        depth_pos[:, None, None, None] * depth_freq[None, None, :, None] * time_cells
        + time_pos[None, :, None, None] * time_freq[None, None, None, :] * depth_cells
    )
    phase_int = jnp.mod(phase_int, total_cells).reshape(total_cells, modes_depth * modes_time)
    angles = phase_int.astype(jnp.float32) * (2.0 * math.pi / total_cells)
    factor = 1.0 / math.sqrt(total_cells)
    return jnp.stack([jnp.cos(angles) * factor, -jnp.sin(angles) * factor], axis=1)


def mode_weight(first_mode, mode_count, modes_time):
    mode_ids = first_mode + jnp.arange(mode_count, dtype=jnp.int32)
    weights = jnp.where(jnp.mod(mode_ids, modes_time) == 0, 1.0, 2.0).astype(jnp.float32)
    return weights.reshape(mode_count, 1, 1, 1, 1)


def mix_pair(left_part, right_part):
    return jnp.einsum("mwkj,mwokj->mokj", left_part, right_part, precision=HIGHEST_PRECISION)


def adjoint_pair(left_part, right_part):
    return jnp.einsum("mwokj,mokj->mwkj", left_part, right_part, precision=HIGHEST_PRECISION)


def complex_mix(spectra, weights):
    real_in, imag_in = (spectra[:, 0], spectra[:, 1])
    real_w, imag_w = (weights[:, 0], weights[:, 1])
    real_out = mix_pair(real_in, real_w) - mix_pair(imag_in, imag_w)
    imag_out = mix_pair(real_in, imag_w) + mix_pair(imag_in, real_w)
    return jnp.stack([real_out, imag_out], axis=1)


def adjoint_mix(weights, spectra):
    real_w, imag_w = (weights[:, 0], weights[:, 1])
    real_in, imag_in = (spectra[:, 0], spectra[:, 1])
    real_out = adjoint_pair(real_w, real_in) + adjoint_pair(imag_w, imag_in)
    imag_out = adjoint_pair(real_w, imag_in) - adjoint_pair(imag_w, real_in)
    return jnp.stack([real_out, imag_out], axis=1)


def weight_grad(inputs, outputs):
    real_in = inputs[:, 0][:, :, None]
    imag_in = inputs[:, 1][:, :, None]
    real_out = outputs[:, 0][:, None]
    imag_out = outputs[:, 1][:, None]
    real_part = real_in * real_out + imag_in * imag_out
    imag_part = real_in * imag_out - imag_in * real_out
    return jnp.stack([real_part, imag_part], axis=1)


def on_device(field, cotangent, spectral_weight, pointwise_weight, channel_bias):
    cells_first = field.shape[1]
    cells_second = field.shape[2]
    length_first = cells_first * lax.axis_size("gx")
    length_second = cells_second * lax.axis_size("gy")
    local_modes = spectral_weight.shape[0]
    weights_modes = mode_weight(lax.axis_index("gx") * local_modes, local_modes, KT)
    table_float = depth_time_table(NZ, NT, KZ, KT)
    table_half = table_float.astype(jnp.bfloat16)
    forward_block = rotation(length_first, KX, -1.0, length_first, 0)
    forward_second = rotation(length_second, KY, -1.0, length_second, 0)
    inverse_block = rotation(length_first, KX, 1.0, length_first, 0)
    inverse_second = rotation(length_second, KY, 1.0, length_second, 0)

    def transform_second(pencil):
        return jnp.einsum("mswky,sryj->mrwkj", pencil, forward_second, precision=HIGHEST_PRECISION)

    def finish_cells(pencil):
        return jnp.einsum("msoyx,qsm->oxyq", pencil, table_float, precision=HIGHEST_PRECISION)

    def partial_inverse(pencil):
        return jnp.einsum("msoky,srxk->mroyx", pencil, inverse_block, precision=HIGHEST_PRECISION)

    def forward_spectrum(values):
        first_section = jnp.einsum(
            "wxyq,qsm->mswyx", values, table_half, preferred_element_type=jnp.float32
        )
        gathered_x = lax.all_to_all(first_section, "gx", split_axis=0, concat_axis=4, tiled=True)
        second_section = jnp.einsum(
            "mswyx,srxk->mrwky", gathered_x, forward_block, precision=HIGHEST_PRECISION
        )
        return transform_second(
            lax.all_to_all(second_section, "gy", split_axis=3, concat_axis=4, tiled=True)
        )

    def inverse_cells(spectra):
        first_section = jnp.einsum(
            "msokj,sryj->mroky", spectra, inverse_second, precision=HIGHEST_PRECISION
        )
        returned = lax.all_to_all(first_section, "gy", split_axis=4, concat_axis=3, tiled=True)
        gathered = lax.all_to_all(
            partial_inverse(returned), "gx", split_axis=4, concat_axis=0, tiled=True
        )
        spatial = finish_cells(gathered)
        return spatial

    spectra = forward_spectrum(field)
    mixed_modes = complex_mix(spectra, spectral_weight) * weights_modes
    spatial = inverse_cells(mixed_modes)
    local_term = jnp.einsum(
        "wo,wxyq->oxyq", pointwise_weight, field, preferred_element_type=jnp.float32
    )
    pre_act = spatial + local_term + channel_bias[:, None, None, None]
    activated, pullback = jax.vjp(jax.nn.gelu, pre_act)
    signal = pullback(cotangent.astype(jnp.float32))[0].astype(jnp.bfloat16)
    layer_out = activated.astype(jnp.bfloat16)
    back_spectra = forward_spectrum(signal) * weights_modes
    grad_spectral = weight_grad(spectra, back_spectra)
    back_cells = inverse_cells(adjoint_mix(spectral_weight, back_spectra))
    back_local = jnp.einsum(
        "wo,oxyq->wxyq", pointwise_weight, signal, preferred_element_type=jnp.float32
    )
    grad_field = (back_cells + back_local).astype(jnp.bfloat16)
    return (layer_out, grad_field, grad_spectral)


def solution(mesh):
    return jax.shard_map(
        on_device,
        mesh=mesh,
        in_specs=(
            P(None, "gx", "gy", None),
            P(None, "gx", "gy", None),
            P("gx", None, None, None, "gy", None),
            P(),
            P(),
        ),
        out_specs=(
            P(None, "gx", "gy", None),
            P(None, "gx", "gy", None),
            P("gx", None, None, None, "gy", None),
        ),
        check_vma=False,
    )
```

```python
import math

import jax
import jax.numpy as jnp
import numpy as np
from jax import lax
from jax.experimental import pallas as pl
from jax.experimental.pallas import tpu as pltpu
from jax.sharding import PartitionSpec as P

W = 20
WP = 32
GX = 16
GY = 16
Q = 512
F32 = jnp.float32
BF16 = jnp.bfloat16
HIGHEST = lax.Precision.HIGHEST


def frequencies():
    j = np.arange(16)
    return np.where(j < 8, j, j - 16)


def rotation_blocks(length, sign):
    phase = np.mod(frequencies()[:, None] * np.arange(length)[None, :], length)
    angle = sign * 2.0 * np.pi * phase / length
    c, s = np.cos(angle) / np.sqrt(length), np.sin(angle) / np.sqrt(length)
    return np.stack([np.stack([c, -s]), np.stack([s, c])])


def tables():
    eye = np.eye(4)
    fx = rotation_blocks(32, -1.0).reshape(2, 2, 16, 16, 2)
    tx = np.einsum("rskcx,yv->krycsxv", fx, eye).reshape(128, 256)
    fy = rotation_blocks(64, -1.0).reshape(2, 2, 16, 16, 4)
    ty = np.einsum("rskpy->rkpsy", fy).reshape(32, 128)
    iy = rotation_blocks(64, 1.0).reshape(2, 2, 16, 16, 4)
    tyi = np.einsum("rskpy->prysk", iy).reshape(128, 32)
    ix = rotation_blocks(32, 1.0).reshape(2, 2, 16, 16, 2)
    txi = np.einsum("rskcx,yv->crxyksv", ix, eye).reshape(256, 128)
    z, t = np.arange(32), np.arange(16)
    f = frequencies()
    phase = (
        f[None, :, None, None] * z[None, None, :, None] * 16
        + np.arange(4)[:, None, None, None] * t[None, None, None, :] * 32
    )
    angle = np.mod(phase, 512).reshape(4, 16, 512) * (2.0 * np.pi / 512)
    zt = np.stack([np.cos(angle), -np.sin(angle)], axis=1).reshape(128, 512) / np.sqrt(512)
    return [a.astype(np.float32) for a in (tx, ty, tyi, txi, zt)]


def lane_blocks(rows):
    return lax.broadcasted_iota(jnp.int32, (rows, 128), 1) // WP


def block_transpose(parts):
    which = lane_blocks(parts[0].shape[0])
    out = []
    for b in range(4):
        acc = None
        for a in range(4):
            shift = ((a - b) * WP) % 128
            piece = parts[a] if shift == 0 else pltpu.roll(parts[a], shift, 1)
            acc = piece if acc is None else jnp.where(which == a, piece, acc)
        out.append(acc)
    return out


def kernel(
    field, cot, weight, pw, bias, zt_h, tx_h, ty_h, tyi_h, txi_h,
    out_h, gfield_h, gspec_h,
    u, cv, wv, pwv, bv, zt, tx, ty, tyi, txi,
    wt, local, pre, sig, outv, gout, gs, spec,
    s1, s2, s3, s4, e, d, z, v,
    load_sem, store_sem, send_sem, recv_sem,
):
    cx = lax.axis_index("gx")
    cy = lax.axis_index("gy")

    sources = (field, zt_h, tx_h, ty_h, tyi_h, txi_h, weight, pw, bias, cot)
    sinks = (u, zt, tx, ty, tyi, txi, wv, pwv, bv, cv)
    loads = [
        pltpu.make_async_copy(a, b, load_sem.at[i]) for i, (a, b) in enumerate(zip(sources, sinks))
    ]
    for copy in loads:
        copy.start()

    def peer_x(off):
        dx, dz = off // 4, off % 4
        return lax.rem(cx // 4 + dx, 4) * 4 + lax.rem(lax.rem(cx, 4) + dz, 4)

    def peer_y(off):
        dz, rest = off // 8, off % 8
        dy, dc = rest // 2, rest % 2
        zl, yy, cc = cy // 8, lax.rem(cy // 2, 4), lax.rem(cy, 2)
        return lax.rem(zl + dz, 2) * 8 + lax.rem(yy + dy, 4) * 2 + lax.rem(cc + dc, 2)

    def ring(n):
        return min(n, 4 - n)

    order_x = sorted(range(1, 16), key=lambda o: -(ring(o // 4) + 2 * ring(o % 4)))
    order_y = sorted(range(1, 16), key=lambda o: -(3 * (o // 8) + 3 * ring((o % 8) // 2) + o % 2))

    barrier = pltpu.get_barrier_semaphore()
    for off in order_x:
        pl.semaphore_signal(
            barrier, inc=1, device_id=(peer_x(off), cy), device_id_type=pl.DeviceIdType.MESH
        )
    for off in order_y:
        pl.semaphore_signal(
            barrier, inc=1, device_id=(cx, peer_y(off)), device_id_type=pl.DeviceIdType.MESH
        )

    def exchange(step, axis, src, dst):
        copies = []
        for off in order_x if axis == "gx" else order_y:
            if axis == "gx":
                peer, me, device = peer_x(off), cx, (peer_x(off), cy)
            else:
                peer, me, device = peer_y(off), cy, (cx, peer_y(off))
            copy = pltpu.make_async_remote_copy(
                src_ref=src.at[peer],
                dst_ref=dst.at[me],
                send_sem=send_sem.at[step, off],
                recv_sem=recv_sem.at[step, off],
                device_id=device,
                device_id_type=pl.DeviceIdType.MESH,
            )
            copy.start()
            copies.append(copy)
        me = cx if axis == "gx" else cy
        dst[me] = src[me]
        return copies

    def arrive(copies):
        for copy in copies:
            copy.wait_recv()

    def drain(copies):
        for copy in copies:
            copy.wait_send()

    def pack_modes(values, send):
        spectra = lax.dot_general(
            zt[...], values[...], (((1,), (1,)), ((), ())), preferred_element_type=F32
        )
        for half in range(2):
            parts = [
                spectra[jt * 32 : jt * 32 + 32, half * 128 : half * 128 + 128] for jt in range(4)
            ]
            for sub, block in enumerate(block_transpose(parts)):
                for s in range(2):
                    send[:, s * 8 + half * 4 + sub, :] = block[s * 16 : s * 16 + 16]

    def unpack_modes(recv, half):
        parts = [
            jnp.concatenate([recv[:, s * 8 + half * 4 + sub, :] for s in range(2)], axis=0)
            for sub in range(4)
        ]
        stacked = jnp.concatenate(block_transpose(parts), axis=0)
        return stacked.T.astype(BF16)

    def matmul(a, b):
        return lax.dot_general(
            a, b, (((1,), (0,)), ((), ())), precision=HIGHEST, preferred_element_type=F32
        )

    kappa = jnp.where(lax.broadcasted_iota(jnp.int32, (16, 128), 1) < WP, 1.0, 2.0).astype(F32)
    gather_base = lane_blocks(16) * WP

    def spread(value, w):
        return jnp.take_along_axis(value, gather_base + w, axis=1)

    loads[0].wait()
    loads[1].wait()
    pack_modes(u, s1)
    pl.semaphore_wait(barrier, 30)
    c0 = exchange(0, "gx", s1, e.at[0])

    for copy in loads[2:]:
        copy.wait()
    zeros = jnp.zeros((16, WP - W), F32)

    @pl.loop(0, W)
    def _(w):
        for s in range(2):
            pieces = []
            for jt in range(4):
                pieces += [wv[jt, s, w], zeros]
            wt[s, w] = jnp.concatenate(pieces, axis=1)

    for xy in range(8):
        rows = slice(xy * WP, xy * WP + WP)
        local[rows] = (
            jnp.dot(pwv[0], u[rows], preferred_element_type=F32) + bv[...]
        )

    arrive(c0)
    s2[...] = matmul(tx[...], e[0].reshape(256, 128)).reshape(16, 8, 128)
    c1 = exchange(1, "gy", s2, d.at[0])
    arrive(c1)
    spec[...] = matmul(ty[...], d[0].reshape(128, 128))

    def mix(w, acc):
        sr, si = spread(spec[0:16], w), spread(spec[16:32], w)
        wr, wi = wt[0, w], wt[1, w]
        return acc[0] + wr * sr - wi * si, acc[1] + wi * sr + wr * si

    acc = (jnp.zeros((16, 128), F32), jnp.zeros((16, 128), F32))
    for w in range(W):
        acc = mix(w, acc)
    mixed = jnp.concatenate([acc[0] * kappa, acc[1] * kappa], axis=0)

    s3[...] = matmul(tyi[...], mixed).reshape(16, 8, 128)
    c2 = exchange(2, "gy", s3, z.at[0])
    arrive(c2)
    s4[...] = matmul(txi[...], z[0].reshape(128, 128)).reshape(16, 16, 128)
    c3 = exchange(3, "gx", s4, v.at[0])
    drain(c0)
    arrive(c3)

    for half in range(2):
        rows = slice(half * 128, half * 128 + 128)
        pre[rows] = local[rows] + jnp.dot(
            unpack_modes(v.at[0], half), zt[...], preferred_element_type=F32
        )
    root = math.sqrt(2.0 / math.pi)
    for xy in range(8):
        rows = slice(xy * WP, xy * WP + WP)
        p = pre[rows]
        square = p * p
        t = jnp.tanh(root * p * (1.0 + 0.044715 * square))
        outv[rows] = (0.5 * p * (1.0 + t)).astype(BF16)
        slope = 0.5 * (1.0 + t) + (0.5 * root) * p * (1.0 - t * t) * (
            1.0 + (3.0 * 0.044715) * square
        )
        sig[rows] = (cv[rows].astype(F32) * slope).astype(BF16)

    pack_modes(sig, s1)
    c4 = exchange(4, "gx", s1, e.at[1])
    put_out = pltpu.make_async_copy(outv, out_h, store_sem.at[0])
    put_out.start()
    for xy in range(8):
        rows = slice(xy * WP, xy * WP + WP)
        local[rows] = jnp.dot(pwv[1], sig[rows], preferred_element_type=F32)
    drain(c1)
    drain(c2)
    drain(c3)
    arrive(c4)
    s2[...] = matmul(tx[...], e[1].reshape(256, 128)).reshape(16, 8, 128)
    c5 = exchange(5, "gy", s2, d.at[1])
    arrive(c5)
    back = matmul(ty[...], d[1].reshape(128, 128))
    br, bi = back[0:16] * kappa, back[16:32] * kappa

    lane = lax.broadcasted_iota(jnp.int32, (32, 128), 1)

    def combine(a, b, h):
        bit = (lane & h) != 0
        flip = lane ^ h
        if b is None:
            return jnp.where(bit, 0.0, a + jnp.take_along_axis(a, flip, axis=1))
        return jnp.where(bit, b, a) + jnp.take_along_axis(jnp.where(bit, a, b), flip, axis=1)

    def product(w):
        wr, wi = wt[0, w], wt[1, w]
        return jnp.concatenate([wr * br + wi * bi, wr * bi - wi * br], axis=0)

    def reduce_tree(w, h):
        if h == 32:
            return product(w) if w < W else None
        a, b = reduce_tree(w, h * 2), reduce_tree(w + h, h * 2)
        return combine(a, b, h) if a is not None else None

    back_mixed = reduce_tree(0, 1)
    s3[...] = matmul(tyi[...], back_mixed).reshape(16, 8, 128)
    c6 = exchange(6, "gy", s3, z.at[1])

    @pl.loop(0, W)
    def _(w):
        sr, si = spread(spec[0:16], w), spread(spec[16:32], w)
        parts = (sr * br + si * bi, sr * bi - si * br)
        for s in range(2):
            for jt in range(4):
                gs[jt, s, w] = parts[s][:, jt * WP : jt * WP + W]

    put_gs = pltpu.make_async_copy(gs, gspec_h, store_sem.at[1])
    put_gs.start()

    arrive(c6)
    s4[...] = matmul(txi[...], z[1].reshape(128, 128)).reshape(16, 16, 128)
    c7 = exchange(7, "gx", s4, v.at[1])
    drain(c4)
    drain(c5)
    drain(c6)
    arrive(c7)
    for half in range(2):
        rows = slice(half * 128, half * 128 + 128)
        gout[rows] = (
            local[rows]
            + jnp.dot(unpack_modes(v.at[1], half), zt[...], preferred_element_type=F32)
        ).astype(BF16)
    put_grad = pltpu.make_async_copy(gout, gfield_h, store_sem.at[2])
    put_grad.start()
    drain(c7)
    put_out.wait()
    put_gs.wait()
    put_grad.wait()


def on_device(field, cotangent, spectral_weight, pointwise_weight, channel_bias):
    tx, ty, tyi, txi, zt = tables()

    def rows(a):
        a = jnp.transpose(a, (1, 2, 0, 3)).reshape(8, W, Q)
        return jnp.pad(a, ((0, 0), (0, WP - W), (0, 0))).reshape(8 * WP, Q)

    def cells(a):
        a = a.reshape(2, 4, WP, Q)[:, :, :W]
        return jnp.transpose(a, (2, 0, 1, 3))

    pad = ((0, WP - W), (0, WP - W))
    pw = jnp.stack([jnp.pad(pointwise_weight.T, pad), jnp.pad(pointwise_weight, pad)])
    bias = jnp.pad(channel_bias, (0, WP - W)).reshape(WP, 1)
    weight = jnp.transpose(spectral_weight, (0, 1, 2, 4, 5, 3)).reshape(4, 2, W, 16, W)
    any_spec = pl.BlockSpec(memory_space=pl.ANY)
    out, gfield, gspec = pl.pallas_call(
        kernel,
        out_shape=(
            jax.ShapeDtypeStruct((256, Q), BF16),
            jax.ShapeDtypeStruct((256, Q), BF16),
            jax.ShapeDtypeStruct((4, 2, W, 16, W), F32),
        ),
        in_specs=[any_spec] * 10,
        out_specs=(any_spec,) * 3,
        scratch_shapes=[
            pltpu.VMEM((256, Q), BF16),
            pltpu.VMEM((256, Q), BF16),
            pltpu.VMEM((4, 2, W, 16, W), F32),
            pltpu.VMEM((2, WP, WP), BF16),
            pltpu.VMEM((WP, 1), F32),
            pltpu.VMEM((128, Q), BF16),
            pltpu.VMEM((128, 256), F32),
            pltpu.VMEM((32, 128), F32),
            pltpu.VMEM((128, 32), F32),
            pltpu.VMEM((256, 128), F32),
            pltpu.VMEM((2, W, 16, 128), F32),
            pltpu.VMEM((256, Q), F32),
            pltpu.VMEM((256, Q), F32),
            pltpu.VMEM((256, Q), BF16),
            pltpu.VMEM((256, Q), BF16),
            pltpu.VMEM((256, Q), BF16),
            pltpu.VMEM((4, 2, W, 16, W), F32),
            pltpu.VMEM((32, 128), F32),
            pltpu.VMEM((16, 16, 128), F32),
            pltpu.VMEM((16, 8, 128), F32),
            pltpu.VMEM((16, 8, 128), F32),
            pltpu.VMEM((16, 16, 128), F32),
            pltpu.VMEM((2, 16, 16, 128), F32),
            pltpu.VMEM((2, 16, 8, 128), F32),
            pltpu.VMEM((2, 16, 8, 128), F32),
            pltpu.VMEM((2, 16, 16, 128), F32),
            pltpu.SemaphoreType.DMA((10,)),
            pltpu.SemaphoreType.DMA((3,)),
            pltpu.SemaphoreType.DMA((8, 16)),
            pltpu.SemaphoreType.DMA((8, 16)),
        ],
        compiler_params=pltpu.CompilerParams(
            collective_id=0, has_side_effects=True, vmem_limit_bytes=40 << 20
        ),
    )(
        rows(field), rows(cotangent), weight, pw, bias,
        jnp.asarray(zt, BF16), tx, ty, tyi, txi,
    )
    grad = jnp.transpose(gspec.reshape(4, 2, W, 1, 16, W), (0, 1, 2, 5, 3, 4))
    return cells(out), cells(gfield), grad


def solution(mesh):
    return jax.shard_map(
        on_device,
        mesh=mesh,
        in_specs=(
            P(None, "gx", "gy", None),
            P(None, "gx", "gy", None),
            P("gx", None, None, None, "gy", None),
            P(),
            P(),
        ),
        out_specs=(
            P(None, "gx", "gy", None),
            P(None, "gx", "gy", None),
            P("gx", None, None, None, "gy", None),
        ),
        check_vma=False,
    )
```

```python
import math

import jax
import jax.numpy as jnp
import numpy as np
from jax import lax
from jax.experimental import pallas as pl
from jax.experimental.pallas import tpu as pltpu
from jax.sharding import PartitionSpec as P

W = 20
WP = 32
GX = 16
GY = 16
Q = 512
F32 = jnp.float32
BF16 = jnp.bfloat16
HIGHEST = lax.Precision.HIGHEST


def frequencies():
    j = np.arange(16)
    return np.where(j < 8, j, j - 16)


def rotation_blocks(length, sign):
    phase = np.mod(frequencies()[:, None] * np.arange(length)[None, :], length)
    angle = sign * 2.0 * np.pi * phase / length
    c, s = np.cos(angle) / np.sqrt(length), np.sin(angle) / np.sqrt(length)
    return np.stack([np.stack([c, -s]), np.stack([s, c])])


def split(a):
    a = a.astype(np.float32)
    hi = a.astype(BF16)
    lo = (a - hi.astype(np.float32)).astype(BF16)
    return np.concatenate([hi, lo, hi], axis=1)


def tables():
    fx = rotation_blocks(32, -1.0).reshape(2, 2, 16, 16, 2)
    tx = np.einsum("rskcx->krcsx", fx).reshape(32, 64)
    fy = rotation_blocks(64, -1.0).reshape(2, 2, 16, 16, 4)
    ty = np.einsum("rskpy->rkpsy", fy).reshape(32, 128)
    iy = rotation_blocks(64, 1.0).reshape(2, 2, 16, 16, 4)
    tyi = np.einsum("rskpy->prysk", iy).reshape(128, 32)
    ix = rotation_blocks(32, 1.0).reshape(2, 2, 16, 16, 2)
    txi = np.einsum("rskcx->crxks", ix).reshape(64, 32)
    z, t = np.arange(32), np.arange(16)
    f = frequencies()
    phase = (
        f[None, :, None, None] * z[None, None, :, None] * 16
        + np.arange(4)[:, None, None, None] * t[None, None, None, :] * 32
    )
    angle = np.mod(phase, 512).reshape(4, 16, 512) * (2.0 * np.pi / 512)
    zt = np.stack([np.cos(angle), -np.sin(angle)], axis=1).reshape(128, 512) / np.sqrt(512)
    return [zt.astype(np.float32).astype(BF16)] + [split(a) for a in (tx, ty, tyi, txi)]


def lane_blocks(rows):
    return lax.broadcasted_iota(jnp.int32, (rows, 128), 1) // WP


def block_transpose(parts):
    which = lane_blocks(parts[0].shape[0])
    out = []
    for b in range(4):
        acc = None
        for a in range(4):
            shift = ((a - b) * WP) % 128
            piece = parts[a] if shift == 0 else pltpu.roll(parts[a], shift, 1)
            acc = piece if acc is None else jnp.where(which == a, piece, acc)
        out.append(acc)
    return out


def kernel(
    field, cot, weight, pw, bias, zt_h, tx_h, ty_h, tyi_h, txi_h,
    out_h, gfield_h, gspec_h,
    fin, cin, wv, pwv, bv, zt, tx, ty, tyi, txi,
    u, cells, ccells, square, wt, local, pre, sig, outv, gout, gs, spec,
    s1, s2, s3, s4, e, d, z, v,
    load_sem, store_sem, send_sem, recv_sem,
):
    cx = lax.axis_index("gx")
    cy = lax.axis_index("gy")

    sources = (field, zt_h, tx_h, ty_h, tyi_h, txi_h, weight, pw, bias, cot)
    sinks = (fin, zt, tx, ty, tyi, txi, wv, pwv, bv, cin)
    loads = [
        pltpu.make_async_copy(a, b, load_sem.at[i]) for i, (a, b) in enumerate(zip(sources, sinks))
    ]
    for copy in loads:
        copy.start()

    def peer_x(off):
        dx, dz = off // 4, off % 4
        return lax.rem(cx // 4 + dx, 4) * 4 + lax.rem(lax.rem(cx, 4) + dz, 4)

    def peer_y(off):
        dz, rest = off // 8, off % 8
        dy, dc = rest // 2, rest % 2
        zl, yy, cc = cy // 8, lax.rem(cy // 2, 4), lax.rem(cy, 2)
        return lax.rem(zl + dz, 2) * 8 + lax.rem(yy + dy, 4) * 2 + lax.rem(cc + dc, 2)

    def ring(n):
        return min(n, 4 - n)

    order_x = sorted(range(1, 16), key=lambda o: -(ring(o // 4) + 2 * ring(o % 4)))
    order_y = sorted(range(1, 16), key=lambda o: -(3 * (o // 8) + 3 * ring((o % 8) // 2) + o % 2))

    barrier = pltpu.get_barrier_semaphore()
    for off in order_x:
        pl.semaphore_signal(
            barrier, inc=1, device_id=(peer_x(off), cy), device_id_type=pl.DeviceIdType.MESH
        )
    for off in order_y:
        pl.semaphore_signal(
            barrier, inc=1, device_id=(cx, peer_y(off)), device_id_type=pl.DeviceIdType.MESH
        )

    def exchange(step, axis, src, dst):
        copies = []
        for off in order_x if axis == "gx" else order_y:
            if axis == "gx":
                peer, me, device = peer_x(off), cx, (peer_x(off), cy)
            else:
                peer, me, device = peer_y(off), cy, (cx, peer_y(off))
            copy = pltpu.make_async_remote_copy(
                src_ref=src.at[peer],
                dst_ref=dst.at[me],
                send_sem=send_sem.at[step, off],
                recv_sem=recv_sem.at[step, off],
                device_id=device,
                device_id_type=pl.DeviceIdType.MESH,
            )
            copy.start()
            copies.append(copy)
        me = cx if axis == "gx" else cy
        dst[me] = src[me]
        return copies

    def arrive(copies):
        for copy in copies:
            copy.wait_recv()

    def drain(copies):
        for copy in copies:
            copy.wait_send()

    def pack_modes(values, send):
        spectra = lax.dot_general(
            zt[...], values[...], (((1,), (1,)), ((), ())), preferred_element_type=F32
        )
        for half in range(2):
            parts = [
                spectra[jt * 32 : jt * 32 + 32, half * 128 : half * 128 + 128] for jt in range(4)
            ]
            for sub, block in enumerate(block_transpose(parts)):
                for s in range(2):
                    send[:, s * 8 + half * 4 + sub, :] = block[s * 16 : s * 16 + 16]

    def unpack_modes(recv, half):
        parts = [
            jnp.concatenate([recv[:, s * 8 + half * 4 + sub, :] for s in range(2)], axis=0)
            for sub in range(4)
        ]
        stacked = jnp.concatenate(block_transpose(parts), axis=0)
        return stacked.T.astype(BF16)

    def matmul(table, b):
        hi = b.astype(BF16)
        lo = (b - hi.astype(F32)).astype(BF16)
        return jnp.dot(
            table[...], jnp.concatenate([hi, hi, lo], axis=0), preferred_element_type=F32
        )

    def y_to_lanes(recv, n):
        return jnp.concatenate([recv[pl.ds(y, n, stride=4), :] for y in range(4)], axis=1)

    def x_forward(recv, send):
        out = matmul(tx, y_to_lanes(recv, 64))
        for y in range(4):
            send[pl.ds(y, 32, stride=4), :] = out[:, y * 128 : y * 128 + 128]

    def x_inverse(recv, send):
        out = matmul(txi, y_to_lanes(recv, 32))
        for y in range(4):
            send[pl.ds(y, 64, stride=4), :] = out[:, y * 128 : y * 128 + 128]

    def to_cells(source, target):
        for x in range(2):
            target[:, 4 * x : 4 * x + 4, :] = source[:, x].astype(F32)

    def from_cells(source, target):
        for x in range(2):
            target[:, x] = source[:, 4 * x : 4 * x + 4, :].astype(BF16)

    kappa = jnp.where(lax.broadcasted_iota(jnp.int32, (16, 128), 1) < WP, 1.0, 2.0).astype(F32)
    gather_base = lane_blocks(16) * WP

    def spread(value, w):
        return jnp.take_along_axis(value, gather_base + w, axis=1)

    loads[0].wait()
    to_cells(fin, cells)
    pad = jnp.zeros((WP - W, Q), F32)
    for xy in range(8):
        u[xy * WP : xy * WP + WP] = jnp.concatenate([cells[:, xy, :], pad], axis=0).astype(BF16)
    loads[1].wait()
    pack_modes(u, s1)
    pl.semaphore_wait(barrier, 30)
    c0 = exchange(0, "gx", s1, e.at[0])

    for copy in loads[2:]:
        copy.wait()
    zeros = jnp.zeros((16, WP - W), F32)

    @pl.loop(0, W)
    def _(w):
        for s in range(2):
            pieces = []
            for jt in range(4):
                pieces += [wv[jt, s, w], zeros]
            wt[s, w] = jnp.concatenate(pieces, axis=1)

    square[...] = jnp.zeros((128, 128), F32)
    square[0:W, 0:W] = pwv[...].astype(F32)
    square[WP : WP + 1, 0:W] = bv[...].reshape(1, W)
    turned = square[...].T
    pw_back = square[0:WP, 0:WP].astype(BF16)
    pw_forward = turned[0:WP, 0:WP].astype(BF16)
    bias_column = turned[0:W, WP : WP + 1]
    for xy in range(8):
        rows = slice(xy * WP, xy * WP + WP)
        local[xy] = jnp.dot(pw_forward, u[rows], preferred_element_type=F32)[0:W] + bias_column
    to_cells(cin, ccells)

    arrive(c0)
    x_forward(e.at[0].reshape(256, 128), s2.reshape(128, 128))
    c1 = exchange(1, "gy", s2, d.at[0])
    arrive(c1)
    spec[...] = matmul(ty, d[0].reshape(128, 128))

    acc_r = acc_i = jnp.zeros((16, 128), F32)
    for w in range(W):
        sr, si = spread(spec[0:16], w), spread(spec[16:32], w)
        wr, wi = wt[0, w], wt[1, w]
        acc_r = acc_r + (wr * sr - wi * si)
        acc_i = acc_i + (wi * sr + wr * si)
    mixed = jnp.concatenate([acc_r * kappa, acc_i * kappa], axis=0)

    s3[...] = matmul(tyi, mixed).reshape(16, 8, 128)
    c2 = exchange(2, "gy", s3, z.at[0])
    arrive(c2)
    x_inverse(z.at[0].reshape(128, 128), s4.reshape(256, 128))
    c3 = exchange(3, "gx", s4, v.at[0])
    drain(c0)
    arrive(c3)

    root = math.sqrt(2.0 / math.pi)
    cubic = 0.044715
    for half in range(2):
        spatial = jnp.dot(unpack_modes(v.at[0], half), zt[...], preferred_element_type=F32)
        for sub in range(4):
            xy = half * 4 + sub
            p = local[xy] + spatial[sub * WP : sub * WP + W]
            pre[xy] = p
            p2 = p * p
            t = jnp.tanh(p * (root * cubic * p2 + root))
            b = p * (1.5 * root * cubic * p2 + 0.5 * root)
            slope = t * (0.5 - b * t) + (b + 0.5)
            signal = ccells[:, xy, :] * slope
            sig[xy * WP : xy * WP + WP] = jnp.concatenate([signal, pad], axis=0).astype(BF16)

    pack_modes(sig, s1)
    c4 = exchange(4, "gx", s1, e.at[1])

    for xy in range(8):
        p = pre[xy]
        t = jnp.tanh(p * (root * cubic * (p * p) + root))
        cells[:, xy, :] = 0.5 * p * (1.0 + t)
        rows = slice(xy * WP, xy * WP + WP)
        local[xy] = jnp.dot(pw_back, sig[rows], preferred_element_type=F32)[0:W]
    from_cells(cells, outv)
    put_out = pltpu.make_async_copy(outv, out_h, store_sem.at[0])
    put_out.start()
    drain(c1)
    drain(c2)
    drain(c3)
    arrive(c4)
    x_forward(e.at[1].reshape(256, 128), s2.reshape(128, 128))
    c5 = exchange(5, "gy", s2, d.at[1])
    arrive(c5)
    back = matmul(ty, d[1].reshape(128, 128))
    br, bi = back[0:16] * kappa, back[16:32] * kappa

    lane = lax.broadcasted_iota(jnp.int32, (32, 128), 1)

    def combine(a, b, h):
        bit = (lane & h) != 0
        flip = lane ^ h
        if b is None:
            return jnp.where(bit, 0.0, a + jnp.take_along_axis(a, flip, axis=1))
        return jnp.where(bit, b, a) + jnp.take_along_axis(jnp.where(bit, a, b), flip, axis=1)

    def product(w):
        wr, wi = wt[0, w], wt[1, w]
        return jnp.concatenate([wr * br + wi * bi, wr * bi - wi * br], axis=0)

    def reduce_tree(w, h):
        if h == WP:
            return product(w) if w < W else None
        a, b = reduce_tree(w, h * 2), reduce_tree(w + h, h * 2)
        return combine(a, b, h) if a is not None else None

    s3[...] = matmul(tyi, reduce_tree(0, 1)).reshape(16, 8, 128)
    c6 = exchange(6, "gy", s3, z.at[1])

    @pl.loop(0, W)
    def _(w):
        sr, si = spread(spec[0:16], w), spread(spec[16:32], w)
        parts = (sr * br + si * bi, sr * bi - si * br)
        for s in range(2):
            for jt in range(4):
                gs[jt, s, w] = parts[s][:, jt * WP : jt * WP + W]

    put_gs = pltpu.make_async_copy(gs, gspec_h, store_sem.at[1])
    put_gs.start()

    arrive(c6)
    x_inverse(z.at[1].reshape(128, 128), s4.reshape(256, 128))
    c7 = exchange(7, "gx", s4, v.at[1])
    drain(c4)
    drain(c5)
    drain(c6)
    arrive(c7)
    for half in range(2):
        spatial = jnp.dot(unpack_modes(v.at[1], half), zt[...], preferred_element_type=F32)
        for sub in range(4):
            xy = half * 4 + sub
            cells[:, xy, :] = local[xy] + spatial[sub * WP : sub * WP + W]
    from_cells(cells, gout)
    put_grad = pltpu.make_async_copy(gout, gfield_h, store_sem.at[2])
    put_grad.start()
    drain(c7)
    put_out.wait()
    put_gs.wait()
    put_grad.wait()


def on_device(field, cotangent, spectral_weight, pointwise_weight, channel_bias):
    constants = tables()
    weight = jnp.transpose(spectral_weight, (0, 1, 2, 4, 5, 3)).reshape(4, 2, W, 16, W)
    hbm = pl.BlockSpec(memory_space=pltpu.MemorySpace.HBM)
    out, gfield, gspec = pl.pallas_call(
        kernel,
        out_shape=(
            jax.ShapeDtypeStruct((W, 2, 4, Q), BF16),
            jax.ShapeDtypeStruct((W, 2, 4, Q), BF16),
            jax.ShapeDtypeStruct((4, 2, W, 16, W), F32),
        ),
        in_specs=[hbm] * 10,
        out_specs=(hbm,) * 3,
        scratch_shapes=[
            pltpu.VMEM((W, 2, 4, Q), BF16),
            pltpu.VMEM((W, 2, 4, Q), BF16),
            pltpu.VMEM((4, 2, W, 16, W), F32),
            pltpu.VMEM((W, W), BF16),
            pltpu.VMEM((W,), F32),
            pltpu.VMEM((128, Q), BF16),
            pltpu.VMEM((32, 192), BF16),
            pltpu.VMEM((32, 384), BF16),
            pltpu.VMEM((128, 96), BF16),
            pltpu.VMEM((64, 96), BF16),
            pltpu.VMEM((256, Q), BF16),
            pltpu.VMEM((W, 8, Q), F32),
            pltpu.VMEM((W, 8, Q), F32),
            pltpu.VMEM((128, 128), F32),
            pltpu.VMEM((2, W, 16, 128), F32),
            pltpu.VMEM((8, W, Q), F32),
            pltpu.VMEM((8, W, Q), F32),
            pltpu.VMEM((256, Q), BF16),
            pltpu.VMEM((W, 2, 4, Q), BF16),
            pltpu.VMEM((W, 2, 4, Q), BF16),
            pltpu.VMEM((4, 2, W, 16, W), F32),
            pltpu.VMEM((32, 128), F32),
            pltpu.VMEM((16, 16, 128), F32),
            pltpu.VMEM((16, 8, 128), F32),
            pltpu.VMEM((16, 8, 128), F32),
            pltpu.VMEM((16, 16, 128), F32),
            pltpu.VMEM((2, 16, 16, 128), F32),
            pltpu.VMEM((2, 16, 8, 128), F32),
            pltpu.VMEM((2, 16, 8, 128), F32),
            pltpu.VMEM((2, 16, 16, 128), F32),
            pltpu.SemaphoreType.DMA((10,)),
            pltpu.SemaphoreType.DMA((3,)),
            pltpu.SemaphoreType.DMA((8, 16)),
            pltpu.SemaphoreType.DMA((8, 16)),
        ],
        compiler_params=pltpu.CompilerParams(
            collective_id=0, has_side_effects=True, vmem_limit_bytes=40 << 20
        ),
    )(field, cotangent, weight, pointwise_weight, channel_bias, *constants)
    grad = jnp.transpose(gspec.reshape(4, 2, W, 1, 16, W), (0, 1, 2, 5, 3, 4))
    return out, gfield, grad


def solution(mesh):
    return jax.shard_map(
        on_device,
        mesh=mesh,
        in_specs=(
            P(None, "gx", "gy", None),
            P(None, "gx", "gy", None),
            P("gx", None, None, None, "gy", None),
            P(),
            P(),
        ),
        out_specs=(
            P(None, "gx", "gy", None),
            P(None, "gx", "gy", None),
            P("gx", None, None, None, "gy", None),
        ),
        check_vma=False,
    )
```

```python
import math

import jax
import jax.numpy as jnp
import numpy as np
from jax import lax
from jax.experimental import pallas as pl
from jax.experimental.pallas import tpu as pltpu
from jax.sharding import PartitionSpec as P

W = 20
WP = 32
GX = 16
GY = 16
Q = 512
F32 = jnp.float32
BF16 = jnp.bfloat16
HIGHEST = lax.Precision.HIGHEST


def frequencies():
    j = np.arange(16)
    return np.where(j < 8, j, j - 16)


def rotation_blocks(length, sign):
    phase = np.mod(frequencies()[:, None] * np.arange(length)[None, :], length)
    angle = sign * 2.0 * np.pi * phase / length
    c, s = np.cos(angle) / np.sqrt(length), np.sin(angle) / np.sqrt(length)
    return np.stack([np.stack([c, -s]), np.stack([s, c])])


def split(a):
    a = a.astype(np.float32)
    hi = a.astype(BF16)
    lo = (a - hi.astype(np.float32)).astype(BF16)
    return np.concatenate([hi, lo, hi], axis=1)


def tables():
    fx = rotation_blocks(32, -1.0).reshape(2, 2, 16, 16, 2)
    tx = np.einsum("rskcx->krcsx", fx).reshape(32, 64)
    fy = rotation_blocks(64, -1.0).reshape(2, 2, 16, 16, 4)
    ty = np.einsum("rskpy->rkpsy", fy).reshape(32, 128)
    iy = rotation_blocks(64, 1.0).reshape(2, 2, 16, 16, 4)
    tyi = np.einsum("rskpy->prysk", iy).reshape(128, 32)
    ix = rotation_blocks(32, 1.0).reshape(2, 2, 16, 16, 2)
    txi = np.einsum("rskcx->crxks", ix).reshape(64, 32)
    z, t = np.arange(32), np.arange(16)
    f = frequencies()
    phase = (
        f[None, :, None, None] * z[None, None, :, None] * 16
        + np.arange(4)[:, None, None, None] * t[None, None, None, :] * 32
    )
    angle = np.mod(phase, 512).reshape(4, 16, 512) * (2.0 * np.pi / 512)
    zt = np.stack([np.cos(angle), -np.sin(angle)], axis=1).reshape(128, 512) / np.sqrt(512)
    return [zt.astype(np.float32).astype(BF16)] + [split(a) for a in (tx, ty, tyi, txi)]


def lane_blocks(rows):
    return lax.broadcasted_iota(jnp.int32, (rows, 128), 1) // WP


def block_transpose(parts):
    which = lane_blocks(parts[0].shape[0])
    out = []
    for b in range(4):
        acc = None
        for a in range(4):
            shift = ((a - b) * WP) % 128
            piece = parts[a] if shift == 0 else pltpu.roll(parts[a], shift, 1)
            acc = piece if acc is None else jnp.where(which == a, piece, acc)
        out.append(acc)
    return out


def kernel(
    field, cot, weight, pw, bias, zt_h, tx_h, ty_h, tyi_h, txi_h,
    out_h, gfield_h, gspec_h,
    fin, cin, wv, pwv, bv, zt, tx, ty, tyi, txi,
    u, cells, ccells, square, wt, local, pre, sig, outv, gout, gs, spec,
    s1, s2, s3, s4, e, d, z, v,
    load_sem, store_sem, send_sem, recv_sem,
):
    cx = lax.axis_index("gx")
    cy = lax.axis_index("gy")

    sources = (field, zt_h, tx_h, ty_h, tyi_h, txi_h, weight, pw, bias, cot)
    sinks = (fin, zt, tx, ty, tyi, txi, wv, pwv, bv, cin)
    loads = [
        pltpu.make_async_copy(a, b, load_sem.at[i]) for i, (a, b) in enumerate(zip(sources, sinks))
    ]
    for copy in loads:
        copy.start()

    def peer_x(off):
        dx, dz = off // 4, off % 4
        return lax.rem(cx // 4 + dx, 4) * 4 + lax.rem(lax.rem(cx, 4) + dz, 4)

    def peer_y(off):
        dz, rest = off // 8, off % 8
        dy, dc = rest // 2, rest % 2
        zl, yy, cc = cy // 8, lax.rem(cy // 2, 4), lax.rem(cy, 2)
        return lax.rem(zl + dz, 2) * 8 + lax.rem(yy + dy, 4) * 2 + lax.rem(cc + dc, 2)

    def ring(n):
        return min(n, 4 - n)

    order_x = sorted(range(1, 16), key=lambda o: -(ring(o // 4) + 2 * ring(o % 4)))
    order_y = sorted(range(1, 16), key=lambda o: -(3 * (o // 8) + 3 * ring((o % 8) // 2) + o % 2))

    barrier = pltpu.get_barrier_semaphore()
    for off in order_x:
        pl.semaphore_signal(
            barrier, inc=1, device_id=(peer_x(off), cy), device_id_type=pl.DeviceIdType.MESH
        )
    for off in order_y:
        pl.semaphore_signal(
            barrier, inc=1, device_id=(cx, peer_y(off)), device_id_type=pl.DeviceIdType.MESH
        )

    def exchange(step, axis, src, dst):
        copies = []
        for off in order_x if axis == "gx" else order_y:
            if axis == "gx":
                peer, me, device = peer_x(off), cx, (peer_x(off), cy)
            else:
                peer, me, device = peer_y(off), cy, (cx, peer_y(off))
            copy = pltpu.make_async_remote_copy(
                src_ref=src.at[peer],
                dst_ref=dst.at[me],
                send_sem=send_sem.at[step, off],
                recv_sem=recv_sem.at[step, off],
                device_id=device,
                device_id_type=pl.DeviceIdType.MESH,
            )
            copy.start()
            copies.append(copy)
        me = cx if axis == "gx" else cy
        dst[me] = src[me]
        return copies

    def arrive(copies):
        for copy in copies:
            copy.wait_recv()

    def drain(copies):
        for copy in copies:
            copy.wait_send()

    def pack_modes(values, send):
        spectra = lax.dot_general(
            zt[...], values[...], (((1,), (1,)), ((), ())), preferred_element_type=F32
        )
        for half in range(2):
            parts = [
                spectra[jt * 32 : jt * 32 + 32, half * 128 : half * 128 + 128] for jt in range(4)
            ]
            for sub, block in enumerate(block_transpose(parts)):
                for s in range(2):
                    send[:, s * 8 + half * 4 + sub, :] = block[s * 16 : s * 16 + 16]

    def unpack_modes(recv, half):
        parts = [
            jnp.concatenate([recv[:, s * 8 + half * 4 + sub, :] for s in range(2)], axis=0)
            for sub in range(4)
        ]
        stacked = jnp.concatenate(block_transpose(parts), axis=0)
        return stacked.T.astype(BF16)

    def matmul(table, b):
        hi = b.astype(BF16)
        lo = (b - hi.astype(F32)).astype(BF16)
        return jnp.dot(
            table[...], jnp.concatenate([hi, hi, lo], axis=0), preferred_element_type=F32
        )

    def y_to_lanes(recv, n):
        return jnp.concatenate([recv[pl.ds(y, n, stride=4), :] for y in range(4)], axis=1)

    def x_forward(recv, send):
        out = matmul(tx, y_to_lanes(recv, 64))
        for y in range(4):
            send[pl.ds(y, 32, stride=4), :] = out[:, y * 128 : y * 128 + 128]

    def x_inverse(recv, send):
        out = matmul(txi, y_to_lanes(recv, 32))
        for y in range(4):
            send[pl.ds(y, 64, stride=4), :] = out[:, y * 128 : y * 128 + 128]

    def to_cells(source, target):
        for x in range(2):
            target[:, 4 * x : 4 * x + 4, :] = source[:, x].astype(F32)

    def from_cells(source, target):
        for x in range(2):
            target[:, x] = source[:, 4 * x : 4 * x + 4, :].astype(BF16)

    kappa = jnp.where(lax.broadcasted_iota(jnp.int32, (16, 128), 1) < WP, 1.0, 2.0).astype(F32)
    gather_base = lane_blocks(16) * WP

    def spread(value, w):
        return jnp.take_along_axis(value, gather_base + w, axis=1)

    loads[0].wait()
    to_cells(fin, cells)
    pad = jnp.zeros((WP - W, Q), F32)
    for xy in range(8):
        u[xy * WP : xy * WP + WP] = jnp.concatenate([cells[:, xy, :], pad], axis=0).astype(BF16)
    loads[1].wait()
    pack_modes(u, s1)
    pl.semaphore_wait(barrier, 30)
    c0 = exchange(0, "gx", s1, e.at[0])

    for copy in loads[2:]:
        copy.wait()
    zeros = jnp.zeros((16, WP - W), F32)

    @pl.loop(0, W)
    def _(w):
        for s in range(2):
            pieces = []
            for jt in range(4):
                pieces += [wv[jt, s, w], zeros]
            wt[s, w] = jnp.concatenate(pieces, axis=1)

    square[...] = jnp.zeros((128, 128), F32)
    square[0:W, 0:W] = pwv[...].astype(F32)
    square[WP : WP + 1, 0:W] = bv[...].reshape(1, W)
    turned = square[...].T
    pw_back = square[0:WP, 0:WP].astype(BF16)
    pw_forward = turned[0:WP, 0:WP].astype(BF16)
    bias_column = turned[0:W, WP : WP + 1]
    for xy in range(8):
        rows = slice(xy * WP, xy * WP + WP)
        local[xy] = jnp.dot(pw_forward, u[rows], preferred_element_type=F32)[0:W] + bias_column
    to_cells(cin, ccells)

    arrive(c0)
    x_forward(e.at[0].reshape(256, 128), s2.reshape(128, 128))
    c1 = exchange(1, "gy", s2, d.at[0])
    arrive(c1)
    spec[...] = matmul(ty, d[0].reshape(128, 128))

    acc_r = acc_i = jnp.zeros((16, 128), F32)
    for w in range(W):
        sr, si = spread(spec[0:16], w), spread(spec[16:32], w)
        wr, wi = wt[0, w], wt[1, w]
        acc_r = acc_r + (wr * sr - wi * si)
        acc_i = acc_i + (wi * sr + wr * si)
    mixed = jnp.concatenate([acc_r * kappa, acc_i * kappa], axis=0)

    s3[...] = matmul(tyi, mixed).reshape(16, 8, 128)
    c2 = exchange(2, "gy", s3, z.at[0])
    arrive(c2)
    x_inverse(z.at[0].reshape(128, 128), s4.reshape(256, 128))
    c3 = exchange(3, "gx", s4, v.at[0])
    drain(c0)
    arrive(c3)

    root = math.sqrt(2.0 / math.pi)
    cubic = 0.044715
    for half in range(2):
        spatial = jnp.dot(unpack_modes(v.at[0], half), zt[...], preferred_element_type=F32)
        for sub in range(4):
            xy = half * 4 + sub
            p = local[xy] + spatial[sub * WP : sub * WP + W]
            pre[xy] = p
            p2 = p * p
            t = jnp.tanh(p * (root * cubic * p2 + root))
            b = p * (1.5 * root * cubic * p2 + 0.5 * root)
            slope = t * (0.5 - b * t) + (b + 0.5)
            signal = ccells[:, xy, :] * slope
            sig[xy * WP : xy * WP + WP] = jnp.concatenate([signal, pad], axis=0).astype(BF16)

    pack_modes(sig, s1)
    c4 = exchange(4, "gx", s1, e.at[1])

    for xy in range(8):
        p = pre[xy]
        t = jnp.tanh(p * (root * cubic * (p * p) + root))
        cells[:, xy, :] = 0.5 * p * (1.0 + t)
        rows = slice(xy * WP, xy * WP + WP)
        local[xy] = jnp.dot(pw_back, sig[rows], preferred_element_type=F32)[0:W]
    from_cells(cells, outv)
    put_out = pltpu.make_async_copy(outv, out_h, store_sem.at[0])
    put_out.start()
    drain(c1)
    drain(c2)
    drain(c3)
    arrive(c4)
    x_forward(e.at[1].reshape(256, 128), s2.reshape(128, 128))
    c5 = exchange(5, "gy", s2, d.at[1])
    arrive(c5)
    back = matmul(ty, d[1].reshape(128, 128))
    br, bi = back[0:16] * kappa, back[16:32] * kappa

    lane = lax.broadcasted_iota(jnp.int32, (32, 128), 1)

    def combine(a, b, h):
        bit = (lane & h) != 0
        flip = lane ^ h
        if b is None:
            return jnp.where(bit, 0.0, a + jnp.take_along_axis(a, flip, axis=1))
        return jnp.where(bit, b, a) + jnp.take_along_axis(jnp.where(bit, a, b), flip, axis=1)

    def product(w):
        wr, wi = wt[0, w], wt[1, w]
        return jnp.concatenate([wr * br + wi * bi, wr * bi - wi * br], axis=0)

    def reduce_tree(w, h):
        if h == WP:
            return product(w) if w < W else None
        a, b = reduce_tree(w, h * 2), reduce_tree(w + h, h * 2)
        return combine(a, b, h) if a is not None else None

    s3[...] = matmul(tyi, reduce_tree(0, 1)).reshape(16, 8, 128)
    c6 = exchange(6, "gy", s3, z.at[1])

    @pl.loop(0, W)
    def _(w):
        sr, si = spread(spec[0:16], w), spread(spec[16:32], w)
        parts = (sr * br + si * bi, sr * bi - si * br)
        for s in range(2):
            for jt in range(4):
                gs[jt, s, w] = parts[s][:, jt * WP : jt * WP + W]

    put_gs = pltpu.make_async_copy(gs, gspec_h, store_sem.at[1])
    put_gs.start()

    arrive(c6)
    x_inverse(z.at[1].reshape(128, 128), s4.reshape(256, 128))
    c7 = exchange(7, "gx", s4, v.at[1])
    drain(c4)
    drain(c5)
    drain(c6)
    arrive(c7)
    for half in range(2):
        spatial = jnp.dot(unpack_modes(v.at[1], half), zt[...], preferred_element_type=F32)
        for sub in range(4):
            xy = half * 4 + sub
            cells[:, xy, :] = local[xy] + spatial[sub * WP : sub * WP + W]
    from_cells(cells, gout)
    put_grad = pltpu.make_async_copy(gout, gfield_h, store_sem.at[2])
    put_grad.start()
    drain(c7)
    put_out.wait()
    put_gs.wait()
    put_grad.wait()


def on_device(field, cotangent, spectral_weight, pointwise_weight, channel_bias):
    constants = tables()
    weight = jnp.transpose(spectral_weight, (0, 1, 2, 4, 5, 3)).reshape(4, 2, W, 16, W)
    hbm = pl.BlockSpec(memory_space=pltpu.MemorySpace.HBM)
    out, gfield, gspec = pl.pallas_call(
        kernel,
        out_shape=(
            jax.ShapeDtypeStruct((W, 2, 4, Q), BF16),
            jax.ShapeDtypeStruct((W, 2, 4, Q), BF16),
            jax.ShapeDtypeStruct((4, 2, W, 16, W), F32),
        ),
        in_specs=[hbm] * 10,
        out_specs=(hbm,) * 3,
        scratch_shapes=[
            pltpu.VMEM((W, 2, 4, Q), BF16),
            pltpu.VMEM((W, 2, 4, Q), BF16),
            pltpu.VMEM((4, 2, W, 16, W), F32),
            pltpu.VMEM((W, W), BF16),
            pltpu.VMEM((W,), F32),
            pltpu.VMEM((128, Q), BF16),
            pltpu.VMEM((32, 192), BF16),
            pltpu.VMEM((32, 384), BF16),
            pltpu.VMEM((128, 96), BF16),
            pltpu.VMEM((64, 96), BF16),
            pltpu.VMEM((256, Q), BF16),
            pltpu.VMEM((W, 8, Q), F32),
            pltpu.VMEM((W, 8, Q), F32),
            pltpu.VMEM((128, 128), F32),
            pltpu.VMEM((2, W, 16, 128), F32),
            pltpu.VMEM((8, W, Q), F32),
            pltpu.VMEM((8, W, Q), F32),
            pltpu.VMEM((256, Q), BF16),
            pltpu.VMEM((W, 2, 4, Q), BF16),
            pltpu.VMEM((W, 2, 4, Q), BF16),
            pltpu.VMEM((4, 2, W, 16, W), F32),
            pltpu.VMEM((32, 128), F32),
            pltpu.VMEM((16, 16, 128), F32),
            pltpu.VMEM((16, 8, 128), F32),
            pltpu.VMEM((16, 8, 128), F32),
            pltpu.VMEM((16, 16, 128), F32),
            pltpu.VMEM((2, 16, 16, 128), F32),
            pltpu.VMEM((2, 16, 8, 128), F32),
            pltpu.VMEM((2, 16, 8, 128), F32),
            pltpu.VMEM((2, 16, 16, 128), F32),
            pltpu.SemaphoreType.DMA((10,)),
            pltpu.SemaphoreType.DMA((3,)),
            pltpu.SemaphoreType.DMA((8, 16)),
            pltpu.SemaphoreType.DMA((8, 16)),
        ],
        compiler_params=pltpu.CompilerParams(
            collective_id=0, has_side_effects=True, vmem_limit_bytes=67043328
        ),
    )(field, cotangent, weight, pointwise_weight, channel_bias, *constants)
    grad = jnp.transpose(gspec.reshape(4, 2, W, 1, 16, W), (0, 1, 2, 5, 3, 4))
    return out, gfield, grad


def solution(mesh):
    return jax.shard_map(
        on_device,
        mesh=mesh,
        in_specs=(
            P(None, "gx", "gy", None),
            P(None, "gx", "gy", None),
            P("gx", None, None, None, "gy", None),
            P(),
            P(),
        ),
        out_specs=(
            P(None, "gx", "gy", None),
            P(None, "gx", "gy", None),
            P("gx", None, None, None, "gy", None),
        ),
        check_vma=False,
    )
```

```python
import math

import jax
import jax.numpy as jnp
import numpy as np
from jax import lax
from jax.experimental import pallas as pl
from jax.experimental.pallas import tpu as pltpu
from jax.sharding import PartitionSpec as P

W = 20
WP = 32
GX = 16
GY = 16
Q = 512
F32 = jnp.float32
BF16 = jnp.bfloat16
VMEM = 67043328
RESULTS = 2 * 20 * 8 * 512 * 2 + 160 * 16 * 128 * 4


def frequencies():
    j = np.arange(16)
    return np.where(j < 8, j, j - 16)


def rotation_blocks(length, sign):
    phase = np.mod(frequencies()[:, None] * np.arange(length)[None, :], length)
    angle = sign * 2.0 * np.pi * phase / length
    c, s = np.cos(angle) / np.sqrt(length), np.sin(angle) / np.sqrt(length)
    return np.stack([np.stack([c, -s]), np.stack([s, c])])


def split(a):
    a = a.astype(np.float32)
    hi = a.astype(BF16)
    lo = (a - hi.astype(np.float32)).astype(BF16)
    return np.concatenate([hi, lo, hi], axis=1)


def tables():
    fx = rotation_blocks(32, -1.0).reshape(2, 2, 16, 16, 2)
    tx = np.einsum("rskcx->krcsx", fx).reshape(32, 64)
    fy = rotation_blocks(64, -1.0).reshape(2, 2, 16, 16, 4)
    ty = np.einsum("rskpy->rkpsy", fy).reshape(32, 128)
    iy = rotation_blocks(64, 1.0).reshape(2, 2, 16, 16, 4)
    tyi = np.einsum("rskpy->prysk", iy).reshape(128, 32)
    ix = rotation_blocks(32, 1.0).reshape(2, 2, 16, 16, 2)
    txi = np.einsum("rskcx->crxks", ix).reshape(64, 32)
    z, t = np.arange(32), np.arange(16)
    f = frequencies()
    phase = (
        f[None, :, None, None] * z[None, None, :, None] * 16
        + np.arange(4)[:, None, None, None] * t[None, None, None, :] * 32
    )
    angle = np.mod(phase, 512).reshape(4, 16, 512) * (2.0 * np.pi / 512)
    zt = np.stack([np.cos(angle), -np.sin(angle)], axis=1).reshape(128, 512) / np.sqrt(512)
    return [zt.astype(np.float32).astype(BF16)] + [split(a) for a in (tx, ty, tyi, txi)]


def lane_blocks(rows):
    return lax.broadcasted_iota(jnp.int32, (rows, 128), 1) // WP


def block_transpose(parts):
    which = lane_blocks(parts[0].shape[0])
    out = []
    for b in range(4):
        acc = None
        for a in range(4):
            shift = ((a - b) * WP) % 128
            piece = parts[a] if shift == 0 else pltpu.roll(parts[a], shift, 1)
            acc = piece if acc is None else jnp.where(which == a, piece, acc)
        out.append(acc)
    return out


def kernel(
    field, cot, weight, pw, bias, zt_h, tx_h, ty_h, tyi_h, txi_h,
    outv, gout, gs,
    fin, cin, wv, pwv, bv, zt, tx, ty, tyi, txi,
    u, cells, ccells, square, wt, local, pre, sig, spec,
    s1, s2, s3, s4, e, d, z, v,
    load_sem, send_sem, recv_sem,
):
    cx = lax.axis_index("gx")
    cy = lax.axis_index("gy")

    turn_x = [lax.rem(cx // 4 + i, 4) * 4 for i in range(4)]
    turn_z = [lax.rem(lax.rem(cx, 4) + i, 4) for i in range(4)]
    turn_l = [lax.rem(cy // 8 + i, 2) * 8 for i in range(2)]
    turn_y = [lax.rem(cy // 2 + i, 4) * 2 for i in range(4)]
    turn_c = [lax.rem(cy + i, 2) for i in range(2)]
    peer_x = [turn_x[o // 4] + turn_z[o % 4] for o in range(16)]
    peer_y = [turn_l[o // 8] + turn_y[(o % 8) // 2] + turn_c[o % 2] for o in range(16)]

    def ring(n):
        return min(n, 4 - n)

    order_x = sorted(range(1, 16), key=lambda o: -(ring(o // 4) + 2 * ring(o % 4)))
    order_y = sorted(range(1, 16), key=lambda o: -(3 * (o // 8) + 3 * ring((o % 8) // 2) + o % 2))

    barrier = pltpu.get_barrier_semaphore()
    for off in order_x:
        pl.semaphore_signal(
            barrier, inc=1, device_id=(peer_x[off], cy), device_id_type=pl.DeviceIdType.MESH
        )
    for off in order_y:
        pl.semaphore_signal(
            barrier, inc=1, device_id=(cx, peer_y[off]), device_id_type=pl.DeviceIdType.MESH
        )

    sources = (field, zt_h, tx_h, ty_h, tyi_h, txi_h, weight, pw, bias, cot)
    sinks = (fin, zt, tx, ty, tyi, txi, wv, pwv, bv, cin)
    loads = [
        pltpu.make_async_copy(a, b, load_sem.at[i]) for i, (a, b) in enumerate(zip(sources, sinks))
    ]
    for copy in loads:
        copy.start()

    def exchange(step, axis, src, dst):
        copies = []
        for off in order_x if axis == "gx" else order_y:
            if axis == "gx":
                peer, me, device = peer_x[off], cx, (peer_x[off], cy)
            else:
                peer, me, device = peer_y[off], cy, (cx, peer_y[off])
            copy = pltpu.make_async_remote_copy(
                src_ref=src.at[peer],
                dst_ref=dst.at[me],
                send_sem=send_sem.at[step, off],
                recv_sem=recv_sem.at[step, off],
                device_id=device,
                device_id_type=pl.DeviceIdType.MESH,
            )
            copy.start()
            copies.append(copy)
        me = cx if axis == "gx" else cy
        dst[me] = src[me]
        return copies

    def arrive(copies):
        for copy in copies:
            copy.wait_recv()

    def drain(copies):
        for copy in copies:
            copy.wait_send()

    def pack_modes(values, send):
        spectra = lax.dot_general(
            zt[...], values[...], (((1,), (1,)), ((), ())), preferred_element_type=F32
        )
        for half in range(2):
            parts = [
                spectra[jt * 32 : jt * 32 + 32, half * 128 : half * 128 + 128] for jt in range(4)
            ]
            for sub, block in enumerate(block_transpose(parts)):
                for s in range(2):
                    send[:, s * 8 + half * 4 + sub, :] = block[s * 16 : s * 16 + 16]

    def unpack_modes(recv, half):
        parts = [
            jnp.concatenate([recv[:, s * 8 + half * 4 + sub, :] for s in range(2)], axis=0)
            for sub in range(4)
        ]
        stacked = jnp.concatenate(block_transpose(parts), axis=0)
        return stacked.T.astype(BF16)

    def matmul(table, b):
        hi = b.astype(BF16)
        lo = (b - hi.astype(F32)).astype(BF16)
        return jnp.dot(
            table[...], jnp.concatenate([hi, hi, lo], axis=0), preferred_element_type=F32
        )

    def y_to_lanes(recv, n):
        return jnp.concatenate([recv[pl.ds(y, n, stride=4), :] for y in range(4)], axis=1)

    def x_forward(recv, send):
        out = matmul(tx, y_to_lanes(recv, 64))
        for y in range(4):
            send[pl.ds(y, 32, stride=4), :] = out[:, y * 128 : y * 128 + 128]

    def x_inverse(recv, send):
        out = matmul(txi, y_to_lanes(recv, 32))
        for y in range(4):
            send[pl.ds(y, 64, stride=4), :] = out[:, y * 128 : y * 128 + 128]

    def to_cells(source, target):
        for x in range(2):
            target[:, 4 * x : 4 * x + 4, :] = source[:, x].astype(F32)

    def from_cells(source, target):
        for x in range(2):
            target[:, x] = source[:, 4 * x : 4 * x + 4, :].astype(BF16)

    kappa = jnp.where(lax.broadcasted_iota(jnp.int32, (16, 128), 1) < WP, 1.0, 2.0).astype(F32)
    gather_base = lane_blocks(16) * WP

    def spread(value, w):
        return jnp.take_along_axis(value, gather_base + w, axis=1)

    loads[0].wait()
    to_cells(fin, cells)
    pad = jnp.zeros((WP - W, Q), F32)
    for xy in range(8):
        u[xy * WP : xy * WP + WP] = jnp.concatenate([cells[:, xy, :], pad], axis=0).astype(BF16)
    loads[1].wait()
    pack_modes(u, s1)
    pl.semaphore_wait(barrier, 30)
    c0 = exchange(0, "gx", s1, e.at[0])

    for copy in loads[2:]:
        copy.wait()
    zeros = jnp.zeros((16, WP - W), F32)

    @pl.loop(0, W)
    def _(w):
        for s in range(2):
            pieces = []
            for jt in range(4):
                pieces += [wv[jt, s, w], zeros]
            wt[s, w] = jnp.concatenate(pieces, axis=1)

    square[...] = jnp.zeros((128, 128), F32)
    square[0:W, 0:W] = pwv[...].astype(F32)
    square[WP : WP + 1, 0:W] = bv[...].reshape(1, W)
    turned = square[...].T
    pw_back = square[0:WP, 0:WP].astype(BF16)
    pw_forward = turned[0:WP, 0:WP].astype(BF16)
    bias_column = turned[0:W, WP : WP + 1]
    for xy in range(8):
        rows = slice(xy * WP, xy * WP + WP)
        local[xy] = jnp.dot(pw_forward, u[rows], preferred_element_type=F32)[0:W] + bias_column
    to_cells(cin, ccells)

    arrive(c0)
    x_forward(e.at[0].reshape(256, 128), s2.reshape(128, 128))
    c1 = exchange(1, "gy", s2, d.at[0])
    arrive(c1)
    spec[...] = matmul(ty, d[0].reshape(128, 128))

    acc_r = acc_i = jnp.zeros((16, 128), F32)
    for w in range(W):
        sr, si = spread(spec[0:16], w), spread(spec[16:32], w)
        wr, wi = wt[0, w], wt[1, w]
        acc_r = acc_r + (wr * sr - wi * si)
        acc_i = acc_i + (wi * sr + wr * si)
    mixed = jnp.concatenate([acc_r * kappa, acc_i * kappa], axis=0)

    s3[...] = matmul(tyi, mixed).reshape(16, 8, 128)
    c2 = exchange(2, "gy", s3, z.at[0])
    arrive(c2)
    x_inverse(z.at[0].reshape(128, 128), s4.reshape(256, 128))
    c3 = exchange(3, "gx", s4, v.at[0])
    drain(c0)
    arrive(c3)

    root = math.sqrt(2.0 / math.pi)
    cubic = 0.044715
    for half in range(2):
        spatial = jnp.dot(unpack_modes(v.at[0], half), zt[...], preferred_element_type=F32)
        for sub in range(4):
            xy = half * 4 + sub
            p = local[xy] + spatial[sub * WP : sub * WP + W]
            pre[xy] = p
            p2 = p * p
            t = jnp.tanh(p * (root * cubic * p2 + root))
            b = p * (1.5 * root * cubic * p2 + 0.5 * root)
            slope = t * (0.5 - b * t) + (b + 0.5)
            signal = ccells[:, xy, :] * slope
            sig[xy * WP : xy * WP + WP] = jnp.concatenate([signal, pad], axis=0).astype(BF16)

    pack_modes(sig, s1)
    c4 = exchange(4, "gx", s1, e.at[1])

    for xy in range(8):
        p = pre[xy]
        t = jnp.tanh(p * (root * cubic * (p * p) + root))
        cells[:, xy, :] = 0.5 * p * (1.0 + t)
        rows = slice(xy * WP, xy * WP + WP)
        local[xy] = jnp.dot(pw_back, sig[rows], preferred_element_type=F32)[0:W]
    from_cells(cells, outv)
    drain(c1)
    drain(c2)
    drain(c3)
    arrive(c4)
    x_forward(e.at[1].reshape(256, 128), s2.reshape(128, 128))
    c5 = exchange(5, "gy", s2, d.at[1])
    arrive(c5)
    back = matmul(ty, d[1].reshape(128, 128))
    br, bi = back[0:16] * kappa, back[16:32] * kappa

    lane = lax.broadcasted_iota(jnp.int32, (32, 128), 1)

    def combine(a, b, h):
        bit = (lane & h) != 0
        flip = lane ^ h
        if b is None:
            return jnp.where(bit, 0.0, a + jnp.take_along_axis(a, flip, axis=1))
        return jnp.where(bit, b, a) + jnp.take_along_axis(jnp.where(bit, a, b), flip, axis=1)

    def product(w):
        wr, wi = wt[0, w], wt[1, w]
        return jnp.concatenate([wr * br + wi * bi, wr * bi - wi * br], axis=0)

    def reduce_tree(w, h):
        if h == WP:
            return product(w) if w < W else None
        a, b = reduce_tree(w, h * 2), reduce_tree(w + h, h * 2)
        return combine(a, b, h) if a is not None else None

    s3[...] = matmul(tyi, reduce_tree(0, 1)).reshape(16, 8, 128)
    c6 = exchange(6, "gy", s3, z.at[1])

    @pl.loop(0, W)
    def _(w):
        sr, si = spread(spec[0:16], w), spread(spec[16:32], w)
        parts = (sr * br + si * bi, sr * bi - si * br)
        for s in range(2):
            for jt in range(4):
                gs[jt, s, w] = parts[s][:, jt * WP : jt * WP + W]

    arrive(c6)
    x_inverse(z.at[1].reshape(128, 128), s4.reshape(256, 128))
    c7 = exchange(7, "gx", s4, v.at[1])
    drain(c4)
    drain(c5)
    drain(c6)
    arrive(c7)
    for half in range(2):
        spatial = jnp.dot(unpack_modes(v.at[1], half), zt[...], preferred_element_type=F32)
        for sub in range(4):
            xy = half * 4 + sub
            cells[:, xy, :] = local[xy] + spatial[sub * WP : sub * WP + W]
    from_cells(cells, gout)
    drain(c7)


def store_kernel(a, b, c, a_out, b_out, c_out, sems):
    copies = [
        pltpu.make_async_copy(src, dst, sems.at[i])
        for i, (src, dst) in enumerate(((a, a_out), (b, b_out), (c, c_out)))
    ]
    for copy in copies:
        copy.start()
    for copy in copies:
        copy.wait()


def on_device(field, cotangent, spectral_weight, pointwise_weight, channel_bias):
    constants = tables()
    weight = jnp.transpose(spectral_weight, (0, 1, 2, 4, 5, 3)).reshape(4, 2, W, 16, W)
    hbm = pl.BlockSpec(memory_space=pltpu.MemorySpace.HBM)
    vmem = pl.BlockSpec(memory_space=pltpu.MemorySpace.VMEM)
    shapes = (((W, 2, 4, Q), BF16), ((W, 2, 4, Q), BF16), ((4, 2, W, 16, W), F32))
    results = pl.pallas_call(
        kernel,
        out_shape=tuple(pltpu.VMEM(shape, dtype) for shape, dtype in shapes),
        in_specs=[hbm] * 10,
        out_specs=(vmem,) * 3,
        scratch_shapes=[
            pltpu.VMEM((W, 2, 4, Q), BF16),
            pltpu.VMEM((W, 2, 4, Q), BF16),
            pltpu.VMEM((4, 2, W, 16, W), F32),
            pltpu.VMEM((W, W), BF16),
            pltpu.VMEM((W,), F32),
            pltpu.VMEM((128, Q), BF16),
            pltpu.VMEM((32, 192), BF16),
            pltpu.VMEM((32, 384), BF16),
            pltpu.VMEM((128, 96), BF16),
            pltpu.VMEM((64, 96), BF16),
            pltpu.VMEM((256, Q), BF16),
            pltpu.VMEM((W, 8, Q), F32),
            pltpu.VMEM((W, 8, Q), F32),
            pltpu.VMEM((128, 128), F32),
            pltpu.VMEM((2, W, 16, 128), F32),
            pltpu.VMEM((8, W, Q), F32),
            pltpu.VMEM((8, W, Q), F32),
            pltpu.VMEM((256, Q), BF16),
            pltpu.VMEM((32, 128), F32),
            pltpu.VMEM((16, 16, 128), F32),
            pltpu.VMEM((16, 8, 128), F32),
            pltpu.VMEM((16, 8, 128), F32),
            pltpu.VMEM((16, 16, 128), F32),
            pltpu.VMEM((2, 16, 16, 128), F32),
            pltpu.VMEM((2, 16, 8, 128), F32),
            pltpu.VMEM((2, 16, 8, 128), F32),
            pltpu.VMEM((2, 16, 16, 128), F32),
            pltpu.SemaphoreType.DMA((10,)),
            pltpu.SemaphoreType.DMA((8, 16)),
            pltpu.SemaphoreType.DMA((8, 16)),
        ],
        compiler_params=pltpu.CompilerParams(
            collective_id=0, has_side_effects=True, vmem_limit_bytes=VMEM - RESULTS
        ),
    )(field, cotangent, weight, pointwise_weight, channel_bias, *constants)
    out, gfield, gspec = pl.pallas_call(
        store_kernel,
        out_shape=tuple(jax.ShapeDtypeStruct(shape, dtype) for shape, dtype in shapes),
        in_specs=[pl.BlockSpec(memory_space=pl.ANY)] * 3,
        out_specs=(hbm,) * 3,
        scratch_shapes=[pltpu.SemaphoreType.DMA((3,))],
        compiler_params=pltpu.CompilerParams(vmem_limit_bytes=1 << 20),
    )(*results)
    grad = jnp.transpose(gspec.reshape(4, 2, W, 1, 16, W), (0, 1, 2, 5, 3, 4))
    return out, gfield, grad


def solution(mesh):
    return jax.shard_map(
        on_device,
        mesh=mesh,
        in_specs=(
            P(None, "gx", "gy", None),
            P(None, "gx", "gy", None),
            P("gx", None, None, None, "gy", None),
            P(),
            P(),
        ),
        out_specs=(
            P(None, "gx", "gy", None),
            P(None, "gx", "gy", None),
            P("gx", None, None, None, "gy", None),
        ),
        check_vma=False,
    )
```

```python
import math

import jax
import jax.numpy as jnp
import numpy as np
from jax import lax
from jax.experimental import pallas as pl
from jax.experimental.pallas import tpu as pltpu
from jax.sharding import PartitionSpec as P

W = 20
WP = 32
GX = 16
GY = 16
Q = 512
F32 = jnp.float32
BF16 = jnp.bfloat16
VMEM = 67043328
RESULTS = 2 * 20 * 8 * 512 * 2 + 160 * 16 * 128 * 4


def frequencies():
    j = np.arange(16)
    return np.where(j < 8, j, j - 16)


def rotation_blocks(length, sign):
    phase = np.mod(frequencies()[:, None] * np.arange(length)[None, :], length)
    angle = sign * 2.0 * np.pi * phase / length
    c, s = np.cos(angle) / np.sqrt(length), np.sin(angle) / np.sqrt(length)
    return np.stack([np.stack([c, -s]), np.stack([s, c])])


def split(a):
    a = a.astype(np.float32)
    hi = a.astype(BF16)
    lo = (a - hi.astype(np.float32)).astype(BF16)
    return np.concatenate([hi, lo, hi], axis=1)


def tables():
    fx = rotation_blocks(32, -1.0).reshape(2, 2, 16, 16, 2)
    tx = np.einsum("rskcx->krcsx", fx).reshape(32, 64)
    fy = rotation_blocks(64, -1.0).reshape(2, 2, 16, 16, 4)
    ty = np.einsum("rskpy->rkpsy", fy).reshape(32, 128)
    iy = rotation_blocks(64, 1.0).reshape(2, 2, 16, 16, 4)
    tyi = np.einsum("rskpy->prysk", iy).reshape(128, 32)
    ix = rotation_blocks(32, 1.0).reshape(2, 2, 16, 16, 2)
    txi = np.einsum("rskcx->crxks", ix).reshape(64, 32)
    z, t = np.arange(32), np.arange(16)
    f = frequencies()
    phase = (
        f[None, :, None, None] * z[None, None, :, None] * 16
        + np.arange(4)[:, None, None, None] * t[None, None, None, :] * 32
    )
    angle = np.mod(phase, 512).reshape(4, 16, 512) * (2.0 * np.pi / 512)
    zt = np.stack([np.cos(angle), -np.sin(angle)], axis=1).reshape(128, 512) / np.sqrt(512)
    return [zt.astype(np.float32).astype(BF16)] + [split(a) for a in (tx, ty, tyi, txi)]


def lane_blocks(rows):
    return lax.broadcasted_iota(jnp.int32, (rows, 128), 1) // WP


def block_transpose(parts):
    which = lane_blocks(parts[0].shape[0])
    out = []
    for b in range(4):
        acc = None
        for a in range(4):
            shift = ((a - b) * WP) % 128
            piece = parts[a] if shift == 0 else pltpu.roll(parts[a], shift, 1)
            acc = piece if acc is None else jnp.where(which == a, piece, acc)
        out.append(acc)
    return out


def kernel(
    field, cot, weight, pw, bias, zt_h, tx_h, ty_h, tyi_h, txi_h,
    outv, gout, gs,
    fin, cin, wv, pwv, bv, zt, tx, ty, tyi, txi,
    u, cells, ccells, square, wt, local, pre, sig, spec,
    s1, s2, s3, s4, e, d, z, v,
    load_sem, send_sem, recv_sem,
):
    cx = lax.axis_index("gx")
    cy = lax.axis_index("gy")

    turn_x = [lax.rem(cx // 4 + i, 4) * 4 for i in range(4)]
    low = cy // 8
    turn_z = [lax.rem(lax.rem(cx, 4) + i + low * (4 - 2 * i), 4) for i in range(4)]
    turn_l = [lax.rem(low + i, 2) * 8 for i in range(2)]
    turn_y = [lax.rem(cy // 2 + i, 4) * 2 for i in range(4)]
    turn_c = [lax.rem(cy + i, 2) for i in range(2)]
    peer_x = [turn_x[o // 4] + turn_z[o % 4] for o in range(16)]
    peer_y = [turn_l[o // 8] + turn_y[(o % 8) // 2] + turn_c[o % 2] for o in range(16)]

    def ring(n):
        return min(n, 4 - n)

    order_x = sorted(range(16), key=lambda o: -(ring(o // 4) + (1, 3, 3, 1)[o % 4]))
    order_y = sorted(range(1, 16), key=lambda o: -(3 * (o // 8) + 3 * ring((o % 8) // 2) + o % 2))

    other = turn_l[1] + lax.rem(cy, 8)
    flip_y = [turn_l[1 - o // 8] + turn_y[(o % 8) // 2] + turn_c[o % 2] for o in range(16)]
    barrier = pltpu.get_barrier_semaphore()
    for off in order_x:
        pl.semaphore_signal(
            barrier, inc=1, device_id=(peer_x[off], other), device_id_type=pl.DeviceIdType.MESH
        )
    for off in order_y:
        if off == 8:
            continue
        pl.semaphore_signal(
            barrier, inc=1, device_id=(cx, peer_y[off]), device_id_type=pl.DeviceIdType.MESH
        )

    sources = (field, zt_h, tx_h, ty_h, tyi_h, txi_h, weight, pw, bias, cot)
    sinks = (fin, zt, tx, ty, tyi, txi, wv, pwv, bv, cin)
    loads = [
        pltpu.make_async_copy(a, b, load_sem.at[i]) for i, (a, b) in enumerate(zip(sources, sinks))
    ]
    for copy in loads:
        copy.start()

    def start(step, off, src, dst, device):
        copy = pltpu.make_async_remote_copy(
            src_ref=src,
            dst_ref=dst,
            send_sem=send_sem.at[step, off],
            recv_sem=recv_sem.at[step, off],
            device_id=device,
            device_id_type=pl.DeviceIdType.MESH,
        )
        copy.start()
        return copy

    def exchange_x(step, src, dst):
        return [
            start(step, o, src.at[peer_x[o]], dst.at[cx], (peer_x[o], other)) for o in order_x
        ]

    def exchange_y(step, src, dst, inverse):
        copies = [
            start(
                step,
                o,
                src.at[flip_y[o] if inverse else peer_y[o]],
                dst.at[cy if inverse else other],
                (cx, peer_y[o]),
            )
            for o in order_y
        ]
        if inverse:
            dst[cy] = src[other]
        else:
            dst[other] = src[cy]
        return copies

    def arrive(copies):
        for copy in copies:
            copy.wait_recv()

    def drain(copies):
        for copy in copies:
            copy.wait_send()

    def pack_modes(values, send, half):
        spectra = lax.dot_general(
            zt[...],
            values[half * 128 : half * 128 + 128],
            (((1,), (1,)), ((), ())),
            preferred_element_type=F32,
        )
        parts = [spectra[jt * 32 : jt * 32 + 32] for jt in range(4)]
        for sub, block in enumerate(block_transpose(parts)):
            for s in range(2):
                send[:, s * 8 + half * 4 + sub, :] = block[s * 16 : s * 16 + 16]

    def unpack_modes(recv, half):
        parts = [
            jnp.concatenate([recv[:, s * 8 + half * 4 + sub, :] for s in range(2)], axis=0)
            for sub in range(4)
        ]
        stacked = jnp.concatenate(block_transpose(parts), axis=0)
        return stacked.T.astype(BF16)

    def matmul(table, b):
        hi = b.astype(BF16)
        lo = (b - hi.astype(F32)).astype(BF16)
        return jnp.dot(
            table[...], jnp.concatenate([hi, hi, lo], axis=0), preferred_element_type=F32
        )

    def y_to_lanes(recv, n):
        return jnp.concatenate([recv[pl.ds(y, n, stride=4), :] for y in range(4)], axis=1)

    def x_forward(recv, send):
        out = matmul(tx, y_to_lanes(recv, 64))
        for y in range(4):
            send[pl.ds(y, 32, stride=4), :] = out[:, y * 128 : y * 128 + 128]

    def x_inverse(recv, send):
        out = matmul(txi, y_to_lanes(recv, 32))
        for y in range(4):
            send[pl.ds(y, 64, stride=4), :] = out[:, y * 128 : y * 128 + 128]

    def to_cells(source, target):
        for x in range(2):
            target[:, 4 * x : 4 * x + 4, :] = source[:, x].astype(F32)

    def from_cells(source, target):
        for x in range(2):
            target[:, x] = source[:, 4 * x : 4 * x + 4, :].astype(BF16)

    kappa = jnp.where(lax.broadcasted_iota(jnp.int32, (16, 128), 1) < WP, 1.0, 2.0).astype(F32)
    gather_base = lane_blocks(16) * WP

    def spread(value, w):
        return jnp.take_along_axis(value, gather_base + w, axis=1)

    loads[0].wait()
    to_cells(fin, cells)
    pad = jnp.zeros((WP - W, Q), F32)
    for xy in range(8):
        u[xy * WP : xy * WP + WP] = jnp.concatenate([cells[:, xy, :], pad], axis=0).astype(BF16)
    loads[1].wait()
    for half in range(2):
        pack_modes(u, s1, half)
    pl.semaphore_wait(barrier, 30)
    c0 = exchange_x(0, s1, e.at[0])

    for copy in loads[2:]:
        copy.wait()
    zeros = jnp.zeros((16, WP - W), F32)

    @pl.loop(0, W)
    def _(w):
        for s in range(2):
            pieces = []
            for jt in range(4):
                pieces += [wv[jt, s, w], zeros]
            wt[s, w] = jnp.concatenate(pieces, axis=1)

    square[...] = jnp.zeros((128, 128), F32)
    square[0:W, 0:W] = pwv[...].astype(F32)
    square[WP : WP + 1, 0:W] = bv[...].reshape(1, W)
    turned = square[...].T
    pw_back = square[0:WP, 0:WP].astype(BF16)
    pw_forward = turned[0:WP, 0:WP].astype(BF16)
    bias_column = turned[0:W, WP : WP + 1]
    for xy in range(8):
        rows = slice(xy * WP, xy * WP + WP)
        local[xy] = jnp.dot(pw_forward, u[rows], preferred_element_type=F32)[0:W] + bias_column
    to_cells(cin, ccells)

    arrive(c0)
    x_forward(e.at[0].reshape(256, 128), s2.reshape(128, 128))
    c1 = exchange_y(1, s2, d.at[0], False)
    arrive(c1)
    spec[...] = matmul(ty, d[0].reshape(128, 128))

    acc_r = acc_i = jnp.zeros((16, 128), F32)
    for w in range(W):
        sr, si = spread(spec[0:16], w), spread(spec[16:32], w)
        wr, wi = wt[0, w], wt[1, w]
        acc_r = acc_r + (wr * sr - wi * si)
        acc_i = acc_i + (wi * sr + wr * si)
    mixed = jnp.concatenate([acc_r * kappa, acc_i * kappa], axis=0)

    s3[...] = matmul(tyi, mixed).reshape(16, 8, 128)
    c2 = exchange_y(2, s3, z.at[0], True)
    arrive(c2)
    x_inverse(z.at[0].reshape(128, 128), s4.reshape(256, 128))
    c3 = exchange_x(3, s4, v.at[0])
    drain(c0)
    arrive(c3)

    root = math.sqrt(2.0 / math.pi)
    cubic = 0.044715
    for half in range(2):
        spatial = jnp.dot(unpack_modes(v.at[0], half), zt[...], preferred_element_type=F32)
        for sub in range(4):
            xy = half * 4 + sub
            p = local[xy] + spatial[sub * WP : sub * WP + W]
            pre[xy] = p
            p2 = p * p
            t = jnp.tanh(p * (root * cubic * p2 + root))
            b = p * (1.5 * root * cubic * p2 + 0.5 * root)
            slope = t * (0.5 - b * t) + (b + 0.5)
            signal = ccells[:, xy, :] * slope
            sig[xy * WP : xy * WP + WP] = jnp.concatenate([signal, pad], axis=0).astype(BF16)
        pack_modes(sig, s1, half)

    c4 = exchange_x(4, s1, e.at[1])

    for xy in range(8):
        p = pre[xy]
        t = jnp.tanh(p * (root * cubic * (p * p) + root))
        cells[:, xy, :] = 0.5 * p * (1.0 + t)
        rows = slice(xy * WP, xy * WP + WP)
        local[xy] = jnp.dot(pw_back, sig[rows], preferred_element_type=F32)[0:W]
    from_cells(cells, outv)
    drain(c1)
    drain(c2)
    drain(c3)
    arrive(c4)
    x_forward(e.at[1].reshape(256, 128), s2.reshape(128, 128))
    c5 = exchange_y(5, s2, d.at[1], False)
    arrive(c5)
    back = matmul(ty, d[1].reshape(128, 128))
    br, bi = back[0:16] * kappa, back[16:32] * kappa

    lane = lax.broadcasted_iota(jnp.int32, (32, 128), 1)

    def combine(a, b, h):
        bit = (lane & h) != 0
        flip = lane ^ h
        if b is None:
            return jnp.where(bit, 0.0, a + jnp.take_along_axis(a, flip, axis=1))
        return jnp.where(bit, b, a) + jnp.take_along_axis(jnp.where(bit, a, b), flip, axis=1)

    def product(w):
        wr, wi = wt[0, w], wt[1, w]
        return jnp.concatenate([wr * br + wi * bi, wr * bi - wi * br], axis=0)

    def reduce_tree(w, h):
        if h == WP:
            return product(w) if w < W else None
        a, b = reduce_tree(w, h * 2), reduce_tree(w + h, h * 2)
        return combine(a, b, h) if a is not None else None

    s3[...] = matmul(tyi, reduce_tree(0, 1)).reshape(16, 8, 128)
    c6 = exchange_y(6, s3, z.at[1], True)

    @pl.loop(0, W)
    def _(w):
        sr, si = spread(spec[0:16], w), spread(spec[16:32], w)
        parts = (sr * br + si * bi, sr * bi - si * br)
        for s in range(2):
            for jt in range(4):
                gs[jt, s, w] = parts[s][:, jt * WP : jt * WP + W]

    arrive(c6)
    x_inverse(z.at[1].reshape(128, 128), s4.reshape(256, 128))
    c7 = exchange_x(7, s4, v.at[1])
    drain(c4)
    drain(c5)
    drain(c6)
    arrive(c7)
    for half in range(2):
        spatial = jnp.dot(unpack_modes(v.at[1], half), zt[...], preferred_element_type=F32)
        for sub in range(4):
            xy = half * 4 + sub
            cells[:, xy, :] = local[xy] + spatial[sub * WP : sub * WP + W]
    from_cells(cells, gout)
    drain(c7)


def store_kernel(a, b, c, a_out, b_out, c_out, sems):
    copies = [
        pltpu.make_async_copy(src, dst, sems.at[i])
        for i, (src, dst) in enumerate(((a, a_out), (b, b_out), (c, c_out)))
    ]
    for copy in copies:
        copy.start()
    for copy in copies:
        copy.wait()


def on_device(field, cotangent, spectral_weight, pointwise_weight, channel_bias):
    constants = tables()
    weight = jnp.transpose(spectral_weight, (0, 1, 2, 4, 5, 3)).reshape(4, 2, W, 16, W)
    hbm = pl.BlockSpec(memory_space=pltpu.MemorySpace.HBM)
    vmem = pl.BlockSpec(memory_space=pltpu.MemorySpace.VMEM)
    shapes = (((W, 2, 4, Q), BF16), ((W, 2, 4, Q), BF16), ((4, 2, W, 16, W), F32))
    results = pl.pallas_call(
        kernel,
        out_shape=tuple(pltpu.VMEM(shape, dtype) for shape, dtype in shapes),
        in_specs=[hbm] * 10,
        out_specs=(vmem,) * 3,
        scratch_shapes=[
            pltpu.VMEM((W, 2, 4, Q), BF16),
            pltpu.VMEM((W, 2, 4, Q), BF16),
            pltpu.VMEM((4, 2, W, 16, W), F32),
            pltpu.VMEM((W, W), BF16),
            pltpu.VMEM((W,), F32),
            pltpu.VMEM((128, Q), BF16),
            pltpu.VMEM((32, 192), BF16),
            pltpu.VMEM((32, 384), BF16),
            pltpu.VMEM((128, 96), BF16),
            pltpu.VMEM((64, 96), BF16),
            pltpu.VMEM((256, Q), BF16),
            pltpu.VMEM((W, 8, Q), F32),
            pltpu.VMEM((W, 8, Q), F32),
            pltpu.VMEM((128, 128), F32),
            pltpu.VMEM((2, W, 16, 128), F32),
            pltpu.VMEM((8, W, Q), F32),
            pltpu.VMEM((8, W, Q), F32),
            pltpu.VMEM((256, Q), BF16),
            pltpu.VMEM((32, 128), F32),
            pltpu.VMEM((16, 16, 128), F32),
            pltpu.VMEM((16, 8, 128), F32),
            pltpu.VMEM((16, 8, 128), F32),
            pltpu.VMEM((16, 16, 128), F32),
            pltpu.VMEM((2, 16, 16, 128), F32),
            pltpu.VMEM((2, 16, 8, 128), F32),
            pltpu.VMEM((2, 16, 8, 128), F32),
            pltpu.VMEM((2, 16, 16, 128), F32),
            pltpu.SemaphoreType.DMA((10,)),
            pltpu.SemaphoreType.DMA((8, 16)),
            pltpu.SemaphoreType.DMA((8, 16)),
        ],
        compiler_params=pltpu.CompilerParams(
            collective_id=0, has_side_effects=True, vmem_limit_bytes=VMEM - RESULTS
        ),
    )(field, cotangent, weight, pointwise_weight, channel_bias, *constants)
    out, gfield, gspec = pl.pallas_call(
        store_kernel,
        out_shape=tuple(jax.ShapeDtypeStruct(shape, dtype) for shape, dtype in shapes),
        in_specs=[pl.BlockSpec(memory_space=pl.ANY)] * 3,
        out_specs=(hbm,) * 3,
        scratch_shapes=[pltpu.SemaphoreType.DMA((3,))],
        compiler_params=pltpu.CompilerParams(vmem_limit_bytes=1 << 20),
    )(*results)
    grad = jnp.transpose(gspec.reshape(4, 2, W, 1, 16, W), (0, 1, 2, 5, 3, 4))
    return out, gfield, grad


def solution(mesh):
    return jax.shard_map(
        on_device,
        mesh=mesh,
        in_specs=(
            P(None, "gx", "gy", None),
            P(None, "gx", "gy", None),
            P("gx", None, None, None, "gy", None),
            P(),
            P(),
        ),
        out_specs=(
            P(None, "gx", "gy", None),
            P(None, "gx", "gy", None),
            P("gx", None, None, None, "gy", None),
        ),
        check_vma=False,
    )
```

```python
import math

import jax
import jax.numpy as jnp
import numpy as np
from jax import lax
from jax.experimental import pallas as pl
from jax.experimental.pallas import tpu as pltpu
from jax.sharding import PartitionSpec as P

W = 20
WP = 32
GX = 16
GY = 16
Q = 512
F32 = jnp.float32
BF16 = jnp.bfloat16
VMEM = 67043328
RESULTS = 2 * 20 * 8 * 512 * 2 + 160 * 16 * 128 * 4


def frequencies():
    j = np.arange(16)
    return np.where(j < 8, j, j - 16)


def rotation_blocks(length, sign):
    phase = np.mod(frequencies()[:, None] * np.arange(length)[None, :], length)
    angle = sign * 2.0 * np.pi * phase / length
    c, s = np.cos(angle) / np.sqrt(length), np.sin(angle) / np.sqrt(length)
    return np.stack([np.stack([c, -s]), np.stack([s, c])])


def split(a):
    a = a.astype(np.float32)
    hi = a.astype(BF16)
    lo = (a - hi.astype(np.float32)).astype(BF16)
    return np.concatenate([hi, lo, hi], axis=1)


def tables():
    fx = rotation_blocks(32, -1.0).reshape(2, 2, 16, 16, 2)
    tx = np.einsum("rskcx->krcsx", fx).reshape(32, 64)
    fy = rotation_blocks(64, -1.0).reshape(2, 2, 16, 16, 4)
    ty = np.einsum("rskpy->rkpsy", fy).reshape(32, 128)
    iy = rotation_blocks(64, 1.0).reshape(2, 2, 16, 16, 4)
    tyi = np.einsum("rskpy->prysk", iy).reshape(128, 32)
    ix = rotation_blocks(32, 1.0).reshape(2, 2, 16, 16, 2)
    txi = np.einsum("rskcx->crxks", ix).reshape(64, 32)
    z, t = np.arange(32), np.arange(16)
    f = frequencies()
    phase = (
        f[None, :, None, None] * z[None, None, :, None] * 16
        + np.arange(4)[:, None, None, None] * t[None, None, None, :] * 32
    )
    angle = np.mod(phase, 512).reshape(4, 16, 512) * (2.0 * np.pi / 512)
    zt = np.stack([np.cos(angle), -np.sin(angle)], axis=1).reshape(128, 512) / np.sqrt(512)
    return [zt.astype(np.float32).astype(BF16)] + [split(a) for a in (tx, ty, tyi, txi)]


def lane_blocks(rows):
    return lax.broadcasted_iota(jnp.int32, (rows, 128), 1) // WP


def block_transpose(parts):
    which = lane_blocks(parts[0].shape[0])
    out = []
    for b in range(4):
        acc = None
        for a in range(4):
            shift = ((a - b) * WP) % 128
            piece = parts[a] if shift == 0 else pltpu.roll(parts[a], shift, 1)
            acc = piece if acc is None else jnp.where(which == a, piece, acc)
        out.append(acc)
    return out


def kernel(
    field, cot, weight, pw, bias, zt_h, tx_h, ty_h, tyi_h, txi_h,
    outv, gout, gs,
    fin, cin, wv, pwv, bv, zt, tx, ty, tyi, txi,
    u, cells, ccells, square, wt, local, pre, sig, spec,
    s1, s2, s3, s4, e, d, z, v,
    load_sem, send_sem, recv_sem,
):
    cx = lax.axis_index("gx")
    cy = lax.axis_index("gy")

    turn_x = [lax.rem(cx // 4 + i, 4) * 4 for i in range(4)]
    low = cy // 8
    turn_z = [lax.rem(lax.rem(cx, 4) + i + low * (4 - 2 * i), 4) for i in range(4)]
    turn_l = [lax.rem(low + i, 2) * 8 for i in range(2)]
    turn_y = [lax.rem(cy // 2 + i, 4) * 2 for i in range(4)]
    turn_c = [lax.rem(cy + i, 2) for i in range(2)]
    peer_x = [turn_x[o // 4] + turn_z[o % 4] for o in range(16)]
    peer_y = [turn_l[o // 8] + turn_y[(o % 8) // 2] + turn_c[o % 2] for o in range(16)]

    def ring(n):
        return min(n, 4 - n)

    order_x = sorted(range(16), key=lambda o: -(ring(o // 4) + (1, 3, 3, 1)[o % 4]))
    order_y = sorted(range(1, 16), key=lambda o: -(3 * (o // 8) + 3 * ring((o % 8) // 2) + o % 2))

    other = turn_l[1] + turn_y[0] + turn_c[1]
    flip_y = [turn_l[1 - o // 8] + turn_y[(o % 8) // 2] + turn_c[1 - o % 2] for o in range(16)]
    barrier = pltpu.get_barrier_semaphore()
    for off in order_x:
        pl.semaphore_signal(
            barrier, inc=1, device_id=(peer_x[off], other), device_id_type=pl.DeviceIdType.MESH
        )
    for off in order_y:
        if off == 9:
            continue
        pl.semaphore_signal(
            barrier, inc=1, device_id=(cx, peer_y[off]), device_id_type=pl.DeviceIdType.MESH
        )

    sources = (field, zt_h, tx_h, ty_h, tyi_h, txi_h, weight, pw, bias, cot)
    sinks = (fin, zt, tx, ty, tyi, txi, wv, pwv, bv, cin)
    loads = [
        pltpu.make_async_copy(a, b, load_sem.at[i]) for i, (a, b) in enumerate(zip(sources, sinks))
    ]
    for copy in loads:
        copy.start()

    def start(step, off, src, dst, device):
        copy = pltpu.make_async_remote_copy(
            src_ref=src,
            dst_ref=dst,
            send_sem=send_sem.at[step, off],
            recv_sem=recv_sem.at[step, off],
            device_id=device,
            device_id_type=pl.DeviceIdType.MESH,
        )
        copy.start()
        return copy

    def exchange_x(step, src, dst):
        return [
            start(step, o, src.at[peer_x[o]], dst.at[cx], (peer_x[o], other)) for o in order_x
        ]

    def exchange_y(step, src, dst, inverse):
        copies = [
            start(
                step,
                o,
                src.at[flip_y[o] if inverse else peer_y[o]],
                dst.at[cy if inverse else other],
                (cx, peer_y[o]),
            )
            for o in order_y
        ]
        if inverse:
            dst[cy] = src[other]
        else:
            dst[other] = src[cy]
        return copies

    def arrive(copies):
        for copy in copies:
            copy.wait_recv()

    def drain(copies):
        for copy in copies:
            copy.wait_send()

    def pack_modes(values, send, half):
        spectra = lax.dot_general(
            zt[...],
            values[half * 128 : half * 128 + 128],
            (((1,), (1,)), ((), ())),
            preferred_element_type=F32,
        )
        parts = [spectra[jt * 32 : jt * 32 + 32] for jt in range(4)]
        for sub, block in enumerate(block_transpose(parts)):
            for s in range(2):
                send[:, s * 8 + half * 4 + sub, :] = block[s * 16 : s * 16 + 16]

    def unpack_modes(recv, half):
        parts = [
            jnp.concatenate([recv[:, s * 8 + half * 4 + sub, :] for s in range(2)], axis=0)
            for sub in range(4)
        ]
        stacked = jnp.concatenate(block_transpose(parts), axis=0)
        return stacked.T.astype(BF16)

    def matmul(table, b):
        hi = b.astype(BF16)
        lo = (b - hi.astype(F32)).astype(BF16)
        return jnp.dot(
            table[...], jnp.concatenate([hi, hi, lo], axis=0), preferred_element_type=F32
        )

    def y_to_lanes(recv, n):
        return jnp.concatenate([recv[pl.ds(y, n, stride=4), :] for y in range(4)], axis=1)

    def x_forward(recv, send):
        out = matmul(tx, y_to_lanes(recv, 64))
        for y in range(4):
            send[pl.ds(y, 32, stride=4), :] = out[:, y * 128 : y * 128 + 128]

    def x_inverse(recv, send):
        out = matmul(txi, y_to_lanes(recv, 32))
        for y in range(4):
            send[pl.ds(y, 64, stride=4), :] = out[:, y * 128 : y * 128 + 128]

    def to_cells(source, target):
        for x in range(2):
            target[:, 4 * x : 4 * x + 4, :] = source[:, x].astype(F32)

    def from_cells(source, target):
        for x in range(2):
            target[:, x] = source[:, 4 * x : 4 * x + 4, :].astype(BF16)

    kappa = jnp.where(lax.broadcasted_iota(jnp.int32, (16, 128), 1) < WP, 1.0, 2.0).astype(F32)
    gather_base = lane_blocks(16) * WP

    def spread(value, w):
        return jnp.take_along_axis(value, gather_base + w, axis=1)

    loads[0].wait()
    to_cells(fin, cells)
    pad = jnp.zeros((WP - W, Q), F32)
    for xy in range(8):
        u[xy * WP : xy * WP + WP] = jnp.concatenate([cells[:, xy, :], pad], axis=0).astype(BF16)
    loads[1].wait()
    for half in range(2):
        pack_modes(u, s1, half)
    pl.semaphore_wait(barrier, 30)
    c0 = exchange_x(0, s1, e.at[0])

    for copy in loads[2:]:
        copy.wait()
    zeros = jnp.zeros((16, WP - W), F32)

    @pl.loop(0, W)
    def _(w):
        for s in range(2):
            pieces = []
            for jt in range(4):
                pieces += [wv[jt, s, w], zeros]
            wt[s, w] = jnp.concatenate(pieces, axis=1)

    square[...] = jnp.zeros((128, 128), F32)
    square[0:W, 0:W] = pwv[...].astype(F32)
    square[WP : WP + 1, 0:W] = bv[...].reshape(1, W)
    turned = square[...].T
    pw_back = square[0:WP, 0:WP].astype(BF16)
    pw_forward = turned[0:WP, 0:WP].astype(BF16)
    bias_column = turned[0:W, WP : WP + 1]
    for xy in range(8):
        rows = slice(xy * WP, xy * WP + WP)
        local[xy] = jnp.dot(pw_forward, u[rows], preferred_element_type=F32)[0:W] + bias_column
    to_cells(cin, ccells)

    arrive(c0)
    x_forward(e.at[0].reshape(256, 128), s2.reshape(128, 128))
    c1 = exchange_y(1, s2, d.at[0], False)
    arrive(c1)
    spec[...] = matmul(ty, d[0].reshape(128, 128))

    acc_r = acc_i = jnp.zeros((16, 128), F32)
    for w in range(W):
        sr, si = spread(spec[0:16], w), spread(spec[16:32], w)
        wr, wi = wt[0, w], wt[1, w]
        acc_r = acc_r + (wr * sr - wi * si)
        acc_i = acc_i + (wi * sr + wr * si)
    mixed = jnp.concatenate([acc_r * kappa, acc_i * kappa], axis=0)

    s3[...] = matmul(tyi, mixed).reshape(16, 8, 128)
    c2 = exchange_y(2, s3, z.at[0], True)
    arrive(c2)
    x_inverse(z.at[0].reshape(128, 128), s4.reshape(256, 128))
    c3 = exchange_x(3, s4, v.at[0])
    drain(c0)
    arrive(c3)

    root = math.sqrt(2.0 / math.pi)
    cubic = 0.044715
    for half in range(2):
        spatial = jnp.dot(unpack_modes(v.at[0], half), zt[...], preferred_element_type=F32)
        for sub in range(4):
            xy = half * 4 + sub
            p = local[xy] + spatial[sub * WP : sub * WP + W]
            pre[xy] = p
            p2 = p * p
            t = jnp.tanh(p * (root * cubic * p2 + root))
            b = p * (1.5 * root * cubic * p2 + 0.5 * root)
            slope = t * (0.5 - b * t) + (b + 0.5)
            signal = ccells[:, xy, :] * slope
            sig[xy * WP : xy * WP + WP] = jnp.concatenate([signal, pad], axis=0).astype(BF16)
        pack_modes(sig, s1, half)

    c4 = exchange_x(4, s1, e.at[1])

    for xy in range(8):
        p = pre[xy]
        t = jnp.tanh(p * (root * cubic * (p * p) + root))
        cells[:, xy, :] = 0.5 * p * (1.0 + t)
        rows = slice(xy * WP, xy * WP + WP)
        local[xy] = jnp.dot(pw_back, sig[rows], preferred_element_type=F32)[0:W]
    from_cells(cells, outv)
    drain(c1)
    drain(c2)
    drain(c3)
    arrive(c4)
    x_forward(e.at[1].reshape(256, 128), s2.reshape(128, 128))
    c5 = exchange_y(5, s2, d.at[1], False)
    arrive(c5)
    back = matmul(ty, d[1].reshape(128, 128))
    br, bi = back[0:16] * kappa, back[16:32] * kappa

    lane = lax.broadcasted_iota(jnp.int32, (32, 128), 1)

    def combine(a, b, h):
        bit = (lane & h) != 0
        flip = lane ^ h
        if b is None:
            return jnp.where(bit, 0.0, a + jnp.take_along_axis(a, flip, axis=1))
        return jnp.where(bit, b, a) + jnp.take_along_axis(jnp.where(bit, a, b), flip, axis=1)

    def product(w):
        wr, wi = wt[0, w], wt[1, w]
        return jnp.concatenate([wr * br + wi * bi, wr * bi - wi * br], axis=0)

    def reduce_tree(w, h):
        if h == WP:
            return product(w) if w < W else None
        a, b = reduce_tree(w, h * 2), reduce_tree(w + h, h * 2)
        return combine(a, b, h) if a is not None else None

    s3[...] = matmul(tyi, reduce_tree(0, 1)).reshape(16, 8, 128)
    c6 = exchange_y(6, s3, z.at[1], True)

    @pl.loop(0, W)
    def _(w):
        sr, si = spread(spec[0:16], w), spread(spec[16:32], w)
        parts = (sr * br + si * bi, sr * bi - si * br)
        for s in range(2):
            for jt in range(4):
                gs[jt, s, w] = parts[s][:, jt * WP : jt * WP + W]

    arrive(c6)
    x_inverse(z.at[1].reshape(128, 128), s4.reshape(256, 128))
    c7 = exchange_x(7, s4, v.at[1])
    drain(c4)
    drain(c5)
    drain(c6)
    arrive(c7)
    for half in range(2):
        spatial = jnp.dot(unpack_modes(v.at[1], half), zt[...], preferred_element_type=F32)
        for sub in range(4):
            xy = half * 4 + sub
            cells[:, xy, :] = local[xy] + spatial[sub * WP : sub * WP + W]
    from_cells(cells, gout)
    drain(c7)


def store_kernel(a, b, c, a_out, b_out, c_out, sems):
    copies = [
        pltpu.make_async_copy(src, dst, sems.at[i])
        for i, (src, dst) in enumerate(((a, a_out), (b, b_out), (c, c_out)))
    ]
    for copy in copies:
        copy.start()
    for copy in copies:
        copy.wait()


def on_device(field, cotangent, spectral_weight, pointwise_weight, channel_bias):
    constants = tables()
    weight = jnp.transpose(spectral_weight, (0, 1, 2, 4, 5, 3)).reshape(4, 2, W, 16, W)
    hbm = pl.BlockSpec(memory_space=pltpu.MemorySpace.HBM)
    vmem = pl.BlockSpec(memory_space=pltpu.MemorySpace.VMEM)
    shapes = (((W, 2, 4, Q), BF16), ((W, 2, 4, Q), BF16), ((4, 2, W, 16, W), F32))
    results = pl.pallas_call(
        kernel,
        out_shape=tuple(pltpu.VMEM(shape, dtype) for shape, dtype in shapes),
        in_specs=[hbm] * 10,
        out_specs=(vmem,) * 3,
        scratch_shapes=[
            pltpu.VMEM((W, 2, 4, Q), BF16),
            pltpu.VMEM((W, 2, 4, Q), BF16),
            pltpu.VMEM((4, 2, W, 16, W), F32),
            pltpu.VMEM((W, W), BF16),
            pltpu.VMEM((W,), F32),
            pltpu.VMEM((128, Q), BF16),
            pltpu.VMEM((32, 192), BF16),
            pltpu.VMEM((32, 384), BF16),
            pltpu.VMEM((128, 96), BF16),
            pltpu.VMEM((64, 96), BF16),
            pltpu.VMEM((256, Q), BF16),
            pltpu.VMEM((W, 8, Q), F32),
            pltpu.VMEM((W, 8, Q), F32),
            pltpu.VMEM((128, 128), F32),
            pltpu.VMEM((2, W, 16, 128), F32),
            pltpu.VMEM((8, W, Q), F32),
            pltpu.VMEM((8, W, Q), F32),
            pltpu.VMEM((256, Q), BF16),
            pltpu.VMEM((32, 128), F32),
            pltpu.VMEM((16, 16, 128), F32),
            pltpu.VMEM((16, 8, 128), F32),
            pltpu.VMEM((16, 8, 128), F32),
            pltpu.VMEM((16, 16, 128), F32),
            pltpu.VMEM((2, 16, 16, 128), F32),
            pltpu.VMEM((2, 16, 8, 128), F32),
            pltpu.VMEM((2, 16, 8, 128), F32),
            pltpu.VMEM((2, 16, 16, 128), F32),
            pltpu.SemaphoreType.DMA((10,)),
            pltpu.SemaphoreType.DMA((8, 16)),
            pltpu.SemaphoreType.DMA((8, 16)),
        ],
        compiler_params=pltpu.CompilerParams(
            collective_id=0, has_side_effects=True, vmem_limit_bytes=VMEM - RESULTS
        ),
    )(field, cotangent, weight, pointwise_weight, channel_bias, *constants)
    out, gfield, gspec = pl.pallas_call(
        store_kernel,
        out_shape=tuple(jax.ShapeDtypeStruct(shape, dtype) for shape, dtype in shapes),
        in_specs=[pl.BlockSpec(memory_space=pl.ANY)] * 3,
        out_specs=(hbm,) * 3,
        scratch_shapes=[pltpu.SemaphoreType.DMA((3,))],
        compiler_params=pltpu.CompilerParams(vmem_limit_bytes=1 << 20),
    )(*results)
    grad = jnp.transpose(gspec.reshape(4, 2, W, 1, 16, W), (0, 1, 2, 5, 3, 4))
    return out, gfield, grad


def solution(mesh):
    return jax.shard_map(
        on_device,
        mesh=mesh,
        in_specs=(
            P(None, "gx", "gy", None),
            P(None, "gx", "gy", None),
            P("gx", None, None, None, "gy", None),
            P(),
            P(),
        ),
        out_specs=(
            P(None, "gx", "gy", None),
            P(None, "gx", "gy", None),
            P("gx", None, None, None, "gy", None),
        ),
        check_vma=False,
    )
```

```python
import math

import jax
import jax.numpy as jnp
import numpy as np
from jax import lax
from jax.experimental import pallas as pl
from jax.experimental.pallas import tpu as pltpu
from jax.sharding import PartitionSpec as P

W = 20
WP = 32
GX = 16
GY = 16
Q = 512
F32 = jnp.float32
BF16 = jnp.bfloat16
VMEM = 67043328
RESULTS = 2 * 20 * 8 * 512 * 2 + 160 * 16 * 128 * 4


def frequencies():
    j = np.arange(16)
    return np.where(j < 8, j, j - 16)


def rotation_blocks(length, sign):
    phase = np.mod(frequencies()[:, None] * np.arange(length)[None, :], length)
    angle = sign * 2.0 * np.pi * phase / length
    c, s = np.cos(angle) / np.sqrt(length), np.sin(angle) / np.sqrt(length)
    return np.stack([np.stack([c, -s]), np.stack([s, c])])


def split(a):
    a = a.astype(np.float32)
    hi = a.astype(BF16)
    lo = (a - hi.astype(np.float32)).astype(BF16)
    return np.concatenate([hi, lo, hi], axis=1)


def tables():
    fx = rotation_blocks(32, -1.0).reshape(2, 2, 16, 16, 2)
    tx = np.einsum("rskcx->krsxc", fx).reshape(32, 64)
    fy = rotation_blocks(64, -1.0).reshape(2, 2, 16, 16, 4)
    ty = np.einsum("rskpy->rkpsy", fy).reshape(32, 128)
    iy = rotation_blocks(64, 1.0).reshape(2, 2, 16, 16, 4)
    tyi = np.einsum("rskpy->prysk", iy).reshape(128, 32)
    ix = rotation_blocks(32, 1.0).reshape(2, 2, 16, 16, 2)
    txi = np.einsum("rskcx->rxcks", ix).reshape(64, 32)
    z, t = np.arange(32), np.arange(16)
    f = frequencies()
    phase = (
        f[None, :, None, None] * z[None, None, :, None] * 16
        + np.arange(4)[:, None, None, None] * t[None, None, None, :] * 32
    )
    angle = np.mod(phase, 512).reshape(4, 16, 512) * (2.0 * np.pi / 512)
    zt = np.stack([np.cos(angle), -np.sin(angle)], axis=1).reshape(128, 512) / np.sqrt(512)
    return [zt.astype(np.float32).astype(BF16)] + [split(a) for a in (tx, ty, tyi, txi)]


def lane_blocks(rows):
    return lax.broadcasted_iota(jnp.int32, (rows, 128), 1) // WP


def block_transpose(parts):
    which = lane_blocks(parts[0].shape[0])
    out = []
    for b in range(4):
        acc = None
        for a in range(4):
            shift = ((a - b) * WP) % 128
            piece = parts[a] if shift == 0 else pltpu.roll(parts[a], shift, 1)
            acc = piece if acc is None else jnp.where(which == a, piece, acc)
        out.append(acc)
    return out


def kernel(
    field, cot, weight, pw, bias, zt_h, tx_h, ty_h, tyi_h, txi_h,
    outv, gout, gs,
    fin, cin, wv, pwv, bv, zt, tx, ty, tyi, txi,
    u, cells, ccells, square, wt, local, pre, sig, spec,
    s1, s2, s3, s4, e, d, z, v,
    load_sem, send_sem, recv_sem,
):
    cx = lax.axis_index("gx")
    cy = lax.axis_index("gy")

    turn_x = [lax.rem(cx // 4 + i, 4) * 4 for i in range(4)]
    low = cy // 8
    turn_z = [lax.rem(lax.rem(cx, 4) + i + low * (4 - 2 * i), 4) for i in range(4)]
    turn_l = [lax.rem(low + i, 2) * 8 for i in range(2)]
    turn_y = [lax.rem(cy // 2 + i, 4) * 2 for i in range(4)]
    turn_c = [lax.rem(cy + i, 2) for i in range(2)]
    peer_x = [turn_x[o // 4] + turn_z[o % 4] for o in range(16)]
    peer_y = [turn_l[o // 8] + turn_y[(o % 8) // 2] + turn_c[o % 2] for o in range(16)]

    def ring(n):
        return min(n, 4 - n)

    order_x = sorted(range(16), key=lambda o: -(ring(o // 4) + (1, 3, 3, 1)[o % 4]))
    order_y = sorted(range(1, 16), key=lambda o: -(3 * (o // 8) + 3 * ring((o % 8) // 2) + o % 2))

    other = turn_l[1] + lax.rem(cy, 8)
    flip_y = [turn_l[1 - o // 8] + turn_y[(o % 8) // 2] + turn_c[o % 2] for o in range(16)]
    barrier = pltpu.get_barrier_semaphore()
    for off in order_x:
        pl.semaphore_signal(
            barrier, inc=1, device_id=(peer_x[off], other), device_id_type=pl.DeviceIdType.MESH
        )
    for off in order_y:
        if off == 8:
            continue
        pl.semaphore_signal(
            barrier, inc=1, device_id=(cx, peer_y[off]), device_id_type=pl.DeviceIdType.MESH
        )

    sources = (field, zt_h, tx_h, ty_h, tyi_h, txi_h, weight, pw, bias, cot)
    sinks = (fin, zt, tx, ty, tyi, txi, wv, pwv, bv, cin)
    loads = [
        pltpu.make_async_copy(a, b, load_sem.at[i]) for i, (a, b) in enumerate(zip(sources, sinks))
    ]
    for copy in loads:
        copy.start()

    def start(step, off, src, dst, device):
        copy = pltpu.make_async_remote_copy(
            src_ref=src,
            dst_ref=dst,
            send_sem=send_sem.at[step, off],
            recv_sem=recv_sem.at[step, off],
            device_id=device,
            device_id_type=pl.DeviceIdType.MESH,
        )
        copy.start()
        return copy

    def exchange_x(step, src, dst):
        return [
            start(step, o, src.at[peer_x[o]], dst.at[cx], (peer_x[o], other)) for o in order_x
        ]

    def exchange_y(step, src, dst, inverse):
        copies = [
            start(
                step,
                o,
                src.at[flip_y[o] if inverse else peer_y[o]],
                dst.at[cy if inverse else other],
                (cx, peer_y[o]),
            )
            for o in order_y
        ]
        if inverse:
            dst[cy] = src[other]
        else:
            dst[other] = src[cy]
        return copies

    def arrive(copies):
        for copy in copies:
            copy.wait_recv()

    def drain(copies):
        for copy in copies:
            copy.wait_send()

    in_block = lax.rem(lax.broadcasted_iota(jnp.int32, (16, 128), 1), WP)
    lane_from = {n: in_block >= n for n in (4, 8, 12, 16, 24, 28) + (W,)}

    def store_cells(blocks, send):
        for s in range(2):
            c = blocks[s]

            def moved(cell, shift):
                return pltpu.roll(c[cell], shift, 1)

            fill = (
                moved(5, 20),
                jnp.where(lane_from[28], moved(6, 28), moved(5, 8)),
                moved(6, 16),
                jnp.where(lane_from[24], moved(7, 24), moved(6, 4)),
                moved(7, 12),
            )
            for i in range(5):
                send[:, s * 5 + i, :] = jnp.where(lane_from[W], fill[i], c[i])

    def load_cells(recv):
        blocks = []
        for s in range(2):
            c = [recv[:, s * 5 + i, :] for i in range(5)]

            def moved(row, shift):
                return pltpu.roll(c[row], 128 - shift, 1)

            five = jnp.where(lane_from[12], moved(1, 8), moved(0, 20))
            six = jnp.where(lane_from[4], moved(2, 16), moved(1, 28))
            six = jnp.where(lane_from[16], moved(3, 4), six)
            seven = jnp.where(lane_from[8], moved(4, 12), moved(3, 24))
            blocks.append(c + [five, six, seven])
        return blocks

    def pack_modes(values, half):
        spectra = lax.dot_general(
            zt[...],
            values[half * 128 : half * 128 + 128],
            (((1,), (1,)), ((), ())),
            preferred_element_type=F32,
        )
        parts = [spectra[jt * 32 : jt * 32 + 32] for jt in range(4)]
        turned = block_transpose(parts)
        return [[block[s * 16 : s * 16 + 16] for block in turned] for s in range(2)]

    def unpack_modes(blocks, half):
        parts = [
            jnp.concatenate([blocks[s][half * 4 + sub] for s in range(2)], axis=0)
            for sub in range(4)
        ]
        stacked = jnp.concatenate(block_transpose(parts), axis=0)
        return stacked.T.astype(BF16)

    def matmul(table, b):
        hi = b.astype(BF16)
        lo = (b - hi.astype(F32)).astype(BF16)
        return jnp.dot(
            table[...], jnp.concatenate([hi, hi, lo], axis=0), preferred_element_type=F32
        )

    def x_forward(recv, send):
        blocks = load_cells(recv)
        columns = [
            jnp.concatenate([blocks[s][x * 4 + y] for s in range(2) for x in range(2)], axis=0)
            for y in range(4)
        ]
        out = matmul(tx, jnp.concatenate(columns, axis=1))
        for y in range(4):
            send[pl.ds(y, 32, stride=4), :] = out[:, y * 128 : y * 128 + 128]

    def x_inverse(recv, send):
        columns = [recv[pl.ds(y, 32, stride=4), :] for y in range(4)]
        out = matmul(txi, jnp.concatenate(columns, axis=1))
        store_cells(
            [
                [
                    out[(r * 2 + x) * 16 : (r * 2 + x) * 16 + 16, y * 128 : y * 128 + 128]
                    for x in range(2)
                    for y in range(4)
                ]
                for r in range(2)
            ],
            send,
        )

    def to_cells(source, target):
        for x in range(2):
            target[:, 4 * x : 4 * x + 4, :] = source[:, x].astype(F32)

    def from_cells(source, target):
        for x in range(2):
            target[:, x] = source[:, 4 * x : 4 * x + 4, :].astype(BF16)

    kappa = jnp.where(lax.broadcasted_iota(jnp.int32, (16, 128), 1) < WP, 1.0, 2.0).astype(F32)
    gather_base = lane_blocks(16) * WP

    def spread(value, w):
        return jnp.take_along_axis(value, gather_base + w, axis=1)

    loads[0].wait()
    to_cells(fin, cells)
    pad = jnp.zeros((WP - W, Q), F32)
    for xy in range(8):
        u[xy * WP : xy * WP + WP] = jnp.concatenate([cells[:, xy, :], pad], axis=0).astype(BF16)
    loads[1].wait()
    first, second = pack_modes(u, 0), pack_modes(u, 1)
    store_cells([first[s] + second[s] for s in range(2)], s1)
    pl.semaphore_wait(barrier, 30)
    c0 = exchange_x(0, s1, e.at[0])

    for copy in loads[2:]:
        copy.wait()
    zeros = jnp.zeros((16, WP - W), F32)

    @pl.loop(0, W)
    def _(w):
        for s in range(2):
            pieces = []
            for jt in range(4):
                pieces += [wv[jt, s, w], zeros]
            wt[s, w] = jnp.concatenate(pieces, axis=1)

    square[...] = jnp.zeros((128, 128), F32)
    square[0:W, 0:W] = pwv[...].astype(F32)
    square[WP : WP + 1, 0:W] = bv[...].reshape(1, W)
    turned = square[...].T
    pw_back = square[0:WP, 0:WP].astype(BF16)
    pw_forward = turned[0:WP, 0:WP].astype(BF16)
    bias_column = turned[0:W, WP : WP + 1]
    for xy in range(8):
        rows = slice(xy * WP, xy * WP + WP)
        local[xy] = jnp.dot(pw_forward, u[rows], preferred_element_type=F32)[0:W] + bias_column
    to_cells(cin, ccells)

    arrive(c0)
    x_forward(e.at[0], s2.reshape(128, 128))
    c1 = exchange_y(1, s2, d.at[0], False)
    arrive(c1)
    spec[...] = matmul(ty, d[0].reshape(128, 128))

    acc_r = acc_i = jnp.zeros((16, 128), F32)
    for w in range(W):
        sr, si = spread(spec[0:16], w), spread(spec[16:32], w)
        wr, wi = wt[0, w], wt[1, w]
        acc_r = acc_r + (wr * sr - wi * si)
        acc_i = acc_i + (wi * sr + wr * si)
    mixed = jnp.concatenate([acc_r * kappa, acc_i * kappa], axis=0)

    s3[...] = matmul(tyi, mixed).reshape(16, 8, 128)
    c2 = exchange_y(2, s3, z.at[0], True)
    arrive(c2)
    x_inverse(z.at[0].reshape(128, 128), s4)
    c3 = exchange_x(3, s4, v.at[0])
    drain(c0)
    arrive(c3)

    root = math.sqrt(2.0 / math.pi)
    cubic = 0.044715
    arrived = load_cells(v.at[0])
    packed = []
    for half in range(2):
        spatial = jnp.dot(unpack_modes(arrived, half), zt[...], preferred_element_type=F32)
        for sub in range(4):
            xy = half * 4 + sub
            p = local[xy] + spatial[sub * WP : sub * WP + W]
            pre[xy] = p
            p2 = p * p
            t = jnp.tanh(p * (root * cubic * p2 + root))
            b = p * (1.5 * root * cubic * p2 + 0.5 * root)
            slope = t * (0.5 - b * t) + (b + 0.5)
            signal = ccells[:, xy, :] * slope
            sig[xy * WP : xy * WP + WP] = jnp.concatenate([signal, pad], axis=0).astype(BF16)
        packed.append(pack_modes(sig, half))

    store_cells([packed[0][s] + packed[1][s] for s in range(2)], s1)
    c4 = exchange_x(4, s1, e.at[1])

    for xy in range(8):
        p = pre[xy]
        t = jnp.tanh(p * (root * cubic * (p * p) + root))
        cells[:, xy, :] = 0.5 * p * (1.0 + t)
        rows = slice(xy * WP, xy * WP + WP)
        local[xy] = jnp.dot(pw_back, sig[rows], preferred_element_type=F32)[0:W]
    from_cells(cells, outv)
    drain(c1)
    drain(c2)
    drain(c3)
    arrive(c4)
    x_forward(e.at[1], s2.reshape(128, 128))
    c5 = exchange_y(5, s2, d.at[1], False)
    arrive(c5)
    back = matmul(ty, d[1].reshape(128, 128))
    br, bi = back[0:16] * kappa, back[16:32] * kappa

    lane = lax.broadcasted_iota(jnp.int32, (32, 128), 1)

    def combine(a, b, h):
        bit = (lane & h) != 0
        flip = lane ^ h
        if b is None:
            return jnp.where(bit, 0.0, a + jnp.take_along_axis(a, flip, axis=1))
        return jnp.where(bit, b, a) + jnp.take_along_axis(jnp.where(bit, a, b), flip, axis=1)

    def product(w):
        wr, wi = wt[0, w], wt[1, w]
        return jnp.concatenate([wr * br + wi * bi, wr * bi - wi * br], axis=0)

    def reduce_tree(w, h):
        if h == WP:
            return product(w) if w < W else None
        a, b = reduce_tree(w, h * 2), reduce_tree(w + h, h * 2)
        return combine(a, b, h) if a is not None else None

    s3[...] = matmul(tyi, reduce_tree(0, 1)).reshape(16, 8, 128)
    c6 = exchange_y(6, s3, z.at[1], True)

    @pl.loop(0, W)
    def _(w):
        sr, si = spread(spec[0:16], w), spread(spec[16:32], w)
        parts = (sr * br + si * bi, sr * bi - si * br)
        for s in range(2):
            for jt in range(4):
                gs[jt, s, w] = parts[s][:, jt * WP : jt * WP + W]

    arrive(c6)
    x_inverse(z.at[1].reshape(128, 128), s4)
    c7 = exchange_x(7, s4, v.at[1])
    drain(c4)
    drain(c5)
    drain(c6)
    arrive(c7)
    arrived = load_cells(v.at[1])
    for half in range(2):
        spatial = jnp.dot(unpack_modes(arrived, half), zt[...], preferred_element_type=F32)
        for sub in range(4):
            xy = half * 4 + sub
            cells[:, xy, :] = local[xy] + spatial[sub * WP : sub * WP + W]
    from_cells(cells, gout)
    drain(c7)


def store_kernel(a, b, c, a_out, b_out, c_out, sems):
    copies = [
        pltpu.make_async_copy(src, dst, sems.at[i])
        for i, (src, dst) in enumerate(((a, a_out), (b, b_out), (c, c_out)))
    ]
    for copy in copies:
        copy.start()
    for copy in copies:
        copy.wait()


def on_device(field, cotangent, spectral_weight, pointwise_weight, channel_bias):
    constants = tables()
    weight = jnp.transpose(spectral_weight, (0, 1, 2, 4, 5, 3)).reshape(4, 2, W, 16, W)
    hbm = pl.BlockSpec(memory_space=pltpu.MemorySpace.HBM)
    vmem = pl.BlockSpec(memory_space=pltpu.MemorySpace.VMEM)
    shapes = (((W, 2, 4, Q), BF16), ((W, 2, 4, Q), BF16), ((4, 2, W, 16, W), F32))
    results = pl.pallas_call(
        kernel,
        out_shape=tuple(pltpu.VMEM(shape, dtype) for shape, dtype in shapes),
        in_specs=[hbm] * 10,
        out_specs=(vmem,) * 3,
        scratch_shapes=[
            pltpu.VMEM((W, 2, 4, Q), BF16),
            pltpu.VMEM((W, 2, 4, Q), BF16),
            pltpu.VMEM((4, 2, W, 16, W), F32),
            pltpu.VMEM((W, W), BF16),
            pltpu.VMEM((W,), F32),
            pltpu.VMEM((128, Q), BF16),
            pltpu.VMEM((32, 192), BF16),
            pltpu.VMEM((32, 384), BF16),
            pltpu.VMEM((128, 96), BF16),
            pltpu.VMEM((64, 96), BF16),
            pltpu.VMEM((256, Q), BF16),
            pltpu.VMEM((W, 8, Q), F32),
            pltpu.VMEM((W, 8, Q), F32),
            pltpu.VMEM((128, 128), F32),
            pltpu.VMEM((2, W, 16, 128), F32),
            pltpu.VMEM((8, W, Q), F32),
            pltpu.VMEM((8, W, Q), F32),
            pltpu.VMEM((256, Q), BF16),
            pltpu.VMEM((32, 128), F32),
            pltpu.VMEM((16, 10, 128), F32),
            pltpu.VMEM((16, 8, 128), F32),
            pltpu.VMEM((16, 8, 128), F32),
            pltpu.VMEM((16, 10, 128), F32),
            pltpu.VMEM((2, 16, 10, 128), F32),
            pltpu.VMEM((2, 16, 8, 128), F32),
            pltpu.VMEM((2, 16, 8, 128), F32),
            pltpu.VMEM((2, 16, 10, 128), F32),
            pltpu.SemaphoreType.DMA((10,)),
            pltpu.SemaphoreType.DMA((8, 16)),
            pltpu.SemaphoreType.DMA((8, 16)),
        ],
        compiler_params=pltpu.CompilerParams(
            collective_id=0, has_side_effects=True, vmem_limit_bytes=VMEM - RESULTS
        ),
    )(field, cotangent, weight, pointwise_weight, channel_bias, *constants)
    out, gfield, gspec = pl.pallas_call(
        store_kernel,
        out_shape=tuple(jax.ShapeDtypeStruct(shape, dtype) for shape, dtype in shapes),
        in_specs=[pl.BlockSpec(memory_space=pl.ANY)] * 3,
        out_specs=(hbm,) * 3,
        scratch_shapes=[pltpu.SemaphoreType.DMA((3,))],
        compiler_params=pltpu.CompilerParams(vmem_limit_bytes=1 << 20),
    )(*results)
    grad = jnp.transpose(gspec.reshape(4, 2, W, 1, 16, W), (0, 1, 2, 5, 3, 4))
    return out, gfield, grad


def solution(mesh):
    return jax.shard_map(
        on_device,
        mesh=mesh,
        in_specs=(
            P(None, "gx", "gy", None),
            P(None, "gx", "gy", None),
            P("gx", None, None, None, "gy", None),
            P(),
            P(),
        ),
        out_specs=(
            P(None, "gx", "gy", None),
            P(None, "gx", "gy", None),
            P("gx", None, None, None, "gy", None),
        ),
        check_vma=False,
    )
```

```python
import math

import jax
import jax.numpy as jnp
import numpy as np
from jax import lax
from jax.experimental import pallas as pl
from jax.experimental.pallas import tpu as pltpu
from jax.sharding import PartitionSpec as P

W = 20
WP = 32
GX = 16
GY = 16
Q = 512
F32 = jnp.float32
BF16 = jnp.bfloat16
VMEM = 67043328
RESULTS = 2 * 20 * 8 * 512 * 2 + 160 * 16 * 128 * 4


def frequencies():
    j = np.arange(16)
    return np.where(j < 8, j, j - 16)


def rotation_blocks(length, sign):
    phase = np.mod(frequencies()[:, None] * np.arange(length)[None, :], length)
    angle = sign * 2.0 * np.pi * phase / length
    c, s = np.cos(angle) / np.sqrt(length), np.sin(angle) / np.sqrt(length)
    return np.stack([np.stack([c, -s]), np.stack([s, c])])


def split(a):
    a = a.astype(np.float32)
    hi = a.astype(BF16)
    lo = (a - hi.astype(np.float32)).astype(BF16)
    return np.concatenate([hi, lo, hi], axis=1)


def tables():
    fx = rotation_blocks(32, -1.0).reshape(2, 2, 16, 16, 2)
    tx = np.einsum("rskcx->krsxc", fx).reshape(32, 64)
    fy = rotation_blocks(64, -1.0).reshape(2, 2, 16, 16, 4)
    ty = np.einsum("rskpy->rkpsy", fy).reshape(32, 128)
    iy = rotation_blocks(64, 1.0).reshape(2, 2, 16, 16, 4)
    tyi = np.einsum("rskpy->prysk", iy).reshape(128, 32)
    ix = rotation_blocks(32, 1.0).reshape(2, 2, 16, 16, 2)
    txi = np.einsum("rskcx->rxcks", ix).reshape(64, 32)
    z, t = np.arange(32), np.arange(16)
    f = frequencies()
    phase = (
        f[None, :, None, None] * z[None, None, :, None] * 16
        + np.arange(4)[:, None, None, None] * t[None, None, None, :] * 32
    )
    angle = np.mod(phase, 512).reshape(4, 16, 512) * (2.0 * np.pi / 512)
    zt = np.stack([np.cos(angle), -np.sin(angle)], axis=1).reshape(128, 512) / np.sqrt(512)
    return [zt.astype(np.float32).astype(BF16)] + [split(a) for a in (tx, ty, tyi, txi)]


def lane_blocks(rows):
    return lax.broadcasted_iota(jnp.int32, (rows, 128), 1) // WP


def block_transpose(parts):
    which = lane_blocks(parts[0].shape[0])
    out = []
    for b in range(4):
        acc = None
        for a in range(4):
            shift = ((a - b) * WP) % 128
            piece = parts[a] if shift == 0 else pltpu.roll(parts[a], shift, 1)
            acc = piece if acc is None else jnp.where(which == a, piece, acc)
        out.append(acc)
    return out


def kernel(
    field, cot, weight, pw, bias, zt_h, tx_h, ty_h, tyi_h, txi_h,
    outv, gout, gs,
    fin, cin, wv, pwv, bv, zt, tx, ty, tyi, txi,
    u, cells, ccells, square, wt, local, pre, sig, spec,
    s1, s2, s3, s4, e, d, z, v,
    load_sem, send_sem, recv_sem,
):
    cx = lax.axis_index("gx")
    cy = lax.axis_index("gy")

    turn_x = [lax.rem(cx // 4 + i, 4) * 4 for i in range(4)]
    low = cy // 8
    turn_z = [lax.rem(lax.rem(cx, 4) + i + low * (4 - 2 * i), 4) for i in range(4)]
    turn_l = [lax.rem(low + i, 2) * 8 for i in range(2)]
    turn_y = [lax.rem(cy // 2 + i, 4) * 2 for i in range(4)]
    turn_c = [lax.rem(cy + i, 2) for i in range(2)]
    peer_x = [turn_x[o // 4] + turn_z[o % 4] for o in range(16)]
    peer_y = [turn_l[o // 8] + turn_y[(o % 8) // 2] + turn_c[o % 2] for o in range(16)]

    def ring(n):
        return min(n, 4 - n)

    order_x = sorted(range(16), key=lambda o: -(ring(o // 4) + (1, 3, 3, 1)[o % 4]))
    order_y = sorted(range(1, 16), key=lambda o: -(3 * (o // 8) + 3 * ring((o % 8) // 2) + o % 2))

    other = turn_l[1] + lax.rem(cy, 8)
    flip_y = [turn_l[1 - o // 8] + turn_y[(o % 8) // 2] + turn_c[o % 2] for o in range(16)]
    barrier = pltpu.get_barrier_semaphore()
    for off in order_x:
        pl.semaphore_signal(
            barrier, inc=1, device_id=(peer_x[off], other), device_id_type=pl.DeviceIdType.MESH
        )
    for off in order_y:
        if off == 8:
            continue
        pl.semaphore_signal(
            barrier, inc=1, device_id=(cx, peer_y[off]), device_id_type=pl.DeviceIdType.MESH
        )

    sources = (field, zt_h, tx_h, ty_h, tyi_h, txi_h, weight, pw, bias, cot)
    sinks = (fin, zt, tx, ty, tyi, txi, wv, pwv, bv, cin)
    loads = [
        pltpu.make_async_copy(a, b, load_sem.at[i]) for i, (a, b) in enumerate(zip(sources, sinks))
    ]
    for copy in loads:
        copy.start()

    def start(step, off, src, dst, device):
        copy = pltpu.make_async_remote_copy(
            src_ref=src,
            dst_ref=dst,
            send_sem=send_sem.at[step, off],
            recv_sem=recv_sem.at[step, off],
            device_id=device,
            device_id_type=pl.DeviceIdType.MESH,
        )
        copy.start()
        return copy

    used = pl.ds(0, 10)

    def exchange_x(step, src, dst):
        return [
            start(step, o, src.at[peer_x[o], used], dst.at[cx, used], (peer_x[o], other))
            for o in order_x
        ]

    def exchange_y(step, src, dst, inverse):
        copies = [
            start(
                step,
                o,
                src.at[flip_y[o] if inverse else peer_y[o]],
                dst.at[cy if inverse else other],
                (cx, peer_y[o]),
            )
            for o in order_y
        ]
        if inverse:
            dst[cy] = src[other]
        else:
            dst[other] = src[cy]
        return copies

    def arrive(copies):
        for copy in copies:
            copy.wait_recv()

    def drain(copies):
        for copy in copies:
            copy.wait_send()

    in_block = lax.rem(lax.broadcasted_iota(jnp.int32, (16, 128), 1), WP)
    lane_from = {n: in_block >= n for n in (4, 8, 12, 16, 24, 28) + (W,)}

    def store_cells(blocks, send):
        rows = send.reshape(256, 128)
        for s in range(2):
            c = blocks[s]

            def moved(cell, shift):
                return pltpu.roll(c[cell], shift, 1)

            fill = (
                moved(5, 20),
                jnp.where(lane_from[28], moved(6, 28), moved(5, 8)),
                moved(6, 16),
                jnp.where(lane_from[24], moved(7, 24), moved(6, 4)),
                moved(7, 12),
            )
            for i in range(5):
                rows[pl.ds(s * 5 + i, 16, stride=16), :] = jnp.where(lane_from[W], fill[i], c[i])

    def load_cells(recv):
        blocks = []
        rows = recv.reshape(256, 128)
        for s in range(2):
            c = [rows[pl.ds(s * 5 + i, 16, stride=16), :] for i in range(5)]

            def moved(row, shift):
                return pltpu.roll(c[row], 128 - shift, 1)

            five = jnp.where(lane_from[12], moved(1, 8), moved(0, 20))
            six = jnp.where(lane_from[4], moved(2, 16), moved(1, 28))
            six = jnp.where(lane_from[16], moved(3, 4), six)
            seven = jnp.where(lane_from[8], moved(4, 12), moved(3, 24))
            blocks.append(c + [five, six, seven])
        return blocks

    def pack_modes(values, half):
        spectra = lax.dot_general(
            zt[...],
            values[half * 128 : half * 128 + 128],
            (((1,), (1,)), ((), ())),
            preferred_element_type=F32,
        )
        parts = [spectra[jt * 32 : jt * 32 + 32] for jt in range(4)]
        turned = block_transpose(parts)
        return [[block[s * 16 : s * 16 + 16] for block in turned] for s in range(2)]

    def unpack_modes(blocks, half):
        parts = [
            jnp.concatenate([blocks[s][half * 4 + sub] for s in range(2)], axis=0)
            for sub in range(4)
        ]
        stacked = jnp.concatenate(block_transpose(parts), axis=0)
        return stacked.T.astype(BF16)

    def matmul(table, b):
        hi = b.astype(BF16)
        lo = (b - hi.astype(F32)).astype(BF16)
        return jnp.dot(
            table[...], jnp.concatenate([hi, hi, lo], axis=0), preferred_element_type=F32
        )

    def x_forward(recv, send):
        blocks = load_cells(recv)
        columns = [
            jnp.concatenate([blocks[s][x * 4 + y] for s in range(2) for x in range(2)], axis=0)
            for y in range(4)
        ]
        out = matmul(tx, jnp.concatenate(columns, axis=1))
        for y in range(4):
            send[pl.ds(y, 32, stride=4), :] = out[:, y * 128 : y * 128 + 128]

    def x_inverse(recv, send):
        columns = [recv[pl.ds(y, 32, stride=4), :] for y in range(4)]
        out = matmul(txi, jnp.concatenate(columns, axis=1))
        store_cells(
            [
                [
                    out[(r * 2 + x) * 16 : (r * 2 + x) * 16 + 16, y * 128 : y * 128 + 128]
                    for x in range(2)
                    for y in range(4)
                ]
                for r in range(2)
            ],
            send,
        )

    def lanes(i):
        return slice(i * 128, i * 128 + 128)

    def to_cells(source, target):
        for x in range(2):
            value = source[:, x].astype(F32)
            for i in range(4):
                target.at[i].reshape(W, 8, 128)[:, 4 * x : 4 * x + 4, :] = value[:, :, lanes(i)]

    def from_cells(source, target):
        for x in range(2):
            parts = [
                source.at[i].reshape(W, 8, 128)[:, 4 * x : 4 * x + 4, :] for i in range(4)
            ]
            target[:, x] = jnp.concatenate(parts, axis=2).astype(BF16)

    def load_cell(rows, xy):
        return jnp.concatenate([rows[i, pl.ds(xy, W, stride=8), :] for i in range(4)], axis=1)

    def store_cell(rows, xy, value):
        for i in range(4):
            rows[i, pl.ds(xy, W, stride=8), :] = value[:, lanes(i)]

    kappa = jnp.where(lax.broadcasted_iota(jnp.int32, (16, 128), 1) < WP, 1.0, 2.0).astype(F32)
    gather_base = lane_blocks(16) * WP

    def spread(value, w):
        return jnp.take_along_axis(value, gather_base + w, axis=1)

    loads[0].wait()
    to_cells(fin, cells)
    pad = jnp.zeros((WP - W, Q), F32)
    for xy in range(8):
        u[xy * WP : xy * WP + WP] = jnp.concatenate([load_cell(cells, xy), pad], axis=0).astype(BF16)
    loads[1].wait()
    first, second = pack_modes(u, 0), pack_modes(u, 1)
    store_cells([first[s] + second[s] for s in range(2)], s1)
    pl.semaphore_wait(barrier, 30)
    c0 = exchange_x(0, s1, e.at[0])

    for copy in loads[2:]:
        copy.wait()
    zeros = jnp.zeros((16, WP - W), F32)

    @pl.loop(0, W)
    def _(w):
        for s in range(2):
            pieces = []
            for jt in range(4):
                pieces += [wv[jt, s, w], zeros]
            wt[s, w] = jnp.concatenate(pieces, axis=1)

    square[...] = jnp.zeros((128, 128), F32)
    square[0:W, 0:W] = pwv[...].astype(F32)
    square[WP : WP + 1, 0:W] = bv[...].reshape(1, W)
    turned = square[...].T
    pw_back = square[0:WP, 0:WP].astype(BF16)
    pw_forward = turned[0:WP, 0:WP].astype(BF16)
    bias_column = turned[0:W, WP : WP + 1]
    for xy in range(8):
        rows = slice(xy * WP, xy * WP + WP)
        local[xy] = jnp.dot(pw_forward, u[rows], preferred_element_type=F32)[0:W] + bias_column
    to_cells(cin, ccells)

    arrive(c0)
    x_forward(e.at[0], s2.reshape(128, 128))
    c1 = exchange_y(1, s2, d.at[0], False)
    arrive(c1)
    spec[...] = matmul(ty, d[0].reshape(128, 128))

    acc_r = acc_i = jnp.zeros((16, 128), F32)
    for w in range(W):
        sr, si = spread(spec[0:16], w), spread(spec[16:32], w)
        wr, wi = wt[0, w], wt[1, w]
        acc_r = acc_r + (wr * sr - wi * si)
        acc_i = acc_i + (wi * sr + wr * si)
    mixed = jnp.concatenate([acc_r * kappa, acc_i * kappa], axis=0)

    s3[...] = matmul(tyi, mixed).reshape(16, 8, 128)
    c2 = exchange_y(2, s3, z.at[0], True)
    arrive(c2)
    x_inverse(z.at[0].reshape(128, 128), s4)
    c3 = exchange_x(3, s4, v.at[0])
    drain(c0)
    arrive(c3)

    root = math.sqrt(2.0 / math.pi)
    cubic = 0.044715
    arrived = load_cells(v.at[0])
    packed = []
    for half in range(2):
        spatial = jnp.dot(unpack_modes(arrived, half), zt[...], preferred_element_type=F32)
        for sub in range(4):
            xy = half * 4 + sub
            p = local[xy] + spatial[sub * WP : sub * WP + W]
            pre[xy] = p
            p2 = p * p
            t = jnp.tanh(p * (root * cubic * p2 + root))
            b = p * (1.5 * root * cubic * p2 + 0.5 * root)
            slope = t * (0.5 - b * t) + (b + 0.5)
            signal = load_cell(ccells, xy) * slope
            sig[xy * WP : xy * WP + WP] = jnp.concatenate([signal, pad], axis=0).astype(BF16)
        packed.append(pack_modes(sig, half))

    store_cells([packed[0][s] + packed[1][s] for s in range(2)], s1)
    c4 = exchange_x(4, s1, e.at[1])

    for xy in range(8):
        p = pre[xy]
        t = jnp.tanh(p * (root * cubic * (p * p) + root))
        store_cell(cells, xy, 0.5 * p * (1.0 + t))
        rows = slice(xy * WP, xy * WP + WP)
        local[xy] = jnp.dot(pw_back, sig[rows], preferred_element_type=F32)[0:W]
    from_cells(cells, outv)
    drain(c1)
    drain(c2)
    drain(c3)
    arrive(c4)
    x_forward(e.at[1], s2.reshape(128, 128))
    c5 = exchange_y(5, s2, d.at[1], False)
    arrive(c5)
    back = matmul(ty, d[1].reshape(128, 128))
    br, bi = back[0:16] * kappa, back[16:32] * kappa

    lane = lax.broadcasted_iota(jnp.int32, (32, 128), 1)

    def combine(a, b, h):
        bit = (lane & h) != 0
        flip = lane ^ h
        if b is None:
            return jnp.where(bit, 0.0, a + jnp.take_along_axis(a, flip, axis=1))
        return jnp.where(bit, b, a) + jnp.take_along_axis(jnp.where(bit, a, b), flip, axis=1)

    def product(w):
        wr, wi = wt[0, w], wt[1, w]
        return jnp.concatenate([wr * br + wi * bi, wr * bi - wi * br], axis=0)

    def reduce_tree(w, h):
        if h == WP:
            return product(w) if w < W else None
        a, b = reduce_tree(w, h * 2), reduce_tree(w + h, h * 2)
        return combine(a, b, h) if a is not None else None

    s3[...] = matmul(tyi, reduce_tree(0, 1)).reshape(16, 8, 128)
    c6 = exchange_y(6, s3, z.at[1], True)

    @pl.loop(0, W)
    def _(w):
        sr, si = spread(spec[0:16], w), spread(spec[16:32], w)
        parts = (sr * br + si * bi, sr * bi - si * br)
        for s in range(2):
            for jt in range(4):
                gs[jt, s, w] = parts[s][:, jt * WP : jt * WP + W]

    arrive(c6)
    x_inverse(z.at[1].reshape(128, 128), s4)
    c7 = exchange_x(7, s4, v.at[1])
    drain(c4)
    drain(c5)
    drain(c6)
    arrive(c7)
    arrived = load_cells(v.at[1])
    for half in range(2):
        spatial = jnp.dot(unpack_modes(arrived, half), zt[...], preferred_element_type=F32)
        for sub in range(4):
            xy = half * 4 + sub
            store_cell(cells, xy, local[xy] + spatial[sub * WP : sub * WP + W])
    from_cells(cells, gout)
    drain(c7)


def store_kernel(a, b, c, a_out, b_out, c_out, sems):
    copies = [
        pltpu.make_async_copy(src, dst, sems.at[i])
        for i, (src, dst) in enumerate(((a, a_out), (b, b_out), (c, c_out)))
    ]
    for copy in copies:
        copy.start()
    for copy in copies:
        copy.wait()


def on_device(field, cotangent, spectral_weight, pointwise_weight, channel_bias):
    constants = tables()
    weight = jnp.transpose(spectral_weight, (0, 1, 2, 4, 5, 3)).reshape(4, 2, W, 16, W)
    hbm = pl.BlockSpec(memory_space=pltpu.MemorySpace.HBM)
    vmem = pl.BlockSpec(memory_space=pltpu.MemorySpace.VMEM)
    shapes = (((W, 2, 4, Q), BF16), ((W, 2, 4, Q), BF16), ((4, 2, W, 16, W), F32))
    results = pl.pallas_call(
        kernel,
        out_shape=tuple(pltpu.VMEM(shape, dtype) for shape, dtype in shapes),
        in_specs=[hbm] * 10,
        out_specs=(vmem,) * 3,
        scratch_shapes=[
            pltpu.VMEM((W, 2, 4, Q), BF16),
            pltpu.VMEM((W, 2, 4, Q), BF16),
            pltpu.VMEM((4, 2, W, 16, W), F32),
            pltpu.VMEM((W, W), BF16),
            pltpu.VMEM((W,), F32),
            pltpu.VMEM((128, Q), BF16),
            pltpu.VMEM((32, 192), BF16),
            pltpu.VMEM((32, 384), BF16),
            pltpu.VMEM((128, 96), BF16),
            pltpu.VMEM((64, 96), BF16),
            pltpu.VMEM((256, Q), BF16),
            pltpu.VMEM((4, W * 8, 128), F32),
            pltpu.VMEM((4, W * 8, 128), F32),
            pltpu.VMEM((128, 128), F32),
            pltpu.VMEM((2, W, 16, 128), F32),
            pltpu.VMEM((8, W, Q), F32),
            pltpu.VMEM((8, W, Q), F32),
            pltpu.VMEM((256, Q), BF16),
            pltpu.VMEM((32, 128), F32),
            pltpu.VMEM((16, 16, 128), F32),
            pltpu.VMEM((16, 8, 128), F32),
            pltpu.VMEM((16, 8, 128), F32),
            pltpu.VMEM((16, 16, 128), F32),
            pltpu.VMEM((2, 16, 16, 128), F32),
            pltpu.VMEM((2, 16, 8, 128), F32),
            pltpu.VMEM((2, 16, 8, 128), F32),
            pltpu.VMEM((2, 16, 16, 128), F32),
            pltpu.SemaphoreType.DMA((10,)),
            pltpu.SemaphoreType.DMA((8, 16)),
            pltpu.SemaphoreType.DMA((8, 16)),
        ],
        compiler_params=pltpu.CompilerParams(
            collective_id=0, has_side_effects=True, vmem_limit_bytes=VMEM - RESULTS
        ),
    )(field, cotangent, weight, pointwise_weight, channel_bias, *constants)
    out, gfield, gspec = pl.pallas_call(
        store_kernel,
        out_shape=tuple(jax.ShapeDtypeStruct(shape, dtype) for shape, dtype in shapes),
        in_specs=[pl.BlockSpec(memory_space=pl.ANY)] * 3,
        out_specs=(hbm,) * 3,
        scratch_shapes=[pltpu.SemaphoreType.DMA((3,))],
        compiler_params=pltpu.CompilerParams(vmem_limit_bytes=1 << 20),
    )(*results)
    grad = jnp.transpose(gspec.reshape(4, 2, W, 1, 16, W), (0, 1, 2, 5, 3, 4))
    return out, gfield, grad


def solution(mesh):
    return jax.shard_map(
        on_device,
        mesh=mesh,
        in_specs=(
            P(None, "gx", "gy", None),
            P(None, "gx", "gy", None),
            P("gx", None, None, None, "gy", None),
            P(),
            P(),
        ),
        out_specs=(
            P(None, "gx", "gy", None),
            P(None, "gx", "gy", None),
            P("gx", None, None, None, "gy", None),
        ),
        check_vma=False,
    )
```

```python
import math

import jax
import jax.numpy as jnp
import numpy as np
from jax import lax
from jax.experimental import pallas as pl
from jax.experimental.pallas import tpu as pltpu
from jax.sharding import PartitionSpec as P

W = 20
WP = 32
GX = 16
GY = 16
Q = 512
F32 = jnp.float32
BF16 = jnp.bfloat16
VMEM = 67043328
RESULTS = 20 * 8 * 512 * 2 + 160 * 16 * 128 * 4 + 256 * 512 + 192 * 512 * 4 + 128 * 512 * 2


def frequencies():
    j = np.arange(16)
    return np.where(j < 8, j, j - 16)


def rotation_blocks(length, sign):
    phase = np.mod(frequencies()[:, None] * np.arange(length)[None, :], length)
    angle = sign * 2.0 * np.pi * phase / length
    c, s = np.cos(angle) / np.sqrt(length), np.sin(angle) / np.sqrt(length)
    return np.stack([np.stack([c, -s]), np.stack([s, c])])


def split(a):
    a = a.astype(np.float32)
    hi = a.astype(BF16)
    lo = (a - hi.astype(np.float32)).astype(BF16)
    return np.concatenate([hi, lo, hi], axis=1)


def tables():
    fx = rotation_blocks(32, -1.0).reshape(2, 2, 16, 16, 2)
    tx = np.einsum("rskcx->krsxc", fx).reshape(32, 64)
    fy = rotation_blocks(64, -1.0).reshape(2, 2, 16, 16, 4)
    ty = np.einsum("rskpy->rkpsy", fy).reshape(32, 128)
    iy = rotation_blocks(64, 1.0).reshape(2, 2, 16, 16, 4)
    tyi = np.einsum("rskpy->prysk", iy).reshape(128, 32)
    ix = rotation_blocks(32, 1.0).reshape(2, 2, 16, 16, 2)
    txi = np.einsum("rskcx->rxcks", ix).reshape(64, 32)
    z, t = np.arange(32), np.arange(16)
    f = frequencies()
    phase = (
        f[None, :, None, None] * z[None, None, :, None] * 16
        + np.arange(4)[:, None, None, None] * t[None, None, None, :] * 32
    )
    angle = np.mod(phase, 512).reshape(4, 16, 512) * (2.0 * np.pi / 512)
    zt = np.stack([np.cos(angle), -np.sin(angle)], axis=1).reshape(128, 512) / np.sqrt(512)
    return [zt.astype(np.float32).astype(BF16)] + [split(a) for a in (tx, ty, tyi, txi)]


def lane_blocks(rows):
    return lax.broadcasted_iota(jnp.int32, (rows, 128), 1) // WP


def block_transpose(parts):
    which = lane_blocks(parts[0].shape[0])
    out = []
    for b in range(4):
        acc = None
        for a in range(4):
            shift = ((a - b) * WP) % 128
            piece = parts[a] if shift == 0 else pltpu.roll(parts[a], shift, 1)
            acc = piece if acc is None else jnp.where(which == a, piece, acc)
        out.append(acc)
    return out


def lane_masks():
    in_block = lax.rem(lax.broadcasted_iota(jnp.int32, (16, 128), 1), WP)
    return {n: in_block >= n for n in (4, 8, 12, 16, 24, 28) + (W,)}


def load_cells(recv):
    from_lane = lane_masks()
    blocks = []
    rows = recv.reshape(256, 128)
    for s in range(2):
        c = [rows[pl.ds(s * 5 + i, 16, stride=16), :] for i in range(5)]

        def moved(row, shift):
            return pltpu.roll(c[row], 128 - shift, 1)

        five = jnp.where(from_lane[12], moved(1, 8), moved(0, 20))
        six = jnp.where(from_lane[4], moved(2, 16), moved(1, 28))
        six = jnp.where(from_lane[16], moved(3, 4), six)
        seven = jnp.where(from_lane[8], moved(4, 12), moved(3, 24))
        blocks.append(c + [five, six, seven])
    return blocks


def unpack_modes(blocks, half):
    parts = [
        jnp.concatenate([blocks[s][half * 4 + sub] for s in range(2)], axis=0)
        for sub in range(4)
    ]
    stacked = jnp.concatenate(block_transpose(parts), axis=0)
    return stacked.T.astype(BF16)


def lanes(i):
    return slice(i * 128, i * 128 + 128)


def from_cells(source, target):
    for x in range(2):
        parts = [
            source.at[i].reshape(W, 8, 128)[:, 4 * x : 4 * x + 4, :] for i in range(4)
        ]
        target[:, x] = jnp.concatenate(parts, axis=2).astype(BF16)


def store_cell(rows, xy, value):
    for i in range(4):
        rows[i, pl.ds(xy, W, stride=8), :] = value[:, lanes(i)]


def kernel(
    field, cot, weight, pw, bias, zt_h, tx_h, ty_h, tyi_h, txi_h,
    outv, gs, vout, local, zt,
    fin, cin, wv, pwv, bv, tx, ty, tyi, txi,
    u, cells, ccells, square, wt, pre, sig, spec,
    s1, s2, s3, s4, e, d, z, v,
    load_sem, send_sem, recv_sem,
):
    cx = lax.axis_index("gx")
    cy = lax.axis_index("gy")

    turn_x = [lax.rem(cx // 4 + i, 4) * 4 for i in range(4)]
    low = cy // 8
    turn_z = [lax.rem(lax.rem(cx, 4) + i + low * (4 - 2 * i), 4) for i in range(4)]
    turn_l = [lax.rem(low + i, 2) * 8 for i in range(2)]
    turn_y = [lax.rem(cy // 2 + i, 4) * 2 for i in range(4)]
    turn_c = [lax.rem(cy + i, 2) for i in range(2)]
    peer_x = [turn_x[o // 4] + turn_z[o % 4] for o in range(16)]
    peer_y = [turn_l[o // 8] + turn_y[(o % 8) // 2] + turn_c[o % 2] for o in range(16)]

    def ring(n):
        return min(n, 4 - n)

    order_x = sorted(range(16), key=lambda o: -(ring(o // 4) + (1, 3, 3, 1)[o % 4]))
    order_y = sorted(range(1, 16), key=lambda o: -(3 * (o // 8) + 3 * ring((o % 8) // 2) + o % 2))

    other = turn_l[1] + lax.rem(cy, 8)
    flip_y = [turn_l[1 - o // 8] + turn_y[(o % 8) // 2] + turn_c[o % 2] for o in range(16)]
    barrier = pltpu.get_barrier_semaphore()
    for off in order_x:
        pl.semaphore_signal(
            barrier, inc=1, device_id=(peer_x[off], other), device_id_type=pl.DeviceIdType.MESH
        )
    for off in order_y:
        if off == 8:
            continue
        pl.semaphore_signal(
            barrier, inc=1, device_id=(cx, peer_y[off]), device_id_type=pl.DeviceIdType.MESH
        )

    sources = (field, zt_h, tx_h, ty_h, tyi_h, txi_h, weight, pw, bias, cot)
    sinks = (fin, zt, tx, ty, tyi, txi, wv, pwv, bv, cin)
    loads = [
        pltpu.make_async_copy(a, b, load_sem.at[i]) for i, (a, b) in enumerate(zip(sources, sinks))
    ]
    for copy in loads:
        copy.start()

    def start(step, off, src, dst, device):
        copy = pltpu.make_async_remote_copy(
            src_ref=src,
            dst_ref=dst,
            send_sem=send_sem.at[step, off],
            recv_sem=recv_sem.at[step, off],
            device_id=device,
            device_id_type=pl.DeviceIdType.MESH,
        )
        copy.start()
        return copy

    used = pl.ds(0, 10)

    def exchange_x(step, src, dst):
        return [
            start(step, o, src.at[peer_x[o], used], dst.at[cx, used], (peer_x[o], other))
            for o in order_x
        ]

    def exchange_y(step, src, dst, inverse):
        copies = [
            start(
                step,
                o,
                src.at[flip_y[o] if inverse else peer_y[o]],
                dst.at[cy if inverse else other],
                (cx, peer_y[o]),
            )
            for o in order_y
        ]
        if inverse:
            dst[cy] = src[other]
        else:
            dst[other] = src[cy]
        return copies

    def arrive(copies):
        for copy in copies:
            copy.wait_recv()

    def drain(copies):
        for copy in copies:
            copy.wait_send()

    lane_from = lane_masks()

    def store_cells(blocks, send):
        rows = send.reshape(256, 128)
        for s in range(2):
            c = blocks[s]

            def moved(cell, shift):
                return pltpu.roll(c[cell], shift, 1)

            fill = (
                moved(5, 20),
                jnp.where(lane_from[28], moved(6, 28), moved(5, 8)),
                moved(6, 16),
                jnp.where(lane_from[24], moved(7, 24), moved(6, 4)),
                moved(7, 12),
            )
            for i in range(5):
                rows[pl.ds(s * 5 + i, 16, stride=16), :] = jnp.where(lane_from[W], fill[i], c[i])

    def pack_modes(values, half):
        spectra = lax.dot_general(
            zt[...],
            values[half * 128 : half * 128 + 128],
            (((1,), (1,)), ((), ())),
            preferred_element_type=F32,
        )
        parts = [spectra[jt * 32 : jt * 32 + 32] for jt in range(4)]
        turned = block_transpose(parts)
        return [[block[s * 16 : s * 16 + 16] for block in turned] for s in range(2)]

    def matmul(table, b):
        hi = b.astype(BF16)
        lo = (b - hi.astype(F32)).astype(BF16)
        return jnp.dot(
            table[...], jnp.concatenate([hi, hi, lo], axis=0), preferred_element_type=F32
        )

    def x_forward(recv, send):
        blocks = load_cells(recv)
        columns = [
            jnp.concatenate([blocks[s][x * 4 + y] for s in range(2) for x in range(2)], axis=0)
            for y in range(4)
        ]
        out = matmul(tx, jnp.concatenate(columns, axis=1))
        for y in range(4):
            send[pl.ds(y, 32, stride=4), :] = out[:, y * 128 : y * 128 + 128]

    def x_inverse(recv, send):
        columns = [recv[pl.ds(y, 32, stride=4), :] for y in range(4)]
        out = matmul(txi, jnp.concatenate(columns, axis=1))
        store_cells(
            [
                [
                    out[(r * 2 + x) * 16 : (r * 2 + x) * 16 + 16, y * 128 : y * 128 + 128]
                    for x in range(2)
                    for y in range(4)
                ]
                for r in range(2)
            ],
            send,
        )

    def to_cells(source, target):
        for x in range(2):
            value = source[:, x].astype(F32)
            for i in range(4):
                target.at[i].reshape(W, 8, 128)[:, 4 * x : 4 * x + 4, :] = value[:, :, lanes(i)]

    def load_cell(rows, xy):
        return jnp.concatenate([rows[i, pl.ds(xy, W, stride=8), :] for i in range(4)], axis=1)

    kappa = jnp.where(lax.broadcasted_iota(jnp.int32, (16, 128), 1) < WP, 1.0, 2.0).astype(F32)
    gather_base = lane_blocks(16) * WP

    def spread(value, w):
        return jnp.take_along_axis(value, gather_base + w, axis=1)

    loads[0].wait()
    to_cells(fin, cells)
    pad = jnp.zeros((WP - W, Q), F32)
    for xy in range(8):
        u[xy * WP : xy * WP + WP] = jnp.concatenate([load_cell(cells, xy), pad], axis=0).astype(BF16)
    loads[1].wait()
    first, second = pack_modes(u, 0), pack_modes(u, 1)
    store_cells([first[s] + second[s] for s in range(2)], s1)
    pl.semaphore_wait(barrier, 30)
    c0 = exchange_x(0, s1, e.at[0])

    for copy in loads[2:]:
        copy.wait()
    zeros = jnp.zeros((16, WP - W), F32)

    @pl.loop(0, W)
    def _(w):
        for s in range(2):
            pieces = []
            for jt in range(4):
                pieces += [wv[jt, s, w], zeros]
            wt[s, w] = jnp.concatenate(pieces, axis=1)

    square[...] = jnp.zeros((128, 128), F32)
    square[0:W, 0:W] = pwv[...].astype(F32)
    square[WP : WP + 1, 0:W] = bv[...].reshape(1, W)
    turned = square[...].T
    pw_back = square[0:WP, 0:WP].astype(BF16)
    pw_forward = turned[0:WP, 0:WP].astype(BF16)
    bias_column = turned[0:W, WP : WP + 1]
    for xy in range(8):
        rows = slice(xy * WP, xy * WP + WP)
        local[xy] = jnp.dot(pw_forward, u[rows], preferred_element_type=F32)[0:W] + bias_column
    to_cells(cin, ccells)

    arrive(c0)
    x_forward(e.at[0], s2.reshape(128, 128))
    c1 = exchange_y(1, s2, d.at[0], False)
    arrive(c1)
    spec[...] = matmul(ty, d[0].reshape(128, 128))

    acc_r = acc_i = jnp.zeros((16, 128), F32)
    for w in range(W):
        sr, si = spread(spec[0:16], w), spread(spec[16:32], w)
        wr, wi = wt[0, w], wt[1, w]
        acc_r = acc_r + (wr * sr - wi * si)
        acc_i = acc_i + (wi * sr + wr * si)
    mixed = jnp.concatenate([acc_r * kappa, acc_i * kappa], axis=0)

    s3[...] = matmul(tyi, mixed).reshape(16, 8, 128)
    c2 = exchange_y(2, s3, z.at[0], True)
    arrive(c2)
    x_inverse(z.at[0].reshape(128, 128), s4)
    c3 = exchange_x(3, s4, v.at[0])
    drain(c0)
    arrive(c3)

    root = math.sqrt(2.0 / math.pi)
    cubic = 0.044715
    arrived = load_cells(v.at[0])
    packed = []
    both = jnp.concatenate([unpack_modes(arrived, half) for half in range(2)], axis=0)
    both = jnp.dot(both, zt[...], preferred_element_type=F32)
    for half in range(2):
        spatial = both[half * 128 : half * 128 + 128]
        for sub in range(4):
            xy = half * 4 + sub
            p = local[xy] + spatial[sub * WP : sub * WP + W]
            pre[xy] = p
            p2 = p * p
            t = jnp.tanh(p * (root * cubic * p2 + root))
            b = p * (1.5 * root * cubic * p2 + 0.5 * root)
            slope = t * (0.5 - b * t) + (b + 0.5)
            signal = load_cell(ccells, xy) * slope
            sig[xy * WP : xy * WP + WP] = jnp.concatenate([signal, pad], axis=0).astype(BF16)
        packed.append(pack_modes(sig, half))

    store_cells([packed[0][s] + packed[1][s] for s in range(2)], s1)
    c4 = exchange_x(4, s1, e.at[1])

    @pl.when(cx < GX)
    def _():
        for xy in range(8):
            p = pre[xy]
            t = jnp.tanh(p * (root * cubic * (p * p) + root))
            store_cell(cells, xy, 0.5 * p * (1.0 + t))
            rows = slice(xy * WP, xy * WP + WP)
            local[xy] = jnp.dot(pw_back, sig[rows], preferred_element_type=F32)[0:W]
        from_cells(cells, outv)

    drain(c1)
    drain(c2)
    drain(c3)
    arrive(c4)
    x_forward(e.at[1], s2.reshape(128, 128))
    c5 = exchange_y(5, s2, d.at[1], False)
    arrive(c5)
    back = matmul(ty, d[1].reshape(128, 128))
    br, bi = back[0:16] * kappa, back[16:32] * kappa

    lane = lax.broadcasted_iota(jnp.int32, (32, 128), 1)

    def combine(a, b, h):
        bit = (lane & h) != 0
        flip = lane ^ h
        if b is None:
            return jnp.where(bit, 0.0, a + jnp.take_along_axis(a, flip, axis=1))
        return jnp.where(bit, b, a) + jnp.take_along_axis(jnp.where(bit, a, b), flip, axis=1)

    def product(w):
        wr, wi = wt[0, w], wt[1, w]
        return jnp.concatenate([wr * br + wi * bi, wr * bi - wi * br], axis=0)

    def reduce_tree(w, h):
        if h == WP:
            return product(w) if w < W else None
        a, b = reduce_tree(w, h * 2), reduce_tree(w + h, h * 2)
        return combine(a, b, h) if a is not None else None

    s3[...] = matmul(tyi, reduce_tree(0, 1)).reshape(16, 8, 128)
    c6 = exchange_y(6, s3, z.at[1], True)

    @pl.loop(0, W)
    def _(w):
        sr, si = spread(spec[0:16], w), spread(spec[16:32], w)
        parts = (sr * br + si * bi, sr * bi - si * br)
        for s in range(2):
            for jt in range(4):
                gs[jt, s, w] = parts[s][:, jt * WP : jt * WP + W]

    arrive(c6)
    x_inverse(z.at[1].reshape(128, 128), s4)
    c7 = exchange_x(7, s4, v.at[1])
    drain(c4)
    drain(c5)
    drain(c6)
    arrive(c7)
    vout[:, 0:10, :] = v[1, :, 0:10, :]
    drain(c7)


def store_kernel(a, b, v, local, zt, a_out, gfield, b_out, cells, gout, sems):
    copies = [
        pltpu.make_async_copy(a, a_out, sems.at[0]),
        pltpu.make_async_copy(b, b_out, sems.at[1]),
        pltpu.make_async_copy(gout, gfield, sems.at[2]),
    ]
    copies[0].start()
    copies[1].start()
    arrived = load_cells(v)
    both = jnp.concatenate([unpack_modes(arrived, half) for half in range(2)], axis=0)
    both = jnp.dot(both, zt[...], preferred_element_type=F32)
    for xy in range(8):
        store_cell(cells, xy, local[xy] + both[xy * WP : xy * WP + W])
    from_cells(cells, gout)
    copies[2].start()
    for copy in copies:
        copy.wait()


def on_device(field, cotangent, spectral_weight, pointwise_weight, channel_bias):
    constants = tables()
    weight = jnp.transpose(spectral_weight, (0, 1, 2, 4, 5, 3)).reshape(4, 2, W, 16, W)
    hbm = pl.BlockSpec(memory_space=pltpu.MemorySpace.HBM)
    vmem = pl.BlockSpec(memory_space=pltpu.MemorySpace.VMEM)
    shapes = (
        ((W, 2, 4, Q), BF16),
        ((4, 2, W, 16, W), F32),
        ((16, 16, 128), F32),
        ((8, W, Q), F32),
        ((128, Q), BF16),
    )
    field_shape = jax.ShapeDtypeStruct((W, 2, 4, Q), BF16)
    results = pl.pallas_call(
        kernel,
        out_shape=tuple(pltpu.VMEM(shape, dtype) for shape, dtype in shapes),
        in_specs=[hbm] * 10,
        out_specs=(vmem,) * 5,
        scratch_shapes=[
            pltpu.VMEM((W, 2, 4, Q), BF16),
            pltpu.VMEM((W, 2, 4, Q), BF16),
            pltpu.VMEM((4, 2, W, 16, W), F32),
            pltpu.VMEM((W, W), BF16),
            pltpu.VMEM((W,), F32),
            pltpu.VMEM((32, 192), BF16),
            pltpu.VMEM((32, 384), BF16),
            pltpu.VMEM((128, 96), BF16),
            pltpu.VMEM((64, 96), BF16),
            pltpu.VMEM((256, Q), BF16),
            pltpu.VMEM((4, W * 8, 128), F32),
            pltpu.VMEM((4, W * 8, 128), F32),
            pltpu.VMEM((128, 128), F32),
            pltpu.VMEM((2, W, 16, 128), F32),
            pltpu.VMEM((8, W, Q), F32),
            pltpu.VMEM((256, Q), BF16),
            pltpu.VMEM((32, 128), F32),
            pltpu.VMEM((16, 16, 128), F32),
            pltpu.VMEM((16, 8, 128), F32),
            pltpu.VMEM((16, 8, 128), F32),
            pltpu.VMEM((16, 16, 128), F32),
            pltpu.VMEM((2, 16, 16, 128), F32),
            pltpu.VMEM((2, 16, 8, 128), F32),
            pltpu.VMEM((2, 16, 8, 128), F32),
            pltpu.VMEM((2, 16, 16, 128), F32),
            pltpu.SemaphoreType.DMA((10,)),
            pltpu.SemaphoreType.DMA((8, 16)),
            pltpu.SemaphoreType.DMA((8, 16)),
        ],
        compiler_params=pltpu.CompilerParams(
            collective_id=0, has_side_effects=True, vmem_limit_bytes=VMEM - RESULTS
        ),
    )(field, cotangent, weight, pointwise_weight, channel_bias, *constants)
    out, gfield, gspec = pl.pallas_call(
        store_kernel,
        out_shape=(field_shape, field_shape, jax.ShapeDtypeStruct(*shapes[1])),
        in_specs=[pl.BlockSpec(memory_space=pl.ANY)] * 2 + [vmem] * 3,
        out_specs=(hbm,) * 3,
        scratch_shapes=[
            pltpu.VMEM((4, W * 8, 128), F32),
            pltpu.VMEM((W, 2, 4, Q), BF16),
            pltpu.SemaphoreType.DMA((3,)),
        ],
        compiler_params=pltpu.CompilerParams(vmem_limit_bytes=4 << 20),
    )(*results)
    grad = jnp.transpose(gspec.reshape(4, 2, W, 1, 16, W), (0, 1, 2, 5, 3, 4))
    return out, gfield, grad


def solution(mesh):
    return jax.shard_map(
        on_device,
        mesh=mesh,
        in_specs=(
            P(None, "gx", "gy", None),
            P(None, "gx", "gy", None),
            P("gx", None, None, None, "gy", None),
            P(),
            P(),
        ),
        out_specs=(
            P(None, "gx", "gy", None),
            P(None, "gx", "gy", None),
            P("gx", None, None, None, "gy", None),
        ),
        check_vma=False,
    )
```

```python
import math

import jax
import jax.numpy as jnp
import numpy as np
from jax import lax
from jax.experimental import pallas as pl
from jax.experimental.pallas import tpu as pltpu
from jax.sharding import PartitionSpec as P

W = 20
WP = 32
GX = 16
GY = 16
Q = 512
F32 = jnp.float32
BF16 = jnp.bfloat16
VMEM = 67043328
RESULTS = 20 * 8 * 512 * 2 + 160 * 16 * 128 * 4 + 256 * 512 + 192 * 512 * 4 + 128 * 512 * 2


def frequencies():
    j = np.arange(16)
    return np.where(j < 8, j, j - 16)


def rotation_blocks(length, sign):
    phase = np.mod(frequencies()[:, None] * np.arange(length)[None, :], length)
    angle = sign * 2.0 * np.pi * phase / length
    c, s = np.cos(angle) / np.sqrt(length), np.sin(angle) / np.sqrt(length)
    return np.stack([np.stack([c, -s]), np.stack([s, c])])


def split(a):
    a = a.astype(np.float32)
    hi = a.astype(BF16)
    lo = (a - hi.astype(np.float32)).astype(BF16)
    return np.concatenate([hi, lo, hi], axis=1)


def tables():
    fx = rotation_blocks(32, -1.0).reshape(2, 2, 16, 16, 2)
    tx = np.einsum("rskcx->krsxc", fx).reshape(32, 64)
    fy = rotation_blocks(64, -1.0).reshape(2, 2, 16, 16, 4)
    ty = np.einsum("rskpy->rkpsy", fy).reshape(32, 128)
    iy = rotation_blocks(64, 1.0).reshape(2, 2, 16, 16, 4)
    tyi = np.einsum("rskpy->prysk", iy).reshape(128, 32)
    ix = rotation_blocks(32, 1.0).reshape(2, 2, 16, 16, 2)
    txi = np.einsum("rskcx->rxcks", ix).reshape(64, 32)
    z, t = np.arange(32), np.arange(16)
    f = frequencies()
    phase = (
        f[None, :, None, None] * z[None, None, :, None] * 16
        + np.arange(4)[:, None, None, None] * t[None, None, None, :] * 32
    )
    angle = np.mod(phase, 512).reshape(4, 16, 512) * (2.0 * np.pi / 512)
    zt = np.stack([np.cos(angle), -np.sin(angle)], axis=1).reshape(128, 512) / np.sqrt(512)
    return [zt.astype(np.float32).astype(BF16)] + [split(a) for a in (tx, ty, tyi, txi)]


def lane_blocks(rows):
    return lax.broadcasted_iota(jnp.int32, (rows, 128), 1) // WP


def block_transpose(parts):
    which = lane_blocks(parts[0].shape[0])
    out = []
    for b in range(4):
        acc = None
        for a in range(4):
            shift = ((a - b) * WP) % 128
            piece = parts[a] if shift == 0 else pltpu.roll(parts[a], shift, 1)
            acc = piece if acc is None else jnp.where(which == a, piece, acc)
        out.append(acc)
    return out


def lane_masks():
    in_block = lax.rem(lax.broadcasted_iota(jnp.int32, (16, 128), 1), WP)
    return {n: in_block >= n for n in (4, 8, 12, 16, 24, 28) + (W,)}


def load_cells(recv):
    from_lane = lane_masks()
    blocks = []
    rows = recv.reshape(256, 128)
    for s in range(2):
        c = [rows[pl.ds(s * 5 + i, 16, stride=16), :] for i in range(5)]

        def moved(row, shift):
            return pltpu.roll(c[row], 128 - shift, 1)

        five = jnp.where(from_lane[12], moved(1, 8), moved(0, 20))
        six = jnp.where(from_lane[4], moved(2, 16), moved(1, 28))
        six = jnp.where(from_lane[16], moved(3, 4), six)
        seven = jnp.where(from_lane[8], moved(4, 12), moved(3, 24))
        blocks.append(c + [five, six, seven])
    return blocks


def unpack_modes(blocks, half):
    parts = [
        jnp.concatenate([blocks[s][half * 4 + sub] for s in range(2)], axis=0)
        for sub in range(4)
    ]
    stacked = jnp.concatenate(block_transpose(parts), axis=0)
    return stacked.astype(BF16).T


def lanes(i):
    return slice(i * 128, i * 128 + 128)


def from_cells(source, target):
    for x in range(2):
        parts = [
            source.at[i].reshape(W, 8, 128)[:, 4 * x : 4 * x + 4, :] for i in range(4)
        ]
        target[:, x] = jnp.concatenate(parts, axis=2).astype(BF16)


def store_cell(rows, xy, value):
    for i in range(4):
        rows[i, pl.ds(xy, W, stride=8), :] = value[:, lanes(i)]


def kernel(
    field, cot, weight, pw, bias, zt_h, tx_h, ty_h, tyi_h, txi_h,
    outv, gs, vout, local, zt,
    fin, cin, wv, pwv, bv, tx, ty, tyi, txi,
    u, cells, ccells, square, wt, pre, sig, spec,
    s1, s2, s3, s4, e, d, z, v,
    load_sem, send_sem, recv_sem,
):
    cx = lax.axis_index("gx")
    cy = lax.axis_index("gy")

    turn_x = [lax.rem(cx // 4 + i, 4) * 4 for i in range(4)]
    low = cy // 8
    turn_z = [lax.rem(lax.rem(cx, 4) + i + low * (4 - 2 * i), 4) for i in range(4)]
    turn_l = [lax.rem(low + i, 2) * 8 for i in range(2)]
    turn_y = [lax.rem(cy // 2 + i, 4) * 2 for i in range(4)]
    turn_c = [lax.rem(cy + i, 2) for i in range(2)]
    peer_x = [turn_x[o // 4] + turn_z[o % 4] for o in range(16)]
    peer_y = [turn_l[o // 8] + turn_y[(o % 8) // 2] + turn_c[o % 2] for o in range(16)]

    def ring(n):
        return min(n, 4 - n)

    order_x = sorted(range(16), key=lambda o: -(ring(o // 4) + (1, 3, 3, 1)[o % 4]))
    order_y = sorted(range(1, 16), key=lambda o: -(3 * (o // 8) + 3 * ring((o % 8) // 2) + o % 2))

    other = turn_l[1] + lax.rem(cy, 8)
    flip_y = [turn_l[1 - o // 8] + turn_y[(o % 8) // 2] + turn_c[o % 2] for o in range(16)]
    barrier = pltpu.get_barrier_semaphore()
    for off in order_x:
        pl.semaphore_signal(
            barrier, inc=1, device_id=(peer_x[off], other), device_id_type=pl.DeviceIdType.MESH
        )
    for off in order_y:
        if off == 8:
            continue
        pl.semaphore_signal(
            barrier, inc=1, device_id=(cx, peer_y[off]), device_id_type=pl.DeviceIdType.MESH
        )

    sources = (field, zt_h, tx_h, ty_h, tyi_h, txi_h, weight, pw, bias, cot)
    sinks = (fin, zt, tx, ty, tyi, txi, wv, pwv, bv, cin)
    loads = [
        pltpu.make_async_copy(a, b, load_sem.at[i]) for i, (a, b) in enumerate(zip(sources, sinks))
    ]
    for copy in loads:
        copy.start()

    def start(step, off, src, dst, device):
        copy = pltpu.make_async_remote_copy(
            src_ref=src,
            dst_ref=dst,
            send_sem=send_sem.at[step, off],
            recv_sem=recv_sem.at[step, off],
            device_id=device,
            device_id_type=pl.DeviceIdType.MESH,
        )
        copy.start()
        return copy

    used = pl.ds(0, 10)

    def exchange_x(step, src, dst):
        return [
            start(step, o, src.at[peer_x[o], used], dst.at[cx, used], (peer_x[o], other))
            for o in order_x
        ]

    def exchange_y(step, src, dst, inverse):
        copies = [
            start(
                step,
                o,
                src.at[flip_y[o] if inverse else peer_y[o]],
                dst.at[cy if inverse else other],
                (cx, peer_y[o]),
            )
            for o in order_y
        ]
        if inverse:
            dst[cy] = src[other]
        else:
            dst[other] = src[cy]
        return copies

    def arrive(copies):
        for copy in copies:
            copy.wait_recv()

    def drain(copies):
        for copy in copies:
            copy.wait_send()

    lane_from = lane_masks()

    def store_cells(blocks, send):
        rows = send.reshape(256, 128)
        for s in range(2):
            c = blocks[s]

            def moved(cell, shift):
                return pltpu.roll(c[cell], shift, 1)

            fill = (
                moved(5, 20),
                jnp.where(lane_from[28], moved(6, 28), moved(5, 8)),
                moved(6, 16),
                jnp.where(lane_from[24], moved(7, 24), moved(6, 4)),
                moved(7, 12),
            )
            for i in range(5):
                rows[pl.ds(s * 5 + i, 16, stride=16), :] = jnp.where(lane_from[W], fill[i], c[i])

    def pack_modes(values, half):
        spectra = lax.dot_general(
            zt[...],
            values[half * 128 : half * 128 + 128],
            (((1,), (1,)), ((), ())),
            preferred_element_type=F32,
        )
        parts = [spectra[jt * 32 : jt * 32 + 32] for jt in range(4)]
        turned = block_transpose(parts)
        return [[block[s * 16 : s * 16 + 16] for block in turned] for s in range(2)]

    def matmul(table, b):
        hi = b.astype(BF16)
        lo = (b - hi.astype(F32)).astype(BF16)
        return jnp.dot(
            table[...], jnp.concatenate([hi, hi, lo], axis=0), preferred_element_type=F32
        )

    def x_forward(recv, send):
        blocks = load_cells(recv)
        columns = [
            jnp.concatenate([blocks[s][x * 4 + y] for s in range(2) for x in range(2)], axis=0)
            for y in range(4)
        ]
        out = matmul(tx, jnp.concatenate(columns, axis=1))
        for y in range(4):
            send[pl.ds(y, 32, stride=4), :] = out[:, y * 128 : y * 128 + 128]

    def x_inverse(recv, send):
        columns = [recv[pl.ds(y, 32, stride=4), :] for y in range(4)]
        out = matmul(txi, jnp.concatenate(columns, axis=1))
        store_cells(
            [
                [
                    out[(r * 2 + x) * 16 : (r * 2 + x) * 16 + 16, y * 128 : y * 128 + 128]
                    for x in range(2)
                    for y in range(4)
                ]
                for r in range(2)
            ],
            send,
        )

    def to_cells(source, target):
        for x in range(2):
            value = source[:, x].astype(F32)
            for i in range(4):
                target.at[i].reshape(W, 8, 128)[:, 4 * x : 4 * x + 4, :] = value[:, :, lanes(i)]

    def load_cell(rows, xy):
        return jnp.concatenate([rows[i, pl.ds(xy, W, stride=8), :] for i in range(4)], axis=1)

    kappa = jnp.where(lax.broadcasted_iota(jnp.int32, (16, 128), 1) < WP, 1.0, 2.0).astype(F32)
    gather_base = lane_blocks(16) * WP

    def spread(value, w):
        return jnp.take_along_axis(value, gather_base + w, axis=1)

    loads[0].wait()
    to_cells(fin, cells)
    pad = jnp.zeros((WP - W, Q), F32)
    for xy in range(8):
        u[xy * WP : xy * WP + WP] = jnp.concatenate([load_cell(cells, xy), pad], axis=0).astype(BF16)
    loads[1].wait()
    first, second = pack_modes(u, 0), pack_modes(u, 1)
    store_cells([first[s] + second[s] for s in range(2)], s1)
    pl.semaphore_wait(barrier, 30)
    c0 = exchange_x(0, s1, e.at[0])

    for copy in loads[2:]:
        copy.wait()
    zeros = jnp.zeros((16, WP - W), F32)

    @pl.loop(0, W)
    def _(w):
        for s in range(2):
            pieces = []
            for jt in range(4):
                pieces += [wv[jt, s, w], zeros]
            wt[s, w] = jnp.concatenate(pieces, axis=1)

    square[...] = jnp.zeros((128, 128), F32)
    square[0:W, 0:W] = pwv[...].astype(F32)
    square[WP : WP + 1, 0:W] = bv[...].reshape(1, W)
    turned = square[...].T
    pw_back = square[0:WP, 0:WP].astype(BF16)
    pw_forward = turned[0:WP, 0:WP].astype(BF16)
    bias_column = turned[0:W, WP : WP + 1]
    for xy in range(8):
        rows = slice(xy * WP, xy * WP + WP)
        local[xy] = jnp.dot(pw_forward, u[rows], preferred_element_type=F32)[0:W] + bias_column
    to_cells(cin, ccells)

    arrive(c0)
    x_forward(e.at[0], s2.reshape(128, 128))
    c1 = exchange_y(1, s2, d.at[0], False)
    arrive(c1)
    spec[...] = matmul(ty, d[0].reshape(128, 128))

    acc_r = acc_i = jnp.zeros((16, 128), F32)
    for w in range(W):
        sr, si = spread(spec[0:16], w), spread(spec[16:32], w)
        wr, wi = wt[0, w], wt[1, w]
        acc_r = acc_r + (wr * sr - wi * si)
        acc_i = acc_i + (wi * sr + wr * si)
    mixed = jnp.concatenate([acc_r * kappa, acc_i * kappa], axis=0)

    s3[...] = matmul(tyi, mixed).reshape(16, 8, 128)
    c2 = exchange_y(2, s3, z.at[0], True)
    arrive(c2)
    x_inverse(z.at[0].reshape(128, 128), s4)
    c3 = exchange_x(3, s4, v.at[0])
    drain(c0)
    arrive(c3)

    root = math.sqrt(2.0 / math.pi)
    cubic = 0.044715
    arrived = load_cells(v.at[0])
    packed = []
    both = jnp.concatenate([unpack_modes(arrived, half) for half in range(2)], axis=0)
    both = jnp.dot(both, zt[...], preferred_element_type=F32)
    for half in range(2):
        spatial = both[half * 128 : half * 128 + 128]
        for sub in range(4):
            xy = half * 4 + sub
            p = local[xy] + spatial[sub * WP : sub * WP + W]
            pre[xy] = p
            p2 = p * p
            t = jnp.tanh(p * (root * cubic * p2 + root))
            b = p * (1.5 * root * cubic * p2 + 0.5 * root)
            slope = t * (0.5 - b * t) + (b + 0.5)
            signal = load_cell(ccells, xy) * slope
            sig[xy * WP : xy * WP + WP] = jnp.concatenate([signal, pad], axis=0).astype(BF16)
        packed.append(pack_modes(sig, half))

    store_cells([packed[0][s] + packed[1][s] for s in range(2)], s1)
    c4 = exchange_x(4, s1, e.at[1])

    @pl.when(cx < GX)
    def _():
        for xy in range(8):
            p = pre[xy]
            t = jnp.tanh(p * (root * cubic * (p * p) + root))
            store_cell(cells, xy, 0.5 * p * (1.0 + t))
            rows = slice(xy * WP, xy * WP + WP)
            local[xy] = jnp.dot(pw_back, sig[rows], preferred_element_type=F32)[0:W]
        from_cells(cells, outv)

    drain(c1)
    drain(c2)
    drain(c3)
    arrive(c4)
    x_forward(e.at[1], s2.reshape(128, 128))
    c5 = exchange_y(5, s2, d.at[1], False)
    arrive(c5)
    back = matmul(ty, d[1].reshape(128, 128))
    br, bi = back[0:16] * kappa, back[16:32] * kappa

    lane = lax.broadcasted_iota(jnp.int32, (32, 128), 1)

    def combine(a, b, h):
        bit = (lane & h) != 0
        flip = lane ^ h
        if b is None:
            return jnp.where(bit, 0.0, a + jnp.take_along_axis(a, flip, axis=1))
        return jnp.where(bit, b, a) + jnp.take_along_axis(jnp.where(bit, a, b), flip, axis=1)

    def product(w):
        wr, wi = wt[0, w], wt[1, w]
        return jnp.concatenate([wr * br + wi * bi, wr * bi - wi * br], axis=0)

    def reduce_tree(w, h):
        if h == WP:
            return product(w) if w < W else None
        a, b = reduce_tree(w, h * 2), reduce_tree(w + h, h * 2)
        return combine(a, b, h) if a is not None else None

    s3[...] = matmul(tyi, reduce_tree(0, 1)).reshape(16, 8, 128)
    c6 = exchange_y(6, s3, z.at[1], True)

    @pl.loop(0, W)
    def _(w):
        sr, si = spread(spec[0:16], w), spread(spec[16:32], w)
        parts = (sr * br + si * bi, sr * bi - si * br)
        for s in range(2):
            for jt in range(4):
                gs[jt, s, w] = parts[s][:, jt * WP : jt * WP + W]

    arrive(c6)
    x_inverse(z.at[1].reshape(128, 128), s4)
    c7 = exchange_x(7, s4, v.at[1])
    drain(c4)
    drain(c5)
    drain(c6)
    arrive(c7)
    vout[:, 0:10, :] = v[1, :, 0:10, :]
    drain(c7)


def store_kernel(a, b, v, local, zt, a_out, gfield, b_out, cells, gout, sems):
    copies = [
        pltpu.make_async_copy(a, a_out, sems.at[0]),
        pltpu.make_async_copy(b, b_out, sems.at[1]),
        pltpu.make_async_copy(gout, gfield, sems.at[2]),
    ]
    copies[0].start()
    copies[1].start()
    arrived = load_cells(v)
    both = jnp.concatenate([unpack_modes(arrived, half) for half in range(2)], axis=0)
    both = jnp.dot(both, zt[...], preferred_element_type=F32)
    for xy in range(8):
        store_cell(cells, xy, local[xy] + both[xy * WP : xy * WP + W])
    from_cells(cells, gout)
    copies[2].start()
    for copy in copies:
        copy.wait()


def on_device(field, cotangent, spectral_weight, pointwise_weight, channel_bias):
    constants = tables()
    weight = jnp.transpose(spectral_weight, (0, 1, 2, 4, 5, 3)).reshape(4, 2, W, 16, W)
    hbm = pl.BlockSpec(memory_space=pltpu.MemorySpace.HBM)
    vmem = pl.BlockSpec(memory_space=pltpu.MemorySpace.VMEM)
    shapes = (
        ((W, 2, 4, Q), BF16),
        ((4, 2, W, 16, W), F32),
        ((16, 16, 128), F32),
        ((8, W, Q), F32),
        ((128, Q), BF16),
    )
    field_shape = jax.ShapeDtypeStruct((W, 2, 4, Q), BF16)
    results = pl.pallas_call(
        kernel,
        out_shape=tuple(pltpu.VMEM(shape, dtype) for shape, dtype in shapes),
        in_specs=[hbm] * 10,
        out_specs=(vmem,) * 5,
        scratch_shapes=[
            pltpu.VMEM((W, 2, 4, Q), BF16),
            pltpu.VMEM((W, 2, 4, Q), BF16),
            pltpu.VMEM((4, 2, W, 16, W), F32),
            pltpu.VMEM((W, W), BF16),
            pltpu.VMEM((W,), F32),
            pltpu.VMEM((32, 192), BF16),
            pltpu.VMEM((32, 384), BF16),
            pltpu.VMEM((128, 96), BF16),
            pltpu.VMEM((64, 96), BF16),
            pltpu.VMEM((256, Q), BF16),
            pltpu.VMEM((4, W * 8, 128), F32),
            pltpu.VMEM((4, W * 8, 128), F32),
            pltpu.VMEM((128, 128), F32),
            pltpu.VMEM((2, W, 16, 128), F32),
            pltpu.VMEM((8, W, Q), F32),
            pltpu.VMEM((256, Q), BF16),
            pltpu.VMEM((32, 128), F32),
            pltpu.VMEM((16, 16, 128), F32),
            pltpu.VMEM((16, 8, 128), F32),
            pltpu.VMEM((16, 8, 128), F32),
            pltpu.VMEM((16, 16, 128), F32),
            pltpu.VMEM((2, 16, 16, 128), F32),
            pltpu.VMEM((2, 16, 8, 128), F32),
            pltpu.VMEM((2, 16, 8, 128), F32),
            pltpu.VMEM((2, 16, 16, 128), F32),
            pltpu.SemaphoreType.DMA((10,)),
            pltpu.SemaphoreType.DMA((8, 16)),
            pltpu.SemaphoreType.DMA((8, 16)),
        ],
        compiler_params=pltpu.CompilerParams(
            collective_id=0, has_side_effects=True, vmem_limit_bytes=VMEM - RESULTS
        ),
    )(field, cotangent, weight, pointwise_weight, channel_bias, *constants)
    out, gfield, gspec = pl.pallas_call(
        store_kernel,
        out_shape=(field_shape, field_shape, jax.ShapeDtypeStruct(*shapes[1])),
        in_specs=[pl.BlockSpec(memory_space=pl.ANY)] * 2 + [vmem] * 3,
        out_specs=(hbm,) * 3,
        scratch_shapes=[
            pltpu.VMEM((4, W * 8, 128), F32),
            pltpu.VMEM((W, 2, 4, Q), BF16),
            pltpu.SemaphoreType.DMA((3,)),
        ],
        compiler_params=pltpu.CompilerParams(vmem_limit_bytes=4 << 20),
    )(*results)
    grad = jnp.transpose(gspec.reshape(4, 2, W, 1, 16, W), (0, 1, 2, 5, 3, 4))
    return out, gfield, grad


def solution(mesh):
    return jax.shard_map(
        on_device,
        mesh=mesh,
        in_specs=(
            P(None, "gx", "gy", None),
            P(None, "gx", "gy", None),
            P("gx", None, None, None, "gy", None),
            P(),
            P(),
        ),
        out_specs=(
            P(None, "gx", "gy", None),
            P(None, "gx", "gy", None),
            P("gx", None, None, None, "gy", None),
        ),
        check_vma=False,
    )
```
